512 devices in a mesh: row: 16 (over x, y_hi, core), col: 32 (over z, y_lo).
Axes of the slice: x: 4, y: 8 (y_hi: 2, y_lo: 4; y = y_hi * 4 + y_lo), z: 8, core: 2. Of those that a mesh axis runs over, the one named last changes fastest.
Arguments:
- observations: float32 [4096, 32768], P('row', 'col'), may hold values from -6 to 6
- omega: float32 [32, 3, 16, 128, 128], P('col'), as said below
- block_slots: int32 [32, 3, 16], P('col'), may hold values from -1 to 63, as said below
Outputs:
- new_omega: float32 [32, 3, 16, 128, 128], P('col', None, 'row')
The draws below stay inside these ranges and needn't reach their ends.
Inputs may be any that keep to these rules, and one draw needn't show every extreme that they name: `block_slots`: active slots come first in each tile. The pattern is symmetric: slot j of [t, 2] and slot j of [t + 1, 0] (modulo 32) name mirrored blocks, a and b swapped; in [t, 1] the 8 diagonal blocks come first in order, then mirrored pairs side by side. Some tile has all 16 slots active. `omega`: the blocks of active slots form one symmetric matrix: the block of slot j of [t, 2] is the transpose of that of slot j of [t + 1, 0], mirrored pairs of [t, 1] are transposes of each other, and diagonal blocks are symmetric with diagonal entries of 0.8 or more. Empty slots hold arbitrary values.
All inputs are finite; a program needn't handle non-finite values.
Results may differ from the reference program's by a relative error of at most 0.0003.
Values sent between devices are 32-bit elements; how exact they have to be, the bound alone decides.
No kernel may reach another device: no remote copies, remote signals or barrier semaphores. Data moves between devices by JAX's collectives and lax.ppermute only.
A program may use at most 128 MiB of HBM per device.

```python
import jax
import jax.numpy as jnp
import numpy as np
from jax import lax

TILE = 1024
BLK = 128
KMAX = 16
SAMPLES = 4096
VARS = 32768
N_COL = 32


def slot_layout(key):
    tile_blocks = TILE // BLK
    capacity = min(KMAX, tile_blocks * tile_blocks)
    pair_most = (capacity - tile_blocks) // 2
    keys_all = jax.random.split(jax.random.fold_in(key, 11), 6)
    strips = jnp.arange(N_COL)
    counts = jax.random.randint(keys_all[0], (N_COL,), 1, capacity + 1)
    chosen = jax.random.randint(keys_all[1], (), 0, N_COL)
    counts = jnp.where(strips == chosen, capacity, counts)
    orders = jax.vmap(lambda sub_key: jax.random.permutation(sub_key, tile_blocks * tile_blocks))(jax.random.split(keys_all[2], N_COL))
    upper = orders[:, :capacity].astype(jnp.int32)
    upper = jnp.where(jnp.arange(capacity)[None, :] < counts[:, None], upper, -1)
    upper = jnp.pad(upper, ((0, 0), (0, KMAX - capacity)), constant_values=-1)
    mirrored = jnp.where(upper >= 0, upper % tile_blocks * tile_blocks + upper // tile_blocks, -1)
    lower = jnp.roll(mirrored, 1, axis=0)
    rows_table, cols_table = np.triu_indices(tile_blocks, 1)
    rows_jnp = jnp.asarray(rows_table, jnp.int32)
    cols_jnp = jnp.asarray(cols_table, jnp.int32)
    pair_orders = jax.vmap(lambda sub_key: jax.random.permutation(sub_key, rows_table.size))(jax.random.split(keys_all[3], N_COL))[:, :pair_most]
    first_pos = rows_jnp[pair_orders] * tile_blocks + cols_jnp[pair_orders]
    second_pos = cols_jnp[pair_orders] * tile_blocks + rows_jnp[pair_orders]
    pair_counts = jax.random.randint(keys_all[4], (N_COL,), 0, pair_most + 1)
    chosen_pair = jax.random.randint(keys_all[5], (), 0, N_COL)
    pair_counts = jnp.where(strips == chosen_pair, pair_most, pair_counts)
    live_pairs = jnp.arange(pair_most)[None, :] < pair_counts[:, None]
    first_pos = jnp.where(live_pairs, first_pos, -1)
    second_pos = jnp.where(live_pairs, second_pos, -1)
    pairs = jnp.stack([first_pos, second_pos], axis=2).reshape(N_COL, 2 * pair_most).astype(jnp.int32)
    diagonal = jnp.broadcast_to(jnp.arange(tile_blocks, dtype=jnp.int32) * (tile_blocks + 1), (N_COL, tile_blocks))
    centre = jnp.concatenate([diagonal, pairs], axis=1)
    centre = jnp.pad(centre, ((0, 0), (0, KMAX - tile_blocks - 2 * pair_most)), constant_values=-1)
    return jnp.stack([lower, centre, upper], axis=1).astype(jnp.int32)


def draw_block_slots(key, part):
    return slot_layout(key)


def draw_omega(key, part):
    tile_blocks = TILE // BLK
    capacity = min(KMAX, tile_blocks * tile_blocks)
    pair_most = (capacity - tile_blocks) // 2
    keys_all = jax.random.split(jax.random.fold_in(key, 23), 3)
    shape = (N_COL, KMAX, BLK, BLK)
    upper = 0.1 * jax.random.normal(keys_all[0], shape, jnp.float32)
    raw_blocks = 0.1 * jax.random.normal(keys_all[1], shape, jnp.float32)
    diag_vals = jax.random.uniform(keys_all[2], (N_COL, KMAX, BLK), jnp.float32, 1.0, 2.0)
    lower = jnp.roll(jnp.swapaxes(upper, 2, 3), 1, axis=0)
    identity = jnp.eye(BLK, dtype=bool)
    symmetric = (raw_blocks + jnp.swapaxes(raw_blocks, 2, 3)) * 0.7071
    symmetric = jnp.where(identity, diag_vals[:, :, :, None], symmetric)
    source = np.arange(KMAX)
    second = np.zeros(KMAX, dtype=bool)
    for slot_index in range(tile_blocks, tile_blocks + 2 * pair_most):
        source[slot_index] = tile_blocks + 2 * ((slot_index - tile_blocks) // 2)
        second[slot_index] = (slot_index - tile_blocks) % 2 == 1
    paired = raw_blocks[:, source]
    paired = jnp.where(second[None, :, None, None], jnp.swapaxes(paired, 2, 3), paired)
    centre = jnp.where((np.arange(KMAX) < tile_blocks)[None, :, None, None], symmetric, paired)
    return jnp.stack([lower, centre, upper], axis=1)


def shard_levels(stream_key, shape, cuts, least, top_value):
    level, own = 1.0, jax.random.fold_in(stream_key, 6)
    for axis_at, parts in cuts:
        heights = jnp.exp(jax.random.uniform(jax.random.fold_in(own, axis_at), (parts,), jnp.float32, least / len(cuts), top_value / len(cuts)))
        level = level * jnp.repeat(heights, shape[axis_at] // parts).reshape([-1 if axis == axis_at else 1 for axis in range(len(shape))])
    return level


def gaussian(own_key, extent, width, most, pieces=(), kind=jnp.bfloat16):
    gain = shard_levels(own_key, extent, pieces, -0.22, 0.18) if pieces else 1.0
    entries = jax.random.normal(own_key, extent, jnp.float32) * width * gain
    return jnp.minimum(jnp.maximum(entries, -most), most).astype(kind)


def setup_inputs(seed: int = 0) -> dict:
    seeds = jax.random.split(jax.random.key(seed), 4)
    return {
        "observations": gaussian(seeds[0], (SAMPLES, VARS), 1.0, 6.0, ((0, 16), (1, 32)), jnp.float32),
        "omega": draw_omega(jax.random.fold_in(seeds[3], 71), 0),
        "block_slots": draw_block_slots(jax.random.fold_in(seeds[3], 71), 0),
    }


step_size = 0.5
penalty = 0.1
highest = lax.Precision.HIGHEST


def strip_terms(tile_view, omega_strip, slot_ids, column):
    tile_blocks = TILE // BLK
    nearby = jnp.stack([lax.dynamic_index_in_dim(tile_view, ((column + tile_step) % N_COL).astype(jnp.int32), 1, keepdims=False) for tile_step in (-1, 0, 1)])
    active = slot_ids >= 0
    row_pick = jax.nn.one_hot(jnp.where(active, slot_ids // tile_blocks, -1), tile_blocks, dtype=jnp.float32)
    col_pick = jax.nn.one_hot(jnp.where(active, slot_ids % tile_blocks, -1), tile_blocks, dtype=jnp.float32)
    chosen = jnp.einsum('ejn,epnk->ejpk', row_pick, nearby, precision=highest)
    product = jnp.einsum('ejpk,ejkl->ejpl', chosen, omega_strip, precision=highest)
    residual = jnp.einsum('ejn,ejpl->pnl', col_pick, product, precision=highest)
    picked = jnp.einsum('ejn,pnl->ejpl', col_pick, residual, precision=highest)
    return jnp.einsum('ejpk,ejpl->ejkl', chosen, picked, precision=highest)


def mirror_inner(forward_centre, centre_ids):
    tile_blocks = TILE // BLK
    active = centre_ids >= 0
    flipped = jnp.where(active, (centre_ids % tile_blocks) * tile_blocks + centre_ids // tile_blocks, -2)
    match_table = ((centre_ids[..., None, :] == flipped[..., :, None]) & active[..., None, :]).astype(jnp.float32)
    return jnp.einsum('...jk,...kab->...jba', match_table, forward_centre, precision=highest)


def proximal(omega_part, slot_part, smooth):
    tile_blocks = TILE // BLK
    active = slot_part >= 0
    centre_mask = (jnp.arange(3) == 1)[:, None]
    diagonal_block = active & centre_mask & (slot_part // tile_blocks == slot_part % tile_blocks)
    identity = jnp.eye(BLK, dtype=jnp.float32)
    own_diag = jnp.diagonal(omega_part, axis1=-2, axis2=-1)
    safe_diag = jnp.where(diagonal_block[..., None], own_diag, 1.0)
    inverse = jnp.where(diagonal_block[..., None], 1.0 / safe_diag, 0.0)
    gradient = smooth - inverse[..., None] * identity
    trial_step = omega_part - step_size * gradient
    shrunk = jnp.sign(trial_step) * jnp.maximum(jnp.abs(trial_step) - step_size * penalty, 0.0)
    keep_mask = diagonal_block[..., None, None] & (identity > 0.5)
    result = jnp.where(keep_mask, trial_step, shrunk)
    return jnp.where(active[..., None, None], result, 0.0)


def reference(observations, omega, block_slots):
    tile_blocks = TILE // BLK
    tile_view = observations.reshape(observations.shape[0], N_COL, tile_blocks, BLK)
    columns = jnp.arange(N_COL, dtype=jnp.int32)
    forward = lax.map(lambda strip_item: strip_terms(tile_view, strip_item[0], strip_item[1], strip_item[2]), (omega, block_slots, columns))
    forward = forward / SAMPLES
    from_below = jnp.swapaxes(jnp.roll(forward[:, 2], 1, axis=0), -1, -2)
    from_above = jnp.swapaxes(jnp.roll(forward[:, 0], -1, axis=0), -1, -2)
    inner_mirror = mirror_inner(forward[:, 1], block_slots[:, 1])
    mirror = jnp.stack([from_below, inner_mirror, from_above], axis=1)
    smooth = 0.5 * (forward + mirror)
    return proximal(omega, block_slots, smooth)
```

```python
import jax
import jax.numpy as jnp
from jax import lax
from jax.experimental import pallas as pl
from jax.experimental.pallas import tpu as pltpu
from jax.sharding import Mesh, PartitionSpec as P

TILE = 1024
BLK = 128
NB = TILE // BLK
KMAX = 16
ROWS = 256
SAMPLES = 4096
step_size = 0.5
penalty = 0.1
f32 = jnp.float32
bf16 = jnp.bfloat16
VMEM_LIMIT = 48 * 1024 * 1024


def split(value):
    high = value.astype(bf16)
    low = (value - high.astype(f32)).astype(bf16)
    return high, low


def split_tile(x_ref, natural_ref, turned_ref):
    for a in range(NB):
        block = x_ref[:, a * BLK : (a + 1) * BLK]
        high, low = split(block)
        natural_ref[a, :, :BLK] = high
        natural_ref[a, :, BLK:] = low
        high, low = split(block.T)
        turned_ref[a, :BLK, :] = high
        turned_ref[a, BLK:, :] = low


def add_products(slots_ref, omega_ref, natural_ref, residual_ref, offset):
    def body(j, carry):
        slot = slots_ref[0, offset, j]
        active = slot >= 0
        place = jnp.maximum(slot, 0)
        a = place // NB
        b = place % NB
        weight = jnp.where(active, omega_ref[0, 0, j], 0.0)
        high, low = split(weight)
        half = jnp.concatenate([high, low], axis=1)
        weights = jnp.concatenate([half, half], axis=0)
        out = jnp.dot(natural_ref[a], weights, preferred_element_type=f32)
        residual_ref[b] += out[:, :BLK] + out[:, BLK:]
        return carry

    lax.fori_loop(0, KMAX, body, 0, unroll=4)


def partial_kernel(offset, first, *refs):
    if first:
        slots_ref, x_ref, omega_ref, residual_ref, turned_ref, natural_ref = refs
        residual_ref[...] = jnp.zeros_like(residual_ref)
    else:
        slots_ref, x_ref, omega_ref, before_ref, residual_ref, turned_ref, natural_ref = refs
        residual_ref[...] = before_ref[...]
    split_tile(x_ref, natural_ref, turned_ref)
    add_products(slots_ref, omega_ref, natural_ref, residual_ref, offset)


def quadrant_sum(out):
    out = out[:BLK] + out[BLK:]
    return out[:, :BLK] + out[:, BLK:]


def forward_kernel(
    slots_ref, core_ref, x_ref, omega_ref, before_ref, below_ref, centre_ref,
    own_ref, send_ref, residual_ref, natural_ref, above_ref, pieces_ref,
):
    residual_ref[...] = before_ref[...]
    split_tile(x_ref, natural_ref, above_ref)
    add_products(slots_ref, omega_ref, natural_ref, residual_ref, 2)
    for b in range(NB):
        high, low = split(residual_ref[b])
        pieces_ref[b, :, :BLK] = high
        pieces_ref[b, :, BLK:] = low
    core = core_ref[0]
    turned = (below_ref, centre_ref, above_ref)

    def body(i, carry):
        for e in range(3):
            found = []
            for k in range(2):
                place = jnp.maximum(slots_ref[0, e, 2 * i + k], 0)
                a = place // NB
                b = place % NB
                out = jnp.dot(turned[e][a], pieces_ref[b], preferred_element_type=f32)
                found.append(quadrant_sum(out))
            even, odd = found
            if e == 1:
                even_turned, odd_turned = even.T, odd.T
                diagonal = i < NB // 2
                even, odd = (
                    even + jnp.where(diagonal, even_turned, odd_turned),
                    odd + jnp.where(diagonal, odd_turned, even_turned),
                )
            own_ref[i, e] = jnp.where(core == 0, even, odd)
            send_ref[i, e] = jnp.where(core == 0, odd, even)
        return carry

    lax.fori_loop(0, KMAX // 2, body, 0)


def proximal_kernel(
    place_ref, slots_ref, total_ref, left_ref, right_ref, omega_ref, out_ref
):
    j = place_ref[0]
    rows = lax.broadcasted_iota(jnp.int32, (BLK, BLK), 0)
    columns = lax.broadcasted_iota(jnp.int32, (BLK, BLK), 1)
    for e in range(3):
        slot = slots_ref[0, e, j]
        total = total_ref[e]
        if e == 0:
            total = total + left_ref[...].T
        if e == 2:
            total = total + right_ref[...].T
        gradient = total * (0.5 / SAMPLES)
        omega = omega_ref[0, e, 0]
        if e == 1:
            diagonal = (slot >= 0) & (slot // NB == slot % NB)
            on_diagonal = (rows == columns) & diagonal
            inverse = 1.0 / jnp.where(on_diagonal, omega, 1.0)
            gradient = gradient - jnp.where(on_diagonal, inverse, 0.0)
        trial = omega - step_size * gradient
        shrunk = jnp.maximum(jnp.abs(trial) - step_size * penalty, 0.0)
        result = jnp.where(trial < 0.0, -shrunk, shrunk)
        if e == 1:
            result = jnp.where(on_diagonal, trial, result)
        out_ref[0, e, 0] = jnp.where(slot >= 0, result, 0.0)


def params():
    return pltpu.CompilerParams(vmem_limit_bytes=VMEM_LIMIT)


SMEM = pl.BlockSpec(memory_space=pltpu.SMEM)
WHOLE = pl.BlockSpec(memory_space=pltpu.VMEM)
TURNED = (NB, 2 * BLK, ROWS)
NATURAL = (NB, ROWS, 2 * BLK)


def omega_spec(offset):
    return pl.BlockSpec((1, 1, KMAX, BLK, BLK), lambda i: (0, offset, 0, 0, 0))


def full_spec(shape):
    return pl.BlockSpec(shape, lambda i: (0,) * len(shape))


def partial(offset, slots, tile, omega, before=None):
    first = before is None
    in_specs = [SMEM, full_spec((ROWS, TILE)), omega_spec(offset)]
    inputs = [slots, tile, omega]
    if not first:
        in_specs.append(full_spec((NB, ROWS, BLK)))
        inputs.append(before)
    return pl.pallas_call(
        lambda *refs: partial_kernel(offset, first, *refs),
        name="partial_residual",
        grid=(1,),
        out_shape=(
            jax.ShapeDtypeStruct((NB, ROWS, BLK), f32),
            jax.ShapeDtypeStruct(TURNED, bf16),
        ),
        in_specs=in_specs,
        out_specs=(full_spec((NB, ROWS, BLK)), full_spec(TURNED)),
        scratch_shapes=[pltpu.VMEM(NATURAL, bf16)],
        compiler_params=params(),
        cost_estimate=pl.CostEstimate(
            flops=2 * KMAX * ROWS * 256 * 256, bytes_accessed=5 << 20, transcendentals=0
        ),
    )(*inputs)


def forward_blocks(slots, core, tile, omega, before, below, centre):
    shape = (KMAX // 2, 3, BLK, BLK)
    return pl.pallas_call(
        forward_kernel,
        name="forward_blocks",
        grid=(1,),
        out_shape=(jax.ShapeDtypeStruct(shape, f32),) * 2,
        in_specs=[
            SMEM,
            SMEM,
            full_spec((ROWS, TILE)),
            omega_spec(2),
            full_spec((NB, ROWS, BLK)),
            full_spec(TURNED),
            full_spec(TURNED),
        ],
        out_specs=(full_spec(shape),) * 2,
        scratch_shapes=[
            pltpu.VMEM((NB, ROWS, BLK), f32),
            pltpu.VMEM(NATURAL, bf16),
            pltpu.VMEM(TURNED, bf16),
            pltpu.VMEM(NATURAL, bf16),
        ],
        compiler_params=params(),
        cost_estimate=pl.CostEstimate(
            flops=8 * KMAX * ROWS * 256 * 256, bytes_accessed=8 << 20, transcendentals=0
        ),
    )(slots, core, tile, omega, before, below, centre)


def proximal(place, slots, total, left, right, omega):
    return pl.pallas_call(
        proximal_kernel,
        name="proximal",
        grid_spec=pltpu.PrefetchScalarGridSpec(
            num_scalar_prefetch=2,
            grid=(1,),
            in_specs=[
                pl.BlockSpec((3, BLK, BLK), lambda i, place, slots: (0, 0, 0)),
                pl.BlockSpec((BLK, BLK), lambda i, place, slots: (0, 0)),
                pl.BlockSpec((BLK, BLK), lambda i, place, slots: (0, 0)),
                pl.BlockSpec(
                    (1, 3, 1, BLK, BLK), lambda i, place, slots: (0, 0, place[0], 0, 0)
                ),
            ],
            out_specs=pl.BlockSpec(
                (1, 3, 1, BLK, BLK), lambda i, place, slots: (0, 0, 0, 0, 0)
            ),
        ),
        out_shape=jax.ShapeDtypeStruct((1, 3, 1, BLK, BLK), f32),
        compiler_params=params(),
        cost_estimate=pl.CostEstimate(
            flops=20 * 3 * BLK * BLK, bytes_accessed=1 << 19, transcendentals=0
        ),
    )(place, slots, total, left, right, omega)


def shifted(value, axis, steps):
    count = lax.axis_size(axis)
    pairs = [(source, (source + steps) % count) for source in range(count)]
    return lax.ppermute(value, axis, pairs)


def on_device(observations, omega, block_slots):
    core = lax.axis_index("core").astype(jnp.int32)
    place = lax.axis_index(("x", "y_hi", "core")).astype(jnp.int32)
    from_below = shifted(observations, "col", 1)
    from_above = shifted(observations, "col", -1)
    residual, centre = partial(1, block_slots, observations, omega)
    residual, below = partial(0, block_slots, from_below, omega, residual)
    own, send = forward_blocks(
        block_slots, core.reshape(1), from_above, omega, residual, below, centre
    )
    chip = own + shifted(send, "core", 1)
    gathered = lax.all_to_all(chip, ("x", "y_hi"), 0, 0)
    total = jnp.sum(gathered, axis=0)
    left = shifted(total[2], "col", 1)
    right = shifted(total[0], "col", -1)
    return proximal(place.reshape(1), block_slots, total, left, right, omega)


def solution(mesh):
    devices = mesh.devices.reshape(4, 2, 2, 32)
    fine = Mesh(devices, ("x", "y_hi", "core", "col"))
    rows = ("x", "y_hi", "core")
    return jax.shard_map(
        on_device,
        mesh=fine,
        in_specs=(P(rows, "col"), P("col", None, None, None, None), P("col", None, None)),
        out_specs=P("col", None, rows, None, None),
        check_vma=False,
    )
```

```python
import jax
import jax.numpy as jnp
from jax import lax
from jax.experimental import pallas as pl
from jax.experimental.pallas import tpu as pltpu
from jax.sharding import Mesh, PartitionSpec as P

TILE = 1024
BLK = 128
NB = TILE // BLK
KMAX = 16
ROWS = 256
SAMPLES = 4096
step_size = 0.5
penalty = 0.1
f32 = jnp.float32
bf16 = jnp.bfloat16
VMEM_LIMIT = 24 * 1024 * 1024


def split(value):
    high = value.astype(bf16)
    low = (value - high.astype(f32)).astype(bf16)
    return high, low


def split_tile(x_ref, natural_ref, turned_ref):
    for a in range(NB):
        block = x_ref[:, a * BLK : (a + 1) * BLK]
        high, low = split(block)
        natural_ref[a, :, :BLK] = high
        natural_ref[a, :, BLK:] = low
        high, low = split(block.T)
        turned_ref[a, :BLK, :] = high
        turned_ref[a, BLK:, :] = low


def add_products(slots_ref, omega_ref, natural_ref, residual_ref, offset):
    def body(j, carry):
        slot = slots_ref[0, offset, j]
        active = slot >= 0
        place = jnp.maximum(slot, 0)
        a = place // NB
        b = place % NB
        weight = jnp.where(active, omega_ref[0, 0, j], 0.0)
        high, low = split(weight)
        half = jnp.concatenate([high, low], axis=1)
        weights = jnp.concatenate([half, half], axis=0)
        out = jnp.dot(natural_ref[a], weights, preferred_element_type=f32)
        residual_ref[b] += out[:, :BLK] + out[:, BLK:]
        return carry

    lax.fori_loop(0, KMAX, body, 0, unroll=4)


def partial_kernel(offset, first, *refs):
    if first:
        slots_ref, x_ref, omega_ref, residual_ref, turned_ref, natural_ref = refs
        residual_ref[...] = jnp.zeros_like(residual_ref)
    else:
        slots_ref, x_ref, omega_ref, before_ref, residual_ref, turned_ref, natural_ref = refs
        residual_ref[...] = before_ref[...]
    split_tile(x_ref, natural_ref, turned_ref)
    add_products(slots_ref, omega_ref, natural_ref, residual_ref, offset)


def quadrant_sum(out):
    out = out[:BLK] + out[BLK:]
    return out[:, :BLK] + out[:, BLK:]


def slot_block(slots_ref, e, j, turned, pieces_ref):
    place = jnp.maximum(slots_ref[0, e, j], 0)
    out = jnp.dot(
        turned[e][place // NB], pieces_ref[place % NB], preferred_element_type=f32
    )
    return quadrant_sum(out)


def group_products(slots_ref, where_ref, turned, pieces_ref, y_hi, keep_ref, pass_ref, send_ref):
    x, core = where_ref[0], where_ref[2]
    even_pair, odd_pair = x ^ 1, 3 - x
    first = jnp.where(core == 0, even_pair, odd_pair)
    second = jnp.where(core == 0, odd_pair, even_pair)
    for r, x_of in enumerate((x, second, first, x ^ 2)):
        i = 2 * x_of + y_hi
        for e in range(3):
            even = slot_block(slots_ref, e, 2 * i, turned, pieces_ref)
            odd = slot_block(slots_ref, e, 2 * i + 1, turned, pieces_ref)
            if e == 1:
                even_turned, odd_turned = even.T, odd.T
                diagonal = i < NB // 2
                even, odd = (
                    even + jnp.where(diagonal, even_turned, odd_turned),
                    odd + jnp.where(diagonal, odd_turned, even_turned),
                )
            own_ref = keep_ref if r < 2 else pass_ref
            own_ref[r % 2, e] = jnp.where(core == 0, even, odd)
            send_ref[(0, 2, 1, 3)[r], e] = jnp.where(core == 0, odd, even)


def far_kernel(
    slots_ref, where_ref, x_ref, omega_ref, before_ref, below_ref, centre_ref,
    keep_ref, pass_ref, send_ref, above_ref, pieces_ref, residual_ref, natural_ref,
):
    residual_ref[...] = before_ref[...]
    split_tile(x_ref, natural_ref, above_ref)
    add_products(slots_ref, omega_ref, natural_ref, residual_ref, 2)
    for b in range(NB):
        high, low = split(residual_ref[b])
        pieces_ref[b, :, :BLK] = high
        pieces_ref[b, :, BLK:] = low
    group_products(
        slots_ref, where_ref, (below_ref, centre_ref, above_ref), pieces_ref,
        1 - where_ref[1], keep_ref, pass_ref, send_ref,
    )


def near_kernel(
    slots_ref, where_ref, below_ref, centre_ref, above_ref, pieces_ref,
    keep_ref, pass_ref, send_ref,
):
    group_products(
        slots_ref, where_ref, (below_ref, centre_ref, above_ref), pieces_ref,
        where_ref[1], keep_ref, pass_ref, send_ref,
    )


def proximal_kernel(
    place_ref, slots_ref, total_ref, left_ref, right_ref, omega_ref, out_ref
):
    j = place_ref[0]
    rows = lax.broadcasted_iota(jnp.int32, (BLK, BLK), 0)
    columns = lax.broadcasted_iota(jnp.int32, (BLK, BLK), 1)
    for e in range(3):
        slot = slots_ref[0, e, j]
        total = total_ref[e]
        if e == 0:
            total = total + left_ref[...].T
        if e == 2:
            total = total + right_ref[...].T
        gradient = total * (0.5 / SAMPLES)
        omega = omega_ref[0, e, 0]
        if e == 1:
            diagonal = (slot >= 0) & (slot // NB == slot % NB)
            on_diagonal = (rows == columns) & diagonal
            inverse = 1.0 / jnp.where(on_diagonal, omega, 1.0)
            gradient = gradient - jnp.where(on_diagonal, inverse, 0.0)
        trial = omega - step_size * gradient
        shrunk = jnp.maximum(jnp.abs(trial) - step_size * penalty, 0.0)
        result = jnp.where(trial < 0.0, -shrunk, shrunk)
        if e == 1:
            result = jnp.where(on_diagonal, trial, result)
        out_ref[0, e, 0] = jnp.where(slot >= 0, result, 0.0)


def params():
    return pltpu.CompilerParams(vmem_limit_bytes=VMEM_LIMIT)


SMEM = pl.BlockSpec(memory_space=pltpu.SMEM)
WHOLE = pl.BlockSpec(memory_space=pltpu.VMEM)
TURNED = (NB, 2 * BLK, ROWS)
NATURAL = (NB, ROWS, 2 * BLK)


def omega_spec(offset):
    return pl.BlockSpec((1, 1, KMAX, BLK, BLK), lambda i: (0, offset, 0, 0, 0))


def full_spec(shape):
    return pl.BlockSpec(shape, lambda i: (0,) * len(shape))


def partial(offset, slots, tile, omega, before=None):
    first = before is None
    in_specs = [SMEM, full_spec((ROWS, TILE)), omega_spec(offset)]
    inputs = [slots, tile, omega]
    if not first:
        in_specs.append(full_spec((NB, ROWS, BLK)))
        inputs.append(before)
    return pl.pallas_call(
        lambda *refs: partial_kernel(offset, first, *refs),
        name="partial_residual",
        grid=(1,),
        out_shape=(
            jax.ShapeDtypeStruct((NB, ROWS, BLK), f32),
            jax.ShapeDtypeStruct(TURNED, bf16),
        ),
        in_specs=in_specs,
        out_specs=(full_spec((NB, ROWS, BLK)), full_spec(TURNED)),
        scratch_shapes=[pltpu.VMEM(NATURAL, bf16)],
        compiler_params=params(),
        cost_estimate=pl.CostEstimate(
            flops=2 * KMAX * ROWS * 256 * 256, bytes_accessed=5 << 20, transcendentals=0
        ),
    )(*inputs)


HALF = (2, 3, BLK, BLK)
WAY = (4, 3, BLK, BLK)
GROUP_OUT = tuple(jax.ShapeDtypeStruct(shape, f32) for shape in (HALF, HALF, WAY))
GROUP_SPECS = tuple(full_spec(shape) for shape in (HALF, HALF, WAY))


def far_blocks(slots, where, tile, omega, before, below, centre):
    return pl.pallas_call(
        far_kernel,
        name="far_blocks",
        grid=(1,),
        out_shape=GROUP_OUT
        + (jax.ShapeDtypeStruct(TURNED, bf16), jax.ShapeDtypeStruct(NATURAL, bf16)),
        in_specs=[
            SMEM,
            SMEM,
            full_spec((ROWS, TILE)),
            omega_spec(2),
            full_spec((NB, ROWS, BLK)),
            full_spec(TURNED),
            full_spec(TURNED),
        ],
        out_specs=GROUP_SPECS + (full_spec(TURNED), full_spec(NATURAL)),
        scratch_shapes=[pltpu.VMEM((NB, ROWS, BLK), f32), pltpu.VMEM(NATURAL, bf16)],
        compiler_params=params(),
        cost_estimate=pl.CostEstimate(
            flops=5 * KMAX * ROWS * 256 * 256, bytes_accessed=8 << 20, transcendentals=0
        ),
    )(slots, where, tile, omega, before, below, centre)


def near_blocks(slots, where, below, centre, above, pieces):
    return pl.pallas_call(
        near_kernel,
        name="near_blocks",
        grid=(1,),
        out_shape=GROUP_OUT,
        in_specs=[SMEM, SMEM]
        + [full_spec(TURNED)] * 3
        + [full_spec(NATURAL)],
        out_specs=GROUP_SPECS,
        compiler_params=params(),
        cost_estimate=pl.CostEstimate(
            flops=3 * KMAX * ROWS * 256 * 256, bytes_accessed=8 << 20, transcendentals=0
        ),
    )(slots, where, below, centre, above, pieces)


def proximal(place, slots, total, left, right, omega):
    return pl.pallas_call(
        proximal_kernel,
        name="proximal",
        grid_spec=pltpu.PrefetchScalarGridSpec(
            num_scalar_prefetch=2,
            grid=(1,),
            in_specs=[
                pl.BlockSpec((3, BLK, BLK), lambda i, place, slots: (0, 0, 0)),
                pl.BlockSpec((BLK, BLK), lambda i, place, slots: (0, 0)),
                pl.BlockSpec((BLK, BLK), lambda i, place, slots: (0, 0)),
                pl.BlockSpec(
                    (1, 3, 1, BLK, BLK), lambda i, place, slots: (0, 0, place[0], 0, 0)
                ),
            ],
            out_specs=pl.BlockSpec(
                (1, 3, 1, BLK, BLK), lambda i, place, slots: (0, 0, 0, 0, 0)
            ),
        ),
        out_shape=jax.ShapeDtypeStruct((1, 3, 1, BLK, BLK), f32),
        compiler_params=params(),
        cost_estimate=pl.CostEstimate(
            flops=20 * 3 * BLK * BLK, bytes_accessed=1 << 19, transcendentals=0
        ),
    )(place, slots, total, left, right, omega)


def shifted(value, axis, steps):
    count = lax.axis_size(axis)
    pairs = [(source, (source + steps) % count) for source in range(count)]
    return lax.ppermute(value, axis, pairs)


def x_exchange(value, step):
    pairs = []
    for x in range(4):
        for core in range(2):
            partner = x ^ 1 if core == step else 3 - x
            pairs.append((2 * x + core, 2 * partner + core))
    return lax.ppermute(value, ("x", "core"), pairs)


def on_device(observations, omega, block_slots):
    x, y_hi, core = (lax.axis_index(n).astype(jnp.int32) for n in ("x", "y_hi", "core"))
    where = jnp.stack([x, y_hi, core])
    place = 4 * x + 2 * y_hi + core
    from_below = shifted(observations, "col", 1)
    from_above = shifted(observations, "col", -1)
    residual, centre = partial(1, block_slots, observations, omega)
    residual, below = partial(0, block_slots, from_below, omega, residual)
    far_keep, far_pass, far_send, above, pieces = far_blocks(
        block_slots, where, from_above, omega, residual, below, centre
    )
    far_got = shifted(far_send, "core", 1)
    near_keep, near_pass, near_send = near_blocks(
        block_slots, where, below, centre, above, pieces
    )
    near_got = shifted(near_send, "core", 1)
    far_first = x_exchange(far_pass + far_got[2:], 0)
    near_first = x_exchange(near_pass + near_got[2:], 0)
    far_second = x_exchange(far_keep[1] + far_got[1] + far_first[1], 1)
    far_sum = far_keep[0] + far_got[0] + far_first[0] + far_second
    other = shifted(far_sum, "y_hi", 1)
    near_second = x_exchange(near_keep[1] + near_got[1] + near_first[1], 1)
    near_sum = near_keep[0] + near_got[0] + near_first[0] + near_second
    total = near_sum + other
    left = shifted(total[2], "col", 1)
    right = shifted(total[0], "col", -1)
    return proximal(place.reshape(1), block_slots, total, left, right, omega)


def solution(mesh):
    devices = mesh.devices.reshape(4, 2, 2, 32)
    fine = Mesh(devices, ("x", "y_hi", "core", "col"))
    rows = ("x", "y_hi", "core")
    return jax.shard_map(
        on_device,
        mesh=fine,
        in_specs=(P(rows, "col"), P("col", None, None, None, None), P("col", None, None)),
        out_specs=P("col", None, rows, None, None),
        check_vma=False,
    )
```

```python
import jax
import jax.numpy as jnp
from jax import lax
from jax.experimental import pallas as pl
from jax.experimental.pallas import tpu as pltpu
from jax.sharding import Mesh, PartitionSpec as P

TILE = 1024
BLK = 128
NB = TILE // BLK
KMAX = 16
ROWS = 256
SAMPLES = 4096
step_size = 0.5
penalty = 0.1
f32 = jnp.float32
bf16 = jnp.bfloat16
VMEM_LIMIT = 24 * 1024 * 1024


def split(value):
    high = value.astype(bf16)
    low = (value - high.astype(f32)).astype(bf16)
    return high, low


def split_tile(x_ref, natural_ref, turned_ref):
    for a in range(NB):
        block = x_ref[:, a * BLK : (a + 1) * BLK]
        high, low = split(block)
        natural_ref[a, :, :BLK] = high
        natural_ref[a, :, BLK:] = low
        high, low = split(block.T)
        turned_ref[a, :BLK, :] = high
        turned_ref[a, BLK:, :] = low


def add_products(slots_ref, omega_ref, natural_ref, residual_ref, offset):
    def body(j, carry):
        slot = slots_ref[0, offset, j]
        active = slot >= 0
        place = jnp.maximum(slot, 0)
        a = place // NB
        b = place % NB
        weight = jnp.where(active, omega_ref[0, 0, j], 0.0)
        high, low = split(weight)
        half = jnp.concatenate([high, low], axis=1)
        weights = jnp.concatenate([half, half], axis=0)
        out = jnp.dot(natural_ref[a], weights, preferred_element_type=f32)
        residual_ref[b] += out[:, :BLK] + out[:, BLK:]
        return carry

    lax.fori_loop(0, KMAX, body, 0, unroll=4)


def partial_kernel(offset, first, *refs):
    if first:
        slots_ref, x_ref, omega_ref, residual_ref, turned_ref, natural_ref = refs
        residual_ref[...] = jnp.zeros_like(residual_ref)
    else:
        slots_ref, x_ref, omega_ref, before_ref, residual_ref, turned_ref, natural_ref = refs
        residual_ref[...] = before_ref[...]
    split_tile(x_ref, natural_ref, turned_ref)
    add_products(slots_ref, omega_ref, natural_ref, residual_ref, offset)


def quadrant_sum(out):
    out = out[:BLK] + out[BLK:]
    return out[:, :BLK] + out[:, BLK:]


def slot_block(slots_ref, e, j, turned, pieces_ref):
    place = jnp.maximum(slots_ref[0, e, j], 0)
    out = jnp.dot(
        turned[e][place // NB], pieces_ref[place % NB], preferred_element_type=f32
    )
    return quadrant_sum(out)


def group_products(slots_ref, where_ref, turned, pieces_ref, y_hi, keep_ref, pass_ref, send_ref):
    x, core = where_ref[0], where_ref[2]
    even_pair, odd_pair = x ^ 1, 3 - x
    first = jnp.where(core == 0, even_pair, odd_pair)
    second = jnp.where(core == 0, odd_pair, even_pair)
    for r, x_of in enumerate((x, second, first, x ^ 2)):
        i = 2 * x_of + y_hi
        for e in range(3):
            even = slot_block(slots_ref, e, 2 * i, turned, pieces_ref)
            odd = slot_block(slots_ref, e, 2 * i + 1, turned, pieces_ref)
            if e == 1:
                even_turned, odd_turned = even.T, odd.T
                diagonal = i < NB // 2
                even, odd = (
                    even + jnp.where(diagonal, even_turned, odd_turned),
                    odd + jnp.where(diagonal, odd_turned, even_turned),
                )
            own_ref = keep_ref if r < 2 else pass_ref
            own_ref[r % 2, e] = jnp.where(core == 0, even, odd)
            send_ref[(0, 2, 1, 3)[r], e] = jnp.where(core == 0, odd, even)


def far_kernel(
    slots_ref, where_ref, x_ref, omega_ref, before_ref, below_ref, centre_ref,
    keep_ref, pass_ref, send_ref, above_ref, pieces_ref, residual_ref, natural_ref,
):
    residual_ref[...] = before_ref[...]
    split_tile(x_ref, natural_ref, above_ref)
    add_products(slots_ref, omega_ref, natural_ref, residual_ref, 2)
    for b in range(NB):
        high, low = split(residual_ref[b])
        pieces_ref[b, :, :BLK] = high
        pieces_ref[b, :, BLK:] = low
    group_products(
        slots_ref, where_ref, (below_ref, centre_ref, above_ref), pieces_ref,
        1 - where_ref[1], keep_ref, pass_ref, send_ref,
    )


def near_kernel(
    slots_ref, where_ref, below_ref, centre_ref, above_ref, pieces_ref,
    keep_ref, pass_ref, send_ref,
):
    group_products(
        slots_ref, where_ref, (below_ref, centre_ref, above_ref), pieces_ref,
        where_ref[1], keep_ref, pass_ref, send_ref,
    )


def proximal_kernel(
    place_ref, slots_ref, total_ref, left_ref, right_ref, omega_ref, out_ref
):
    j = place_ref[0]
    rows = lax.broadcasted_iota(jnp.int32, (BLK, BLK), 0)
    columns = lax.broadcasted_iota(jnp.int32, (BLK, BLK), 1)
    for e in range(3):
        slot = slots_ref[0, e, j]
        total = total_ref[e]
        if e == 0:
            total = total + left_ref[...].T
        if e == 2:
            total = total + right_ref[...].T
        gradient = total * (0.5 / SAMPLES)
        omega = omega_ref[0, e, 0]
        if e == 1:
            diagonal = (slot >= 0) & (slot // NB == slot % NB)
            on_diagonal = (rows == columns) & diagonal
            inverse = 1.0 / jnp.where(on_diagonal, omega, 1.0)
            gradient = gradient - jnp.where(on_diagonal, inverse, 0.0)
        trial = omega - step_size * gradient
        shrunk = jnp.maximum(jnp.abs(trial) - step_size * penalty, 0.0)
        result = jnp.where(trial < 0.0, -shrunk, shrunk)
        if e == 1:
            result = jnp.where(on_diagonal, trial, result)
        out_ref[0, e, 0] = jnp.where(slot >= 0, result, 0.0)


def params():
    return pltpu.CompilerParams(vmem_limit_bytes=VMEM_LIMIT)


SMEM = pl.BlockSpec(memory_space=pltpu.SMEM)
WHOLE = pl.BlockSpec(memory_space=pltpu.VMEM)
TURNED = (NB, 2 * BLK, ROWS)
NATURAL = (NB, ROWS, 2 * BLK)


def omega_spec(offset):
    return pl.BlockSpec((1, 1, KMAX, BLK, BLK), lambda i: (0, offset, 0, 0, 0))


def full_spec(shape):
    return pl.BlockSpec(shape, lambda i: (0,) * len(shape))


def partial(offset, slots, tile, omega, before=None):
    first = before is None
    in_specs = [SMEM, full_spec((ROWS, TILE)), omega_spec(offset)]
    inputs = [slots, tile, omega]
    if not first:
        in_specs.append(full_spec((NB, ROWS, BLK)))
        inputs.append(before)
    return pl.pallas_call(
        lambda *refs: partial_kernel(offset, first, *refs),
        name="partial_residual",
        grid=(1,),
        out_shape=(
            jax.ShapeDtypeStruct((NB, ROWS, BLK), f32),
            jax.ShapeDtypeStruct(TURNED, bf16),
        ),
        in_specs=in_specs,
        out_specs=(full_spec((NB, ROWS, BLK)), full_spec(TURNED)),
        scratch_shapes=[pltpu.VMEM(NATURAL, bf16)],
        compiler_params=params(),
        cost_estimate=pl.CostEstimate(
            flops=2 * KMAX * ROWS * 256 * 256, bytes_accessed=5 << 20, transcendentals=0
        ),
    )(*inputs)


HALF = (2, 3, BLK, BLK)
WAY = (4, 3, BLK, BLK)
GROUP_OUT = tuple(jax.ShapeDtypeStruct(shape, f32) for shape in (HALF, HALF, WAY))
GROUP_SPECS = tuple(full_spec(shape) for shape in (HALF, HALF, WAY))


def far_blocks(slots, where, tile, omega, before, below, centre):
    return pl.pallas_call(
        far_kernel,
        name="far_blocks",
        grid=(1,),
        out_shape=GROUP_OUT
        + (jax.ShapeDtypeStruct(TURNED, bf16), jax.ShapeDtypeStruct(NATURAL, bf16)),
        in_specs=[
            SMEM,
            SMEM,
            full_spec((ROWS, TILE)),
            omega_spec(2),
            full_spec((NB, ROWS, BLK)),
            full_spec(TURNED),
            full_spec(TURNED),
        ],
        out_specs=GROUP_SPECS + (full_spec(TURNED), full_spec(NATURAL)),
        scratch_shapes=[pltpu.VMEM((NB, ROWS, BLK), f32), pltpu.VMEM(NATURAL, bf16)],
        compiler_params=params(),
        cost_estimate=pl.CostEstimate(
            flops=5 * KMAX * ROWS * 256 * 256, bytes_accessed=8 << 20, transcendentals=0
        ),
    )(slots, where, tile, omega, before, below, centre)


def near_blocks(slots, where, below, centre, above, pieces):
    return pl.pallas_call(
        near_kernel,
        name="near_blocks",
        grid=(1,),
        out_shape=GROUP_OUT,
        in_specs=[SMEM, SMEM]
        + [full_spec(TURNED)] * 3
        + [full_spec(NATURAL)],
        out_specs=GROUP_SPECS,
        compiler_params=params(),
        cost_estimate=pl.CostEstimate(
            flops=3 * KMAX * ROWS * 256 * 256, bytes_accessed=8 << 20, transcendentals=0
        ),
    )(slots, where, below, centre, above, pieces)


def proximal(place, slots, total, left, right, omega):
    return pl.pallas_call(
        proximal_kernel,
        name="proximal",
        grid_spec=pltpu.PrefetchScalarGridSpec(
            num_scalar_prefetch=2,
            grid=(1,),
            in_specs=[
                pl.BlockSpec((3, BLK, BLK), lambda i, place, slots: (0, 0, 0)),
                pl.BlockSpec((BLK, BLK), lambda i, place, slots: (0, 0)),
                pl.BlockSpec((BLK, BLK), lambda i, place, slots: (0, 0)),
                pl.BlockSpec(
                    (1, 3, 1, BLK, BLK), lambda i, place, slots: (0, 0, place[0], 0, 0)
                ),
            ],
            out_specs=pl.BlockSpec(
                (1, 3, 1, BLK, BLK), lambda i, place, slots: (0, 0, 0, 0, 0)
            ),
        ),
        out_shape=jax.ShapeDtypeStruct((1, 3, 1, BLK, BLK), f32),
        compiler_params=params(),
        cost_estimate=pl.CostEstimate(
            flops=20 * 3 * BLK * BLK, bytes_accessed=1 << 19, transcendentals=0
        ),
    )(place, slots, total, left, right, omega)


def shifted(value, axis, steps):
    count = lax.axis_size(axis)
    pairs = [(source, (source + steps) % count) for source in range(count)]
    return lax.ppermute(value, axis, pairs)


def x_exchange(value, step):
    pairs = []
    for x in range(4):
        for core in range(2):
            partner = x ^ 1 if core == step else 3 - x
            pairs.append((2 * x + core, 2 * partner + core))
    return lax.ppermute(value, ("x", "core"), pairs)


def after(value, earlier):
    return lax.optimization_barrier((value, earlier))[0]


def on_device(observations, omega, block_slots):
    x, y_hi, core = (lax.axis_index(n).astype(jnp.int32) for n in ("x", "y_hi", "core"))
    where = jnp.stack([x, y_hi, core])
    place = 4 * x + 2 * y_hi + core
    from_below = shifted(observations, "col", 1)
    from_above = shifted(observations, "col", -1)
    residual, centre = partial(1, block_slots, observations, omega)
    residual, below = partial(0, block_slots, from_below, omega, residual)
    far_keep, far_pass, far_send, above, pieces = far_blocks(
        block_slots, where, from_above, omega, residual, below, centre
    )
    far_got = shifted(far_send, "core", 1)
    far_out = far_pass + far_got[2:]
    pieces = after(pieces, far_out)
    far_first = x_exchange(far_out, 0)
    near_keep, near_pass, near_send = near_blocks(
        block_slots, where, below, centre, above, pieces
    )
    near_got = shifted(near_send, "core", 1)
    far_out = far_keep[1] + far_got[1] + far_first[1]
    near_out = after(near_pass + near_got[2:], far_out)
    far_second = x_exchange(far_out, 1)
    near_first = x_exchange(near_out, 0)
    far_sum = far_keep[0] + far_got[0] + far_first[0] + far_second
    near_out = near_keep[1] + near_got[1] + near_first[1]
    near_out = after(near_out, far_sum)
    other = shifted(far_sum, "y_hi", 1)
    near_second = x_exchange(near_out, 1)
    near_sum = near_keep[0] + near_got[0] + near_first[0] + near_second
    total = near_sum + other
    left = shifted(total[2], "col", 1)
    right = shifted(total[0], "col", -1)
    return proximal(place.reshape(1), block_slots, total, left, right, omega)


def solution(mesh):
    devices = mesh.devices.reshape(4, 2, 2, 32)
    fine = Mesh(devices, ("x", "y_hi", "core", "col"))
    rows = ("x", "y_hi", "core")
    return jax.shard_map(
        on_device,
        mesh=fine,
        in_specs=(P(rows, "col"), P("col", None, None, None, None), P("col", None, None)),
        out_specs=P("col", None, rows, None, None),
        check_vma=False,
    )
```

```python
import jax
import jax.numpy as jnp
from jax import lax
from jax.experimental import pallas as pl
from jax.experimental.pallas import tpu as pltpu
from jax.sharding import Mesh, PartitionSpec as P

TILE = 1024
BLK = 128
NB = TILE // BLK
KMAX = 16
ROWS = 256
SAMPLES = 4096
step_size = 0.5
penalty = 0.1
f32 = jnp.float32
bf16 = jnp.bfloat16
VMEM_LIMIT = 24 * 1024 * 1024


def split(value):
    high = value.astype(bf16)
    low = (value - high.astype(f32)).astype(bf16)
    return high, low


def split_tile(x_ref, natural_ref, turned_ref, start=0):
    rows = x_ref.shape[0]
    for a in range(NB):
        block = x_ref[:, a * BLK : (a + 1) * BLK]
        high, low = split(block)
        natural_ref[a, :, :BLK] = high
        natural_ref[a, :, BLK:] = low
        high, low = split(block.T)
        turned_ref[a, :BLK, start : start + rows] = high
        turned_ref[a, BLK:, start : start + rows] = low


def add_products(slots_ref, omega_ref, natural_ref, residual_ref, offset, start=0):
    rows = natural_ref.shape[1]

    def body(j, carry):
        slot = slots_ref[0, offset, j]
        active = slot >= 0
        place = jnp.maximum(slot, 0)
        a = place // NB
        b = place % NB
        weight = jnp.where(active, omega_ref[0, 0, j], 0.0)
        high, low = split(weight)
        half = jnp.concatenate([high, low], axis=1)
        weights = jnp.concatenate([half, half], axis=0)
        out = jnp.dot(natural_ref[a], weights, preferred_element_type=f32)
        residual_ref[b, start : start + rows] += out[:, :BLK] + out[:, BLK:]
        return carry

    lax.fori_loop(0, KMAX, body, 0, unroll=4)


def partial_kernel(offset, first, *refs):
    if first:
        slots_ref, x_ref, omega_ref, residual_ref, turned_ref, natural_ref = refs
        residual_ref[...] = jnp.zeros_like(residual_ref)
    else:
        slots_ref, x_ref, omega_ref, before_ref, residual_ref, turned_ref, natural_ref = refs
        residual_ref[...] = before_ref[...]
    split_tile(x_ref, natural_ref, turned_ref)
    add_products(slots_ref, omega_ref, natural_ref, residual_ref, offset)


def quadrant_sum(out):
    out = out[:BLK] + out[BLK:]
    return out[:, :BLK] + out[:, BLK:]


def slot_block(slots_ref, e, j, turned, pieces_ref):
    place = jnp.maximum(slots_ref[0, e, j], 0)
    out = jnp.dot(
        turned[e][place // NB], pieces_ref[place % NB], preferred_element_type=f32
    )
    return quadrant_sum(out)


def forward_kernel(
    slots_ref, where_ref, x_ref, omega_ref, before_ref, half_ref, below_ref, centre_ref,
    keep_ref, pass_ref, send_ref, residual_ref, natural_ref, above_ref, pieces_ref,
):
    residual_ref[...] = before_ref[...]
    done = half_ref.shape[2]
    above_ref[:, :, :done] = half_ref[...]
    split_tile(x_ref, natural_ref, above_ref, done)
    add_products(slots_ref, omega_ref, natural_ref, residual_ref, 2, done)
    for b in range(NB):
        high, low = split(residual_ref[b])
        pieces_ref[b, :, :BLK] = high
        pieces_ref[b, :, BLK:] = low
    turned = (below_ref, centre_ref, above_ref)
    x, own_y, core = where_ref[0], where_ref[1], where_ref[2]
    even_pair, odd_pair = x ^ 1, 3 - x
    first = jnp.where(core == 0, even_pair, odd_pair)
    second = jnp.where(core == 0, odd_pair, even_pair)
    for r, x_of in enumerate((x, second, first, x ^ 2)):
        for q in range(2):
            i = 2 * x_of + (own_y ^ q)
            for e in range(3):
                even = slot_block(slots_ref, e, 2 * i, turned, pieces_ref)
                odd = slot_block(slots_ref, e, 2 * i + 1, turned, pieces_ref)
                if e == 1:
                    even_turned, odd_turned = even.T, odd.T
                    diagonal = i < NB // 2
                    even, odd = (
                        even + jnp.where(diagonal, even_turned, odd_turned),
                        odd + jnp.where(diagonal, odd_turned, even_turned),
                    )
                own_ref = keep_ref if r < 2 else pass_ref
                own_ref[r % 2, q, e] = jnp.where(core == 0, even, odd)
                send_ref[(0, 2, 1, 3)[r], q, e] = jnp.where(core == 0, odd, even)


def proximal_kernel(
    place_ref, slots_ref, near_ref, other_ref, right_ref, left_ref, omega_ref, out_ref
):
    j = place_ref[0]
    rows = lax.broadcasted_iota(jnp.int32, (BLK, BLK), 0)
    columns = lax.broadcasted_iota(jnp.int32, (BLK, BLK), 1)
    for e in range(3):
        slot = slots_ref[0, e, j]
        total = near_ref[e] + other_ref[e]
        if e == 0:
            total = total + left_ref[...].T
        if e == 2:
            total = total + right_ref[...].T
        gradient = total * (0.5 / SAMPLES)
        omega = omega_ref[0, e, 0]
        if e == 1:
            diagonal = (slot >= 0) & (slot // NB == slot % NB)
            on_diagonal = (rows == columns) & diagonal
            inverse = 1.0 / jnp.where(on_diagonal, omega, 1.0)
            gradient = gradient - jnp.where(on_diagonal, inverse, 0.0)
        trial = omega - step_size * gradient
        shrunk = jnp.maximum(jnp.abs(trial) - step_size * penalty, 0.0)
        result = jnp.where(trial < 0.0, -shrunk, shrunk)
        if e == 1:
            result = jnp.where(on_diagonal, trial, result)
        out_ref[0, e, 0] = jnp.where(slot >= 0, result, 0.0)


def params():
    return pltpu.CompilerParams(vmem_limit_bytes=VMEM_LIMIT)


SMEM = pl.BlockSpec(memory_space=pltpu.SMEM)
WHOLE = pl.BlockSpec(memory_space=pltpu.VMEM)
TURNED = (NB, 2 * BLK, ROWS)
NATURAL = (NB, ROWS, 2 * BLK)


def omega_spec(offset):
    return pl.BlockSpec((1, 1, KMAX, BLK, BLK), lambda i: (0, offset, 0, 0, 0))


def full_spec(shape):
    return pl.BlockSpec(shape, lambda i: (0,) * len(shape))


def partial(offset, slots, tile, omega, before=None):
    first = before is None
    rows = tile.shape[0]
    turned = (NB, 2 * BLK, rows)
    in_specs = [SMEM, full_spec((rows, TILE)), omega_spec(offset)]
    inputs = [slots, tile, omega]
    if not first:
        in_specs.append(full_spec((NB, ROWS, BLK)))
        inputs.append(before)
    return pl.pallas_call(
        lambda *refs: partial_kernel(offset, first, *refs),
        name="partial_residual",
        grid=(1,),
        out_shape=(
            jax.ShapeDtypeStruct((NB, ROWS, BLK), f32),
            jax.ShapeDtypeStruct(turned, bf16),
        ),
        in_specs=in_specs,
        out_specs=(full_spec((NB, ROWS, BLK)), full_spec(turned)),
        scratch_shapes=[pltpu.VMEM((NB, rows, 2 * BLK), bf16)],
        compiler_params=params(),
        cost_estimate=pl.CostEstimate(
            flops=2 * KMAX * rows * 256 * 256, bytes_accessed=5 << 20, transcendentals=0
        ),
    )(*inputs)


HALF = (2, 2, 3, BLK, BLK)
WAY = (4, 2, 3, BLK, BLK)


def forward_blocks(slots, where, tile, omega, before, half, below, centre):
    rows = tile.shape[0]
    return pl.pallas_call(
        forward_kernel,
        name="forward_blocks",
        grid=(1,),
        out_shape=tuple(jax.ShapeDtypeStruct(shape, f32) for shape in (HALF, HALF, WAY)),
        in_specs=[
            SMEM,
            SMEM,
            full_spec((rows, TILE)),
            omega_spec(2),
            full_spec((NB, ROWS, BLK)),
            full_spec((NB, 2 * BLK, ROWS - rows)),
            full_spec(TURNED),
            full_spec(TURNED),
        ],
        out_specs=tuple(full_spec(shape) for shape in (HALF, HALF, WAY)),
        scratch_shapes=[
            pltpu.VMEM((NB, ROWS, BLK), f32),
            pltpu.VMEM((NB, rows, 2 * BLK), bf16),
            pltpu.VMEM(TURNED, bf16),
            pltpu.VMEM(NATURAL, bf16),
        ],
        compiler_params=params(),
        cost_estimate=pl.CostEstimate(
            flops=7 * KMAX * ROWS * 256 * 256, bytes_accessed=8 << 20, transcendentals=0
        ),
    )(slots, where, tile, omega, before, half, below, centre)


def proximal(place, slots, near, other, right, left, omega):
    return pl.pallas_call(
        proximal_kernel,
        name="proximal",
        grid_spec=pltpu.PrefetchScalarGridSpec(
            num_scalar_prefetch=2,
            grid=(1,),
            in_specs=[
                pl.BlockSpec((3, BLK, BLK), lambda i, place, slots: (0, 0, 0)),
                pl.BlockSpec((3, BLK, BLK), lambda i, place, slots: (0, 0, 0)),
                pl.BlockSpec((BLK, BLK), lambda i, place, slots: (0, 0)),
                pl.BlockSpec((BLK, BLK), lambda i, place, slots: (0, 0)),
                pl.BlockSpec(
                    (1, 3, 1, BLK, BLK), lambda i, place, slots: (0, 0, place[0], 0, 0)
                ),
            ],
            out_specs=pl.BlockSpec(
                (1, 3, 1, BLK, BLK), lambda i, place, slots: (0, 0, 0, 0, 0)
            ),
        ),
        out_shape=jax.ShapeDtypeStruct((1, 3, 1, BLK, BLK), f32),
        compiler_params=params(),
        cost_estimate=pl.CostEstimate(
            flops=20 * 3 * BLK * BLK, bytes_accessed=1 << 19, transcendentals=0
        ),
    )(place, slots, near, other, right, left, omega)


def shifted(value, axis, steps):
    count = lax.axis_size(axis)
    pairs = [(source, (source + steps) % count) for source in range(count)]
    return lax.ppermute(value, axis, pairs)


def x_exchange(value, step):
    pairs = []
    for x in range(4):
        for core in range(2):
            partner = x ^ 1 if core == step else 3 - x
            pairs.append((2 * x + core, 2 * partner + core))
    return lax.ppermute(value, ("x", "core"), pairs)


def on_device(observations, omega, block_slots):
    x, y_hi, core = (lax.axis_index(n).astype(jnp.int32) for n in ("x", "y_hi", "core"))
    where = jnp.stack([x, y_hi, core])
    place = 4 * x + 2 * y_hi + core
    cut = ROWS // 2
    from_below = shifted(observations, "col", 1)
    above_early = shifted(observations[:cut], "col", -1)
    above_late = shifted(observations[cut:], "col", -1)
    residual, centre = partial(1, block_slots, observations, omega)
    residual, below = partial(0, block_slots, from_below, omega, residual)
    residual, half = partial(2, block_slots, above_early, omega, residual)
    keep, out, send = forward_blocks(
        block_slots, where, above_late, omega, residual, half, below, centre
    )
    got = shifted(send, "core", 1)
    first = x_exchange(out + got[2:], 0)
    second = x_exchange(keep[1] + got[1] + first[1], 1)
    kept = keep[0] + got[0] + first[0]
    other = shifted(kept[1] + second[1], "y_hi", 1)
    near = kept[0] + second[0]
    right = shifted(near[0] + other[0], "col", -1)
    left = shifted(near[2] + other[2], "col", 1)
    return proximal(place.reshape(1), block_slots, near, other, right, left, omega)


def solution(mesh):
    devices = mesh.devices.reshape(4, 2, 2, 32)
    fine = Mesh(devices, ("x", "y_hi", "core", "col"))
    rows = ("x", "y_hi", "core")
    return jax.shard_map(
        on_device,
        mesh=fine,
        in_specs=(P(rows, "col"), P("col", None, None, None, None), P("col", None, None)),
        out_specs=P("col", None, rows, None, None),
        check_vma=False,
    )
```

```python
import jax
import jax.numpy as jnp
from jax import lax
from jax.experimental import pallas as pl
from jax.experimental.pallas import tpu as pltpu
from jax.sharding import Mesh, PartitionSpec as P

TILE = 1024
BLK = 128
NB = TILE // BLK
KMAX = 16
ROWS = 256
SAMPLES = 4096
step_size = 0.5
penalty = 0.1
f32 = jnp.float32
bf16 = jnp.bfloat16
VMEM_LIMIT = 24 * 1024 * 1024


def split(value):
    high = value.astype(bf16)
    low = (value - high.astype(f32)).astype(bf16)
    return high, low


def split_tile(x_ref, natural_ref, turned_ref, start=0):
    rows = x_ref.shape[0]
    for a in range(NB):
        block = x_ref[:, a * BLK : (a + 1) * BLK]
        high, low = split(block)
        natural_ref[a, :, :BLK] = high
        natural_ref[a, :, BLK:] = low
        high, low = split(block.T)
        turned_ref[a, :BLK, start : start + rows] = high
        turned_ref[a, BLK:, start : start + rows] = low


def add_products(slots_ref, omega_ref, natural_ref, residual_ref, offset, start=0):
    rows = natural_ref.shape[1]

    def body(j, carry):
        slot = slots_ref[0, offset, j]
        active = slot >= 0
        place = jnp.maximum(slot, 0)
        a = place // NB
        b = place % NB
        weight = jnp.where(active, omega_ref[0, 0, j], 0.0)
        high, low = split(weight)
        half = jnp.concatenate([high, low], axis=1)
        weights = jnp.concatenate([half, half], axis=0)
        out = jnp.dot(natural_ref[a], weights, preferred_element_type=f32)
        residual_ref[b, start : start + rows] += out[:, :BLK] + out[:, BLK:]
        return carry

    lax.fori_loop(0, KMAX, body, 0, unroll=4)


def partial_kernel(offset, first, *refs):
    if first:
        slots_ref, x_ref, omega_ref, residual_ref, turned_ref, natural_ref = refs
        residual_ref[...] = jnp.zeros_like(residual_ref)
    else:
        slots_ref, x_ref, omega_ref, before_ref, residual_ref, turned_ref, natural_ref = refs
        residual_ref[...] = before_ref[...]
    split_tile(x_ref, natural_ref, turned_ref)
    add_products(slots_ref, omega_ref, natural_ref, residual_ref, offset)


def quadrant_sum(out):
    out = out[:BLK] + out[BLK:]
    return out[:, :BLK] + out[:, BLK:]


def slot_block(slots_ref, e, j, turned, pieces_ref):
    place = jnp.maximum(slots_ref[0, e, j], 0)
    out = jnp.dot(
        turned[e][place // NB], pieces_ref[place % NB], preferred_element_type=f32
    )
    return quadrant_sum(out)


def forward_kernel(
    slots_ref, where_ref, x_ref, omega_ref, before_ref, half_ref, below_ref, centre_ref,
    keep_ref, pass_ref, send_ref, residual_ref, natural_ref, above_ref, pieces_ref,
):
    residual_ref[...] = before_ref[...]
    done = half_ref.shape[2]
    above_ref[:, :, :done] = half_ref[...]
    split_tile(x_ref, natural_ref, above_ref, done)
    add_products(slots_ref, omega_ref, natural_ref, residual_ref, 2, done)
    for b in range(NB):
        high, low = split(residual_ref[b])
        pieces_ref[b, :, :BLK] = high
        pieces_ref[b, :, BLK:] = low
    turned = (below_ref, centre_ref, above_ref)
    x, own_y, core = where_ref[0], where_ref[1], where_ref[2]
    even_pair, odd_pair = x ^ 1, 3 - x
    first = jnp.where(core == 0, even_pair, odd_pair)
    second = jnp.where(core == 0, odd_pair, even_pair)
    for r, x_of in enumerate((x, second, first, x ^ 2)):
        for q in range(2):
            i = 2 * x_of + (own_y ^ q)
            for e in range(3):
                even = slot_block(slots_ref, e, 2 * i, turned, pieces_ref)
                odd = slot_block(slots_ref, e, 2 * i + 1, turned, pieces_ref)
                if e == 1:
                    even_turned, odd_turned = even.T, odd.T
                    diagonal = i < NB // 2
                    even, odd = (
                        even + jnp.where(diagonal, even_turned, odd_turned),
                        odd + jnp.where(diagonal, odd_turned, even_turned),
                    )
                own_ref = keep_ref if r < 2 else pass_ref
                own_ref[r % 2, q, e] = jnp.where(core == 0, even, odd)
                send_ref[(0, 2, 1, 3)[r], q, e] = jnp.where(core == 0, odd, even)


def proximal_kernel(
    place_ref, slots_ref, near_ref, right_ref, left_ref, far_right_ref, far_left_ref,
    other_ref, omega_ref, out_ref,
):
    j = place_ref[0]
    rows = lax.broadcasted_iota(jnp.int32, (BLK, BLK), 0)
    columns = lax.broadcasted_iota(jnp.int32, (BLK, BLK), 1)
    for e in range(3):
        slot = slots_ref[0, e, j]
        total = near_ref[e] + other_ref[e]
        if e == 0:
            total = total + (left_ref[...] + far_left_ref[...]).T
        if e == 2:
            total = total + (right_ref[...] + far_right_ref[...]).T
        gradient = total * (0.5 / SAMPLES)
        omega = omega_ref[0, e, 0]
        if e == 1:
            diagonal = (slot >= 0) & (slot // NB == slot % NB)
            on_diagonal = (rows == columns) & diagonal
            inverse = 1.0 / jnp.where(on_diagonal, omega, 1.0)
            gradient = gradient - jnp.where(on_diagonal, inverse, 0.0)
        trial = omega - step_size * gradient
        shrunk = jnp.maximum(jnp.abs(trial) - step_size * penalty, 0.0)
        result = jnp.where(trial < 0.0, -shrunk, shrunk)
        if e == 1:
            result = jnp.where(on_diagonal, trial, result)
        out_ref[0, e, 0] = jnp.where(slot >= 0, result, 0.0)


def params():
    return pltpu.CompilerParams(vmem_limit_bytes=VMEM_LIMIT)


SMEM = pl.BlockSpec(memory_space=pltpu.SMEM)
WHOLE = pl.BlockSpec(memory_space=pltpu.VMEM)
TURNED = (NB, 2 * BLK, ROWS)
NATURAL = (NB, ROWS, 2 * BLK)


def omega_spec(offset):
    return pl.BlockSpec((1, 1, KMAX, BLK, BLK), lambda i: (0, offset, 0, 0, 0))


def full_spec(shape):
    return pl.BlockSpec(shape, lambda i: (0,) * len(shape))


def partial(offset, slots, tile, omega, before=None):
    first = before is None
    rows = tile.shape[0]
    turned = (NB, 2 * BLK, rows)
    in_specs = [SMEM, full_spec((rows, TILE)), omega_spec(offset)]
    inputs = [slots, tile, omega]
    if not first:
        in_specs.append(full_spec((NB, ROWS, BLK)))
        inputs.append(before)
    return pl.pallas_call(
        lambda *refs: partial_kernel(offset, first, *refs),
        name="partial_residual",
        grid=(1,),
        out_shape=(
            jax.ShapeDtypeStruct((NB, ROWS, BLK), f32),
            jax.ShapeDtypeStruct(turned, bf16),
        ),
        in_specs=in_specs,
        out_specs=(full_spec((NB, ROWS, BLK)), full_spec(turned)),
        scratch_shapes=[pltpu.VMEM((NB, rows, 2 * BLK), bf16)],
        compiler_params=params(),
        cost_estimate=pl.CostEstimate(
            flops=2 * KMAX * rows * 256 * 256, bytes_accessed=5 << 20, transcendentals=0
        ),
    )(*inputs)


HALF = (2, 2, 3, BLK, BLK)
WAY = (4, 2, 3, BLK, BLK)


def forward_blocks(slots, where, tile, omega, before, half, below, centre):
    rows = tile.shape[0]
    return pl.pallas_call(
        forward_kernel,
        name="forward_blocks",
        grid=(1,),
        out_shape=tuple(jax.ShapeDtypeStruct(shape, f32) for shape in (HALF, HALF, WAY)),
        in_specs=[
            SMEM,
            SMEM,
            full_spec((rows, TILE)),
            omega_spec(2),
            full_spec((NB, ROWS, BLK)),
            full_spec((NB, 2 * BLK, ROWS - rows)),
            full_spec(TURNED),
            full_spec(TURNED),
        ],
        out_specs=tuple(full_spec(shape) for shape in (HALF, HALF, WAY)),
        scratch_shapes=[
            pltpu.VMEM((NB, ROWS, BLK), f32),
            pltpu.VMEM((NB, rows, 2 * BLK), bf16),
            pltpu.VMEM(TURNED, bf16),
            pltpu.VMEM(NATURAL, bf16),
        ],
        compiler_params=params(),
        cost_estimate=pl.CostEstimate(
            flops=7 * KMAX * ROWS * 256 * 256, bytes_accessed=8 << 20, transcendentals=0
        ),
    )(slots, where, tile, omega, before, half, below, centre)


def proximal(place, slots, near, sums, omega):
    block = pl.BlockSpec((BLK, BLK), lambda i, place, slots: (0, 0))
    triple = pl.BlockSpec((3, BLK, BLK), lambda i, place, slots: (0, 0, 0))
    own = pl.BlockSpec((1, 3, 1, BLK, BLK), lambda i, place, slots: (0, 0, place[0], 0, 0))
    return pl.pallas_call(
        proximal_kernel,
        name="proximal",
        grid_spec=pltpu.PrefetchScalarGridSpec(
            num_scalar_prefetch=2,
            grid=(1,),
            in_specs=[triple] + [block] * 4 + [triple, own],
            out_specs=pl.BlockSpec(
                (1, 3, 1, BLK, BLK), lambda i, place, slots: (0, 0, 0, 0, 0)
            ),
        ),
        out_shape=jax.ShapeDtypeStruct((1, 3, 1, BLK, BLK), f32),
        compiler_params=params(),
        cost_estimate=pl.CostEstimate(
            flops=20 * 3 * BLK * BLK, bytes_accessed=1 << 19, transcendentals=0
        ),
    )(place, slots, near, *sums, omega)


def shifted(value, axis, steps):
    count = lax.axis_size(axis)
    pairs = [(source, (source + steps) % count) for source in range(count)]
    return lax.ppermute(value, axis, pairs)


def x_exchange(value, step):
    pairs = []
    for x in range(4):
        for core in range(2):
            partner = x ^ 1 if core == step else 3 - x
            pairs.append((2 * x + core, 2 * partner + core))
    return lax.ppermute(value, ("x", "core"), pairs)


def across(value, steps):
    count = lax.axis_size("col")
    pairs = [
        (y * count + t, (1 - y) * count + (t + steps) % count)
        for y in range(2)
        for t in range(count)
    ]
    return lax.ppermute(value, ("y_hi", "col"), pairs)


def on_device(observations, omega, block_slots):
    x, y_hi, core = (lax.axis_index(n).astype(jnp.int32) for n in ("x", "y_hi", "core"))
    where = jnp.stack([x, y_hi, core])
    place = 4 * x + 2 * y_hi + core
    cut = ROWS // 2
    from_below = shifted(observations, "col", 1)
    above_early = shifted(observations[:cut], "col", -1)
    above_late = shifted(observations[cut:], "col", -1)
    residual, centre = partial(1, block_slots, observations, omega)
    residual, below = partial(0, block_slots, from_below, omega, residual)
    residual, half = partial(2, block_slots, above_early, omega, residual)
    keep, out, send = forward_blocks(
        block_slots, where, above_late, omega, residual, half, below, centre
    )
    got = shifted(send, "core", 1)
    first = x_exchange(out + got[2:], 0)
    second = x_exchange(keep[1] + got[1] + first[1], 1)
    kept = keep[0] + got[0] + first[0]
    near = kept[0] + second[0]
    far = kept[1] + second[1]
    sums = (
        shifted(kept[0, 0] + second[0, 0], "col", -1),
        shifted(kept[0, 2] + second[0, 2], "col", 1),
        across(kept[1, 0] + second[1, 0], -1),
        across(kept[1, 2] + second[1, 2], 1),
        shifted(far, "y_hi", 1),
    )
    return proximal(place.reshape(1), block_slots, near, sums, omega)


def solution(mesh):
    devices = mesh.devices.reshape(4, 2, 2, 32)
    fine = Mesh(devices, ("x", "y_hi", "core", "col"))
    rows = ("x", "y_hi", "core")
    return jax.shard_map(
        on_device,
        mesh=fine,
        in_specs=(P(rows, "col"), P("col", None, None, None, None), P("col", None, None)),
        out_specs=P("col", None, rows, None, None),
        check_vma=False,
    )
```

```python
import jax
import jax.numpy as jnp
from jax import lax
from jax.experimental import pallas as pl
from jax.experimental.pallas import tpu as pltpu
from jax.sharding import Mesh, PartitionSpec as P

TILE = 1024
BLK = 128
NB = TILE // BLK
KMAX = 16
ROWS = 256
SAMPLES = 4096
step_size = 0.5
penalty = 0.1
f32 = jnp.float32
bf16 = jnp.bfloat16
VMEM_LIMIT = 16 * 1024 * 1024


def split(value):
    high = value.astype(bf16)
    low = (value - high.astype(f32)).astype(bf16)
    return high, low


def split_tile(x_ref, natural_ref, turned_ref, start=0):
    rows = x_ref.shape[0]
    for a in range(NB):
        block = x_ref[:, a * BLK : (a + 1) * BLK]
        high, low = split(block)
        natural_ref[a, :, :BLK] = high
        natural_ref[a, :, BLK:] = low
        high, low = split(block.T)
        turned_ref[a, :BLK, start : start + rows] = high
        turned_ref[a, BLK:, start : start + rows] = low


def add_products(slots_ref, omega_ref, natural_ref, residual_ref, offset, start=0):
    rows = natural_ref.shape[1]

    def body(j, carry):
        slot = slots_ref[0, offset, j]
        active = slot >= 0
        place = jnp.maximum(slot, 0)
        a = place // NB
        b = place % NB
        weight = jnp.where(active, omega_ref[0, 0, j], 0.0)
        high, low = split(weight)
        half = jnp.concatenate([high, low], axis=1)
        weights = jnp.concatenate([half, half], axis=0)
        out = jnp.dot(natural_ref[a], weights, preferred_element_type=f32)
        residual_ref[b, start : start + rows] += out[:, :BLK] + out[:, BLK:]
        return carry

    lax.fori_loop(0, KMAX, body, 0, unroll=4)


def partial_kernel(offset, first, *refs):
    if first:
        slots_ref, x_ref, omega_ref, residual_ref, turned_ref, natural_ref = refs
        residual_ref[...] = jnp.zeros_like(residual_ref)
    else:
        slots_ref, x_ref, omega_ref, before_ref, residual_ref, turned_ref, natural_ref = refs
        residual_ref[...] = before_ref[...]
    split_tile(x_ref, natural_ref, turned_ref)
    add_products(slots_ref, omega_ref, natural_ref, residual_ref, offset)


def quadrant_sum(out):
    out = out[:BLK] + out[BLK:]
    return out[:, :BLK] + out[:, BLK:]


def slot_block(slots_ref, e, j, turned, pieces_ref):
    place = jnp.maximum(slots_ref[0, e, j], 0)
    out = jnp.dot(
        turned[e][place // NB], pieces_ref[place % NB], preferred_element_type=f32
    )
    return quadrant_sum(out)


def group_products(slots_ref, where_ref, turned, pieces_ref, y_hi, keep_ref, pass_ref, send_ref):
    x, core = where_ref[0], where_ref[2]
    even_pair, odd_pair = x ^ 1, 3 - x
    first = jnp.where(core == 0, even_pair, odd_pair)
    second = jnp.where(core == 0, odd_pair, even_pair)
    for r, x_of in enumerate((x, second, first, x ^ 2)):
        i = 2 * x_of + y_hi
        for e in range(3):
            even = slot_block(slots_ref, e, 2 * i, turned, pieces_ref)
            odd = slot_block(slots_ref, e, 2 * i + 1, turned, pieces_ref)
            if e == 1:
                even_turned, odd_turned = even.T, odd.T
                diagonal = i < NB // 2
                even, odd = (
                    even + jnp.where(diagonal, even_turned, odd_turned),
                    odd + jnp.where(diagonal, odd_turned, even_turned),
                )
            own_ref = keep_ref if r < 2 else pass_ref
            own_ref[r % 2, e] = jnp.where(core == 0, even, odd)
            send_ref[(0, 2, 1, 3)[r], e] = jnp.where(core == 0, odd, even)


def far_kernel(
    slots_ref, where_ref, x_ref, omega_ref, before_ref, half_ref, below_ref, centre_ref,
    keep_ref, pass_ref, send_ref, above_ref, pieces_ref, residual_ref, natural_ref,
):
    residual_ref[...] = before_ref[...]
    done = half_ref.shape[2]
    above_ref[:, :, :done] = half_ref[...]
    split_tile(x_ref, natural_ref, above_ref, done)
    add_products(slots_ref, omega_ref, natural_ref, residual_ref, 2, done)
    for b in range(NB):
        high, low = split(residual_ref[b])
        pieces_ref[b, :, :BLK] = high
        pieces_ref[b, :, BLK:] = low
    group_products(
        slots_ref, where_ref, (below_ref, centre_ref, above_ref), pieces_ref,
        1 - where_ref[1], keep_ref, pass_ref, send_ref,
    )


def near_kernel(
    slots_ref, where_ref, below_ref, centre_ref, above_ref, pieces_ref,
    keep_ref, pass_ref, send_ref,
):
    group_products(
        slots_ref, where_ref, (below_ref, centre_ref, above_ref), pieces_ref,
        where_ref[1], keep_ref, pass_ref, send_ref,
    )


def proximal_kernel(
    where_ref, slots_ref, near_ref, other_ref, late_ref, early_ref, omega_ref, out_ref
):
    j = where_ref[3]
    odd_tile = where_ref[4] == 1
    rows = lax.broadcasted_iota(jnp.int32, (BLK, BLK), 0)
    columns = lax.broadcasted_iota(jnp.int32, (BLK, BLK), 1)
    for e in range(3):
        slot = slots_ref[0, e, j]
        total = near_ref[e] + other_ref[e]
        if e == 0:
            total = total + jnp.where(odd_tile, early_ref[...], late_ref[...]).T
        if e == 2:
            total = total + jnp.where(odd_tile, late_ref[...], early_ref[...]).T
        gradient = total * (0.5 / SAMPLES)
        omega = omega_ref[0, e, 0]
        if e == 1:
            diagonal = (slot >= 0) & (slot // NB == slot % NB)
            on_diagonal = (rows == columns) & diagonal
            inverse = 1.0 / jnp.where(on_diagonal, omega, 1.0)
            gradient = gradient - jnp.where(on_diagonal, inverse, 0.0)
        trial = omega - step_size * gradient
        shrunk = jnp.maximum(jnp.abs(trial) - step_size * penalty, 0.0)
        result = jnp.where(trial < 0.0, -shrunk, shrunk)
        if e == 1:
            result = jnp.where(on_diagonal, trial, result)
        out_ref[0, e, 0] = jnp.where(slot >= 0, result, 0.0)


def params():
    return pltpu.CompilerParams(vmem_limit_bytes=VMEM_LIMIT)


SMEM = pl.BlockSpec(memory_space=pltpu.SMEM)
WHOLE = pl.BlockSpec(memory_space=pltpu.VMEM)
TURNED = (NB, 2 * BLK, ROWS)
NATURAL = (NB, ROWS, 2 * BLK)


def omega_spec(offset):
    return pl.BlockSpec((1, 1, KMAX, BLK, BLK), lambda i: (0, offset, 0, 0, 0))


def full_spec(shape):
    return pl.BlockSpec(shape, lambda i: (0,) * len(shape))


def partial(offset, slots, tile, omega, before=None):
    first = before is None
    rows = tile.shape[0]
    turned = (NB, 2 * BLK, rows)
    in_specs = [SMEM, full_spec((rows, TILE)), omega_spec(offset)]
    inputs = [slots, tile, omega]
    if not first:
        in_specs.append(full_spec((NB, ROWS, BLK)))
        inputs.append(before)
    return pl.pallas_call(
        lambda *refs: partial_kernel(offset, first, *refs),
        name="partial_residual",
        grid=(1,),
        out_shape=(
            jax.ShapeDtypeStruct((NB, ROWS, BLK), f32),
            jax.ShapeDtypeStruct(turned, bf16),
        ),
        in_specs=in_specs,
        out_specs=(full_spec((NB, ROWS, BLK)), full_spec(turned)),
        scratch_shapes=[pltpu.VMEM((NB, rows, 2 * BLK), bf16)],
        compiler_params=params(),
        cost_estimate=pl.CostEstimate(
            flops=2 * KMAX * rows * 256 * 256, bytes_accessed=5 << 20, transcendentals=0
        ),
    )(*inputs)


HALF = (2, 3, BLK, BLK)
WAY = (4, 3, BLK, BLK)
GROUP_OUT = tuple(jax.ShapeDtypeStruct(shape, f32) for shape in (HALF, HALF, WAY))
GROUP_SPECS = tuple(full_spec(shape) for shape in (HALF, HALF, WAY))


def far_blocks(slots, where, tile, omega, before, half, below, centre):
    rows = tile.shape[0]
    return pl.pallas_call(
        far_kernel,
        name="far_blocks",
        grid=(1,),
        out_shape=GROUP_OUT
        + (jax.ShapeDtypeStruct(TURNED, bf16), jax.ShapeDtypeStruct(NATURAL, bf16)),
        in_specs=[
            SMEM,
            SMEM,
            full_spec((rows, TILE)),
            omega_spec(2),
            full_spec((NB, ROWS, BLK)),
            full_spec((NB, 2 * BLK, ROWS - rows)),
            full_spec(TURNED),
            full_spec(TURNED),
        ],
        out_specs=GROUP_SPECS + (full_spec(TURNED), full_spec(NATURAL)),
        scratch_shapes=[
            pltpu.VMEM((NB, ROWS, BLK), f32),
            pltpu.VMEM((NB, rows, 2 * BLK), bf16),
        ],
        compiler_params=params(),
        cost_estimate=pl.CostEstimate(
            flops=5 * KMAX * ROWS * 256 * 256, bytes_accessed=8 << 20, transcendentals=0
        ),
    )(slots, where, tile, omega, before, half, below, centre)


def near_blocks(slots, where, below, centre, above, pieces):
    return pl.pallas_call(
        near_kernel,
        name="near_blocks",
        grid=(1,),
        out_shape=GROUP_OUT,
        in_specs=[SMEM, SMEM]
        + [full_spec(TURNED)] * 3
        + [full_spec(NATURAL)],
        out_specs=GROUP_SPECS,
        compiler_params=params(),
        cost_estimate=pl.CostEstimate(
            flops=3 * KMAX * ROWS * 256 * 256, bytes_accessed=8 << 20, transcendentals=0
        ),
    )(slots, where, below, centre, above, pieces)


def edge_kernel(where_ref, near_ref, other_ref, late_ref, early_ref):
    odd_tile = where_ref[4] == 1
    downward = near_ref[0] + other_ref[0]
    upward = near_ref[2] + other_ref[2]
    late_ref[...] = jnp.where(odd_tile, upward, downward)
    early_ref[...] = jnp.where(odd_tile, downward, upward)


def edge_values(where, near, other):
    block = jax.ShapeDtypeStruct((BLK, BLK), f32)
    return pl.pallas_call(
        edge_kernel,
        name="edge_values",
        grid=(1,),
        out_shape=(block, block),
        in_specs=[SMEM] + [full_spec((3, BLK, BLK))] * 2,
        out_specs=(full_spec((BLK, BLK)),) * 2,
        compiler_params=params(),
        cost_estimate=pl.CostEstimate(
            flops=4 * BLK * BLK, bytes_accessed=6 * 4 * BLK * BLK, transcendentals=0
        ),
    )(where, near, other)


def proximal(where, slots, near, other, late, early, omega):
    block = pl.BlockSpec((BLK, BLK), lambda i, where, slots: (0, 0))
    triple = pl.BlockSpec((3, BLK, BLK), lambda i, where, slots: (0, 0, 0))
    own = pl.BlockSpec((1, 3, 1, BLK, BLK), lambda i, where, slots: (0, 0, where[3], 0, 0))
    return pl.pallas_call(
        proximal_kernel,
        name="proximal",
        grid_spec=pltpu.PrefetchScalarGridSpec(
            num_scalar_prefetch=2,
            grid=(1,),
            in_specs=[triple, triple, block, block, own],
            out_specs=pl.BlockSpec(
                (1, 3, 1, BLK, BLK), lambda i, where, slots: (0, 0, 0, 0, 0)
            ),
        ),
        out_shape=jax.ShapeDtypeStruct((1, 3, 1, BLK, BLK), f32),
        compiler_params=params(),
        cost_estimate=pl.CostEstimate(
            flops=20 * 3 * BLK * BLK, bytes_accessed=1 << 19, transcendentals=0
        ),
    )(where, slots, near, other, late, early, omega)


def shifted(value, axis, steps):
    count = lax.axis_size(axis)
    pairs = [(source, (source + steps) % count) for source in range(count)]
    return lax.ppermute(value, axis, pairs)


def x_exchange(value, step):
    pairs = []
    for x in range(4):
        for core in range(2):
            partner = x ^ 1 if core == step else 3 - x
            pairs.append((2 * x + core, 2 * partner + core))
    return lax.ppermute(value, ("x", "core"), pairs)


def edge_exchange(value, offset):
    count = lax.axis_size("col")
    pairs = []
    for t in range(offset, count + offset, 2):
        pairs += [(t % count, (t + 1) % count), ((t + 1) % count, t % count)]
    return lax.ppermute(value, "col", pairs)


def on_device(observations, omega, block_slots):
    x, y_hi, core = (lax.axis_index(n).astype(jnp.int32) for n in ("x", "y_hi", "core"))
    odd_tile = lax.axis_index("col").astype(jnp.int32) & 1
    where = jnp.stack([x, y_hi, core, 4 * x + 2 * y_hi + core, odd_tile])
    from_below = shifted(observations, "col", 1)
    cut = ROWS // 2
    above_early = shifted(observations[:cut], "col", -1)
    above_late = shifted(observations[cut:], "col", -1)
    residual, centre = partial(1, block_slots, observations, omega)
    residual, below = partial(0, block_slots, from_below, omega, residual)
    residual, half = partial(2, block_slots, above_early, omega, residual)
    far_keep, far_pass, far_send, above, pieces = far_blocks(
        block_slots, where, above_late, omega, residual, half, below, centre
    )
    far_got = shifted(far_send, "core", 1)
    near_keep, near_pass, near_send = near_blocks(
        block_slots, where, below, centre, above, pieces
    )
    near_got = shifted(near_send, "core", 1)
    far_first = x_exchange(far_pass + far_got[2:], 0)
    near_first = x_exchange(near_pass + near_got[2:], 0)
    far_second = x_exchange(far_keep[1] + far_got[1] + far_first[1], 1)
    far_sum = far_keep[0] + far_got[0] + far_first[0] + far_second
    other = shifted(far_sum, "y_hi", 1)
    near_second = x_exchange(near_keep[1] + near_got[1] + near_first[1], 1)
    near_sum = near_keep[0] + near_got[0] + near_first[0] + near_second
    late_out, early_out = edge_values(where, near_sum, other)
    late = edge_exchange(late_out, 1)
    early = edge_exchange(early_out, 0)
    return proximal(where, block_slots, near_sum, other, late, early, omega)


def solution(mesh):
    devices = mesh.devices.reshape(4, 2, 2, 32)
    fine = Mesh(devices, ("x", "y_hi", "core", "col"))
    rows = ("x", "y_hi", "core")
    return jax.shard_map(
        on_device,
        mesh=fine,
        in_specs=(P(rows, "col"), P("col", None, None, None, None), P("col", None, None)),
        out_specs=P("col", None, rows, None, None),
        check_vma=False,
    )
```

```python
import jax
import jax.numpy as jnp
from jax import lax
from jax.experimental import pallas as pl
from jax.experimental.pallas import tpu as pltpu
from jax.sharding import Mesh, PartitionSpec as P

TILE = 1024
BLK = 128
NB = TILE // BLK
KMAX = 16
ROWS = 256
SAMPLES = 4096
step_size = 0.5
penalty = 0.1
f32 = jnp.float32
bf16 = jnp.bfloat16
VMEM_LIMIT = 16 * 1024 * 1024


def split(value):
    high = value.astype(bf16)
    low = (value - high.astype(f32)).astype(bf16)
    return high, low


def split_tile(x_ref, natural_ref, turned_ref, start=0):
    rows = x_ref.shape[0]
    for a in range(NB):
        block = x_ref[:, a * BLK : (a + 1) * BLK]
        high, low = split(block)
        natural_ref[a, :, :BLK] = high
        natural_ref[a, :, BLK:] = low
        high, low = split(block.T)
        turned_ref[a, :BLK, start : start + rows] = high
        turned_ref[a, BLK:, start : start + rows] = low


def add_products(slots_ref, omega_ref, natural_ref, residual_ref, offset, start=0):
    rows = natural_ref.shape[1]

    def body(j, carry):
        slot = slots_ref[0, offset, j]
        active = slot >= 0
        place = jnp.maximum(slot, 0)
        a = place // NB
        b = place % NB
        weight = jnp.where(active, omega_ref[0, 0, j], 0.0)
        high, low = split(weight)
        half = jnp.concatenate([high, low], axis=1)
        weights = jnp.concatenate([half, half], axis=0)
        out = jnp.dot(natural_ref[a], weights, preferred_element_type=f32)
        residual_ref[b, start : start + rows] += out[:, :BLK] + out[:, BLK:]
        return carry

    lax.fori_loop(0, KMAX, body, 0, unroll=4)


def partial_kernel(offset, first, *refs):
    if first:
        slots_ref, x_ref, omega_ref, residual_ref, turned_ref, natural_ref = refs
        residual_ref[...] = jnp.zeros_like(residual_ref)
    else:
        slots_ref, x_ref, omega_ref, before_ref, residual_ref, turned_ref, natural_ref = refs
        residual_ref[...] = before_ref[...]
    split_tile(x_ref, natural_ref, turned_ref)
    add_products(slots_ref, omega_ref, natural_ref, residual_ref, offset)


def quadrant_sum(out):
    out = out[:BLK] + out[BLK:]
    return out[:, :BLK] + out[:, BLK:]


def slot_block(slots_ref, e, j, turned, pieces_ref):
    place = jnp.maximum(slots_ref[0, e, j], 0)
    out = jnp.dot(
        turned[e][place // NB], pieces_ref[place % NB], preferred_element_type=f32
    )
    return quadrant_sum(out)


def group_products(slots_ref, where_ref, turned, pieces_ref, y_hi, keep_ref, pass_ref, send_ref):
    core = where_ref[2]
    for r in range(4):
        i = 2 * ((where_ref[0] + r) & 3) + y_hi
        for e in range(3):
            even = slot_block(slots_ref, e, 2 * i, turned, pieces_ref)
            odd = slot_block(slots_ref, e, 2 * i + 1, turned, pieces_ref)
            if e == 1:
                even_turned, odd_turned = even.T, odd.T
                diagonal = i < NB // 2
                even, odd = (
                    even + jnp.where(diagonal, even_turned, odd_turned),
                    odd + jnp.where(diagonal, odd_turned, even_turned),
                )
            own_ref = pass_ref.at[r - 1] if r else keep_ref
            own_ref[e] = jnp.where(core == 0, even, odd)
            send_ref[r, e] = jnp.where(core == 0, odd, even)


def far_kernel(
    slots_ref, where_ref, x_ref, omega_ref, before_ref, half_ref, below_ref, centre_ref,
    keep_ref, pass_ref, send_ref, above_ref, pieces_ref, residual_ref, natural_ref,
):
    residual_ref[...] = before_ref[...]
    done = half_ref.shape[2]
    above_ref[:, :, :done] = half_ref[...]
    split_tile(x_ref, natural_ref, above_ref, done)
    add_products(slots_ref, omega_ref, natural_ref, residual_ref, 2, done)
    for b in range(NB):
        high, low = split(residual_ref[b])
        pieces_ref[b, :, :BLK] = high
        pieces_ref[b, :, BLK:] = low
    group_products(
        slots_ref, where_ref, (below_ref, centre_ref, above_ref), pieces_ref,
        1 - where_ref[1], keep_ref, pass_ref, send_ref,
    )


def near_kernel(
    slots_ref, where_ref, below_ref, centre_ref, above_ref, pieces_ref,
    keep_ref, pass_ref, send_ref,
):
    group_products(
        slots_ref, where_ref, (below_ref, centre_ref, above_ref), pieces_ref,
        where_ref[1], keep_ref, pass_ref, send_ref,
    )


def proximal_kernel(
    where_ref, slots_ref, total_ref, early_ref, late_ref, omega_ref, out_ref
):
    j = where_ref[3]
    odd_tile = where_ref[4] == 1
    rows = lax.broadcasted_iota(jnp.int32, (BLK, BLK), 0)
    columns = lax.broadcasted_iota(jnp.int32, (BLK, BLK), 1)
    for e in range(3):
        slot = slots_ref[0, e, j]
        total = total_ref[e]
        if e == 0:
            total = total + jnp.where(odd_tile, early_ref[...], late_ref[...]).T
        if e == 2:
            total = total + jnp.where(odd_tile, late_ref[...], early_ref[...]).T
        gradient = total * (0.5 / SAMPLES)
        omega = omega_ref[0, e, 0]
        if e == 1:
            diagonal = (slot >= 0) & (slot // NB == slot % NB)
            on_diagonal = (rows == columns) & diagonal
            inverse = 1.0 / jnp.where(on_diagonal, omega, 1.0)
            gradient = gradient - jnp.where(on_diagonal, inverse, 0.0)
        trial = omega - step_size * gradient
        shrunk = jnp.maximum(jnp.abs(trial) - step_size * penalty, 0.0)
        result = jnp.where(trial < 0.0, -shrunk, shrunk)
        if e == 1:
            result = jnp.where(on_diagonal, trial, result)
        out_ref[0, e, 0] = jnp.where(slot >= 0, result, 0.0)


def params():
    return pltpu.CompilerParams(vmem_limit_bytes=VMEM_LIMIT)


SMEM = pl.BlockSpec(memory_space=pltpu.SMEM)
WHOLE = pl.BlockSpec(memory_space=pltpu.VMEM)
TURNED = (NB, 2 * BLK, ROWS)
NATURAL = (NB, ROWS, 2 * BLK)


def omega_spec(offset):
    return pl.BlockSpec((1, 1, KMAX, BLK, BLK), lambda i: (0, offset, 0, 0, 0))


def full_spec(shape):
    return pl.BlockSpec(shape, lambda i: (0,) * len(shape))


def partial(offset, slots, tile, omega, before=None):
    first = before is None
    rows = tile.shape[0]
    turned = (NB, 2 * BLK, rows)
    in_specs = [SMEM, full_spec((rows, TILE)), omega_spec(offset)]
    inputs = [slots, tile, omega]
    if not first:
        in_specs.append(full_spec((NB, ROWS, BLK)))
        inputs.append(before)
    return pl.pallas_call(
        lambda *refs: partial_kernel(offset, first, *refs),
        name="partial_residual",
        grid=(1,),
        out_shape=(
            jax.ShapeDtypeStruct((NB, ROWS, BLK), f32),
            jax.ShapeDtypeStruct(turned, bf16),
        ),
        in_specs=in_specs,
        out_specs=(full_spec((NB, ROWS, BLK)), full_spec(turned)),
        scratch_shapes=[pltpu.VMEM((NB, rows, 2 * BLK), bf16)],
        compiler_params=params(),
        cost_estimate=pl.CostEstimate(
            flops=2 * KMAX * rows * 256 * 256, bytes_accessed=5 << 20, transcendentals=0
        ),
    )(*inputs)


WAY = (4, 3, BLK, BLK)
OWN = (3, BLK, BLK)
OTHERS = (3, 3, BLK, BLK)


def f32_outs(*shapes):
    return tuple(jax.ShapeDtypeStruct(shape, f32) for shape in shapes)


def full_specs(*shapes):
    return tuple(full_spec(shape) for shape in shapes)


def far_blocks(slots, where, tile, omega, before, half, below, centre):
    rows = tile.shape[0]
    return pl.pallas_call(
        far_kernel,
        name="far_blocks",
        grid=(1,),
        out_shape=f32_outs(OWN, OTHERS, WAY)
        + (jax.ShapeDtypeStruct(TURNED, bf16), jax.ShapeDtypeStruct(NATURAL, bf16)),
        in_specs=[
            SMEM,
            SMEM,
            full_spec((rows, TILE)),
            omega_spec(2),
            full_spec((NB, ROWS, BLK)),
            full_spec((NB, 2 * BLK, ROWS - rows)),
            full_spec(TURNED),
            full_spec(TURNED),
        ],
        out_specs=full_specs(OWN, OTHERS, WAY, TURNED, NATURAL),
        scratch_shapes=[
            pltpu.VMEM((NB, ROWS, BLK), f32),
            pltpu.VMEM((NB, rows, 2 * BLK), bf16),
        ],
        compiler_params=params(),
        cost_estimate=pl.CostEstimate(
            flops=5 * KMAX * ROWS * 256 * 256, bytes_accessed=8 << 20, transcendentals=0
        ),
    )(slots, where, tile, omega, before, half, below, centre)


def near_blocks(slots, where, below, centre, above, pieces):
    return pl.pallas_call(
        near_kernel,
        name="near_blocks",
        grid=(1,),
        out_shape=f32_outs(OWN, OTHERS, WAY),
        in_specs=[SMEM, SMEM]
        + [full_spec(TURNED)] * 3
        + [full_spec(NATURAL)],
        out_specs=full_specs(OWN, OTHERS, WAY),
        compiler_params=params(),
        cost_estimate=pl.CostEstimate(
            flops=3 * KMAX * ROWS * 256 * 256, bytes_accessed=8 << 20, transcendentals=0
        ),
    )(slots, where, below, centre, above, pieces)


def edge_kernel(where_ref, total_ref, late_ref, early_ref):
    odd_tile = where_ref[4] == 1
    downward, upward = total_ref[0], total_ref[2]
    late_ref[...] = jnp.where(odd_tile, upward, downward)
    early_ref[...] = jnp.where(odd_tile, downward, upward)


def edge_values(where, total):
    block = jax.ShapeDtypeStruct((BLK, BLK), f32)
    return pl.pallas_call(
        edge_kernel,
        name="edge_values",
        grid=(1,),
        out_shape=(block, block),
        in_specs=[SMEM] + [full_spec((3, BLK, BLK))],
        out_specs=(full_spec((BLK, BLK)),) * 2,
        compiler_params=params(),
        cost_estimate=pl.CostEstimate(
            flops=4 * BLK * BLK, bytes_accessed=6 * 4 * BLK * BLK, transcendentals=0
        ),
    )(where, total)


def proximal(where, slots, total, early, late, omega):
    block = pl.BlockSpec((BLK, BLK), lambda i, where, slots: (0, 0))
    triple = pl.BlockSpec((3, BLK, BLK), lambda i, where, slots: (0, 0, 0))
    own = pl.BlockSpec((1, 3, 1, BLK, BLK), lambda i, where, slots: (0, 0, where[3], 0, 0))
    return pl.pallas_call(
        proximal_kernel,
        name="proximal",
        grid_spec=pltpu.PrefetchScalarGridSpec(
            num_scalar_prefetch=2,
            grid=(1,),
            in_specs=[triple, block, block, own],
            out_specs=pl.BlockSpec(
                (1, 3, 1, BLK, BLK), lambda i, where, slots: (0, 0, 0, 0, 0)
            ),
        ),
        out_shape=jax.ShapeDtypeStruct((1, 3, 1, BLK, BLK), f32),
        compiler_params=params(),
        cost_estimate=pl.CostEstimate(
            flops=20 * 3 * BLK * BLK, bytes_accessed=1 << 19, transcendentals=0
        ),
    )(where, slots, total, early, late, omega)


def shifted(value, axis, steps):
    count = lax.axis_size(axis)
    pairs = [(source, (source + steps) % count) for source in range(count)]
    return lax.ppermute(value, axis, pairs)


def after(value, earlier):
    return lax.optimization_barrier((value, earlier))[0]


def edge_exchange(value, offset):
    count = lax.axis_size("col")
    pairs = []
    for t in range(offset, count + offset, 2):
        pairs += [(t % count, (t + 1) % count), ((t + 1) % count, t % count)]
    return lax.ppermute(value, "col", pairs)


def on_device(observations, omega, block_slots):
    x, y_hi, core = (lax.axis_index(n).astype(jnp.int32) for n in ("x", "y_hi", "core"))
    odd_tile = lax.axis_index("col").astype(jnp.int32) & 1
    where = jnp.stack([x, y_hi, core, 4 * x + 2 * y_hi + core, odd_tile])
    from_below = shifted(observations, "col", 1)
    cut = ROWS // 2
    above_early = shifted(observations[:cut], "col", -1)
    above_late = shifted(observations[cut:], "col", -1)
    residual, centre = partial(1, block_slots, observations, omega)
    residual, below = partial(0, block_slots, from_below, omega, residual)
    residual, half = partial(2, block_slots, above_early, omega, residual)
    far_keep, far_pass, far_send, above, pieces = far_blocks(
        block_slots, where, above_late, omega, residual, half, below, centre
    )
    far_got = shifted(far_send, "core", 1)
    near_keep, near_pass, near_send = near_blocks(
        block_slots, where, below, centre, above, pieces
    )
    near_got = shifted(near_send, "core", 1)
    far_sum = far_keep + far_got[0]
    for k in (2, 1, 3):
        far_sum = far_sum + shifted(far_pass[k - 1] + far_got[k], "x", k)
    near_got = after(near_got, far_sum)
    near_out = [near_pass[k - 1] + near_got[k] for k in (1, 2, 3)]
    other = shifted(after(far_sum, near_out), "y_hi", 1)
    total = near_keep + near_got[0]
    for k in (1, 3, 2):
        total = total + shifted(near_out[k - 1], "x", k)
    total = total + other
    late_out, early_out = edge_values(where, total)
    late = edge_exchange(late_out, 1)
    early = edge_exchange(early_out, 0)
    return proximal(where, block_slots, total, early, late, omega)


def solution(mesh):
    devices = mesh.devices.reshape(4, 2, 2, 32)
    fine = Mesh(devices, ("x", "y_hi", "core", "col"))
    rows = ("x", "y_hi", "core")
    return jax.shard_map(
        on_device,
        mesh=fine,
        in_specs=(P(rows, "col"), P("col", None, None, None, None), P("col", None, None)),
        out_specs=P("col", None, rows, None, None),
        check_vma=False,
    )
```

```python
import jax
import jax.numpy as jnp
from jax import lax
from jax.experimental import pallas as pl
from jax.experimental.pallas import tpu as pltpu
from jax.sharding import Mesh, PartitionSpec as P

TILE = 1024
BLK = 128
NB = TILE // BLK
KMAX = 16
ROWS = 256
SAMPLES = 4096
step_size = 0.5
penalty = 0.1
f32 = jnp.float32
bf16 = jnp.bfloat16
VMEM_LIMIT = 16 * 1024 * 1024


def split(value):
    high = value.astype(bf16)
    low = (value - high.astype(f32)).astype(bf16)
    return high, low


def split_tile(x_ref, natural_ref, turned_ref, start=0):
    rows = x_ref.shape[0]
    for a in range(NB):
        block = x_ref[:, a * BLK : (a + 1) * BLK]
        high, low = split(block)
        natural_ref[a, :, :BLK] = high
        natural_ref[a, :, BLK:] = low
        high, low = split(block.T)
        turned_ref[a, :BLK, start : start + rows] = high
        turned_ref[a, BLK:, start : start + rows] = low


def add_products(slots_ref, omega_ref, natural_ref, residual_ref, offset, start=0):
    rows = natural_ref.shape[1]

    def body(j, carry):
        slot = slots_ref[0, offset, j]
        active = slot >= 0
        place = jnp.maximum(slot, 0)
        a = place // NB
        b = place % NB
        weight = jnp.where(active, omega_ref[0, 0, j], 0.0)
        high, low = split(weight)
        half = jnp.concatenate([high, low], axis=1)
        weights = jnp.concatenate([half, half], axis=0)
        out = jnp.dot(natural_ref[a], weights, preferred_element_type=f32)
        residual_ref[b, start : start + rows] += out[:, :BLK] + out[:, BLK:]
        return carry

    lax.fori_loop(0, KMAX, body, 0, unroll=4)


def partial_kernel(offset, first, *refs):
    if first:
        slots_ref, x_ref, omega_ref, residual_ref, turned_ref, natural_ref = refs
        residual_ref[...] = jnp.zeros_like(residual_ref)
    else:
        slots_ref, x_ref, omega_ref, before_ref, residual_ref, turned_ref, natural_ref = refs
        residual_ref[...] = before_ref[...]
    split_tile(x_ref, natural_ref, turned_ref)
    add_products(slots_ref, omega_ref, natural_ref, residual_ref, offset)


def quadrant_sum(out):
    out = out[:BLK] + out[BLK:]
    return out[:, :BLK] + out[:, BLK:]


def slot_block(slots_ref, e, j, turned, pieces_ref):
    place = jnp.maximum(slots_ref[0, e, j], 0)
    out = jnp.dot(
        turned[e][place // NB], pieces_ref[place % NB], preferred_element_type=f32
    )
    return quadrant_sum(out)


def group_products(slots_ref, where_ref, turned, pieces_ref, y_hi, keep_ref, pass_ref, send_ref):
    x, core = where_ref[0], where_ref[2]
    even_pair, odd_pair = x ^ 1, 3 - x
    first = jnp.where(core == 0, even_pair, odd_pair)
    second = jnp.where(core == 0, odd_pair, even_pair)
    for r, x_of in enumerate((x, second, first, x ^ 2)):
        i = 2 * x_of + y_hi
        for e in range(3):
            even = slot_block(slots_ref, e, 2 * i, turned, pieces_ref)
            odd = slot_block(slots_ref, e, 2 * i + 1, turned, pieces_ref)
            if e == 1:
                even_turned, odd_turned = even.T, odd.T
                diagonal = i < NB // 2
                even, odd = (
                    even + jnp.where(diagonal, even_turned, odd_turned),
                    odd + jnp.where(diagonal, odd_turned, even_turned),
                )
            own_ref = keep_ref if r < 2 else pass_ref
            own_ref[r % 2, e] = jnp.where(core == 0, even, odd)
            send_ref[(0, 2, 1, 3)[r], e] = jnp.where(core == 0, odd, even)


def far_kernel(
    slots_ref, where_ref, x_ref, omega_ref, before_ref, half_ref, below_ref, centre_ref,
    keep_ref, pass_ref, send_ref, above_ref, pieces_ref, residual_ref, natural_ref,
):
    residual_ref[...] = before_ref[...]
    done = half_ref.shape[2]
    above_ref[:, :, :done] = half_ref[...]
    split_tile(x_ref, natural_ref, above_ref, done)
    add_products(slots_ref, omega_ref, natural_ref, residual_ref, 2, done)
    for b in range(NB):
        high, low = split(residual_ref[b])
        pieces_ref[b, :, :BLK] = high
        pieces_ref[b, :, BLK:] = low
    group_products(
        slots_ref, where_ref, (below_ref, centre_ref, above_ref), pieces_ref,
        1 - where_ref[1], keep_ref, pass_ref, send_ref,
    )


def near_kernel(
    slots_ref, where_ref, below_ref, centre_ref, above_ref, pieces_ref,
    keep_ref, pass_ref, send_ref,
):
    group_products(
        slots_ref, where_ref, (below_ref, centre_ref, above_ref), pieces_ref,
        where_ref[1], keep_ref, pass_ref, send_ref,
    )


def proximal_kernel(
    where_ref, slots_ref, near_ref, early_ref, far_early_ref, late_ref, far_late_ref,
    other_ref, omega_ref, out_ref,
):
    j = where_ref[3]
    odd_tile = where_ref[4] == 1
    rows = lax.broadcasted_iota(jnp.int32, (BLK, BLK), 0)
    columns = lax.broadcasted_iota(jnp.int32, (BLK, BLK), 1)
    early = early_ref[...] + far_early_ref[...]
    late = late_ref[...] + far_late_ref[...]
    for e in range(3):
        slot = slots_ref[0, e, j]
        total = near_ref[e] + other_ref[e]
        if e == 0:
            total = total + jnp.where(odd_tile, early, late).T
        if e == 2:
            total = total + jnp.where(odd_tile, late, early).T
        gradient = total * (0.5 / SAMPLES)
        omega = omega_ref[0, e, 0]
        if e == 1:
            diagonal = (slot >= 0) & (slot // NB == slot % NB)
            on_diagonal = (rows == columns) & diagonal
            inverse = 1.0 / jnp.where(on_diagonal, omega, 1.0)
            gradient = gradient - jnp.where(on_diagonal, inverse, 0.0)
        trial = omega - step_size * gradient
        shrunk = jnp.maximum(jnp.abs(trial) - step_size * penalty, 0.0)
        result = jnp.where(trial < 0.0, -shrunk, shrunk)
        if e == 1:
            result = jnp.where(on_diagonal, trial, result)
        out_ref[0, e, 0] = jnp.where(slot >= 0, result, 0.0)


def params():
    return pltpu.CompilerParams(vmem_limit_bytes=VMEM_LIMIT)


SMEM = pl.BlockSpec(memory_space=pltpu.SMEM)
WHOLE = pl.BlockSpec(memory_space=pltpu.VMEM)
TURNED = (NB, 2 * BLK, ROWS)
NATURAL = (NB, ROWS, 2 * BLK)


def omega_spec(offset):
    return pl.BlockSpec((1, 1, KMAX, BLK, BLK), lambda i: (0, offset, 0, 0, 0))


def full_spec(shape):
    return pl.BlockSpec(shape, lambda i: (0,) * len(shape))


def partial(offset, slots, tile, omega, before=None):
    first = before is None
    rows = tile.shape[0]
    turned = (NB, 2 * BLK, rows)
    in_specs = [SMEM, full_spec((rows, TILE)), omega_spec(offset)]
    inputs = [slots, tile, omega]
    if not first:
        in_specs.append(full_spec((NB, ROWS, BLK)))
        inputs.append(before)
    return pl.pallas_call(
        lambda *refs: partial_kernel(offset, first, *refs),
        name="partial_residual",
        grid=(1,),
        out_shape=(
            jax.ShapeDtypeStruct((NB, ROWS, BLK), f32),
            jax.ShapeDtypeStruct(turned, bf16),
        ),
        in_specs=in_specs,
        out_specs=(full_spec((NB, ROWS, BLK)), full_spec(turned)),
        scratch_shapes=[pltpu.VMEM((NB, rows, 2 * BLK), bf16)],
        compiler_params=params(),
        cost_estimate=pl.CostEstimate(
            flops=2 * KMAX * rows * 256 * 256, bytes_accessed=5 << 20, transcendentals=0
        ),
    )(*inputs)


HALF = (2, 3, BLK, BLK)
WAY = (4, 3, BLK, BLK)
GROUP_OUT = tuple(jax.ShapeDtypeStruct(shape, f32) for shape in (HALF, HALF, WAY))
GROUP_SPECS = tuple(full_spec(shape) for shape in (HALF, HALF, WAY))


def far_blocks(slots, where, tile, omega, before, half, below, centre):
    rows = tile.shape[0]
    return pl.pallas_call(
        far_kernel,
        name="far_blocks",
        grid=(1,),
        out_shape=GROUP_OUT
        + (jax.ShapeDtypeStruct(TURNED, bf16), jax.ShapeDtypeStruct(NATURAL, bf16)),
        in_specs=[
            SMEM,
            SMEM,
            full_spec((rows, TILE)),
            omega_spec(2),
            full_spec((NB, ROWS, BLK)),
            full_spec((NB, 2 * BLK, ROWS - rows)),
            full_spec(TURNED),
            full_spec(TURNED),
        ],
        out_specs=GROUP_SPECS + (full_spec(TURNED), full_spec(NATURAL)),
        scratch_shapes=[
            pltpu.VMEM((NB, ROWS, BLK), f32),
            pltpu.VMEM((NB, rows, 2 * BLK), bf16),
        ],
        compiler_params=params(),
        cost_estimate=pl.CostEstimate(
            flops=5 * KMAX * ROWS * 256 * 256, bytes_accessed=8 << 20, transcendentals=0
        ),
    )(slots, where, tile, omega, before, half, below, centre)


def near_blocks(slots, where, below, centre, above, pieces):
    return pl.pallas_call(
        near_kernel,
        name="near_blocks",
        grid=(1,),
        out_shape=GROUP_OUT,
        in_specs=[SMEM, SMEM]
        + [full_spec(TURNED)] * 3
        + [full_spec(NATURAL)],
        out_specs=GROUP_SPECS,
        compiler_params=params(),
        cost_estimate=pl.CostEstimate(
            flops=3 * KMAX * ROWS * 256 * 256, bytes_accessed=8 << 20, transcendentals=0
        ),
    )(slots, where, below, centre, above, pieces)


def sum_kernel(where_ref, keep_ref, got_ref, first_ref, second_ref, sum_ref, early_ref, late_ref):
    odd_tile = where_ref[4] == 1
    for e in range(3):
        sum_ref[e] = keep_ref[0, e] + got_ref[0, e] + first_ref[0, e] + second_ref[e]
    early_ref[...] = jnp.where(odd_tile, sum_ref[0], sum_ref[2])
    late_ref[...] = jnp.where(odd_tile, sum_ref[2], sum_ref[0])


def group_sum(where, keep, got, first, second):
    return pl.pallas_call(
        sum_kernel,
        name="group_sum",
        grid=(1,),
        out_shape=tuple(
            jax.ShapeDtypeStruct(shape, f32)
            for shape in ((3, BLK, BLK), (BLK, BLK), (BLK, BLK))
        ),
        in_specs=[SMEM] + [full_spec(x.shape) for x in (keep, got, first, second)],
        out_specs=tuple(
            full_spec(shape) for shape in ((3, BLK, BLK), (BLK, BLK), (BLK, BLK))
        ),
        compiler_params=params(),
        cost_estimate=pl.CostEstimate(
            flops=9 * BLK * BLK, bytes_accessed=17 * 4 * BLK * BLK, transcendentals=0
        ),
    )(where, keep, got, first, second)


def proximal(where, slots, sums, omega):
    block = pl.BlockSpec((BLK, BLK), lambda i, where, slots: (0, 0))
    triple = pl.BlockSpec((3, BLK, BLK), lambda i, where, slots: (0, 0, 0))
    own = pl.BlockSpec((1, 3, 1, BLK, BLK), lambda i, where, slots: (0, 0, where[3], 0, 0))
    return pl.pallas_call(
        proximal_kernel,
        name="proximal",
        grid_spec=pltpu.PrefetchScalarGridSpec(
            num_scalar_prefetch=2,
            grid=(1,),
            in_specs=[triple] + [block] * 4 + [triple, own],
            out_specs=pl.BlockSpec(
                (1, 3, 1, BLK, BLK), lambda i, where, slots: (0, 0, 0, 0, 0)
            ),
        ),
        out_shape=jax.ShapeDtypeStruct((1, 3, 1, BLK, BLK), f32),
        compiler_params=params(),
        cost_estimate=pl.CostEstimate(
            flops=20 * 3 * BLK * BLK, bytes_accessed=1 << 19, transcendentals=0
        ),
    )(where, slots, *sums, omega)


def shifted(value, axis, steps):
    count = lax.axis_size(axis)
    pairs = [(source, (source + steps) % count) for source in range(count)]
    return lax.ppermute(value, axis, pairs)


def x_exchange(value, step):
    pairs = []
    for x in range(4):
        for core in range(2):
            partner = x ^ 1 if core == step else 3 - x
            pairs.append((2 * x + core, 2 * partner + core))
    return lax.ppermute(value, ("x", "core"), pairs)


def after(value, earlier):
    return lax.optimization_barrier((value, earlier))[0]


def edge_exchange(value, offset, flip=0):
    count = lax.axis_size("col")
    pairs = []
    for y in range(2):
        for t in range(offset, count + offset, 2):
            low, high = t % count, (t + 1) % count
            pairs.append((y * count + low, (y ^ flip) * count + high))
            pairs.append((y * count + high, (y ^ flip) * count + low))
    return lax.ppermute(value, ("y_hi", "col"), pairs)


def on_device(observations, omega, block_slots):
    x, y_hi, core = (lax.axis_index(n).astype(jnp.int32) for n in ("x", "y_hi", "core"))
    odd_tile = lax.axis_index("col").astype(jnp.int32) & 1
    where = jnp.stack([x, y_hi, core, 4 * x + 2 * y_hi + core, odd_tile])
    from_below = shifted(observations, "col", 1)
    cut = ROWS // 2
    above_early = shifted(observations[:cut], "col", -1)
    above_late = shifted(observations[cut:], "col", -1)
    residual, centre = partial(1, block_slots, observations, omega)
    residual, below = partial(0, block_slots, from_below, omega, residual)
    residual, half = partial(2, block_slots, above_early, omega, residual)
    far_keep, far_pass, far_send, above, pieces = far_blocks(
        block_slots, where, above_late, omega, residual, half, below, centre
    )
    far_got = shifted(far_send, "core", 1)
    near_keep, near_pass, near_send = near_blocks(
        block_slots, where, below, centre, above, pieces
    )
    near_got = shifted(near_send, "core", 1)
    far_first = x_exchange(far_pass + far_got[2:], 0)
    near_first = x_exchange(near_pass + near_got[2:], 0)
    far_second = x_exchange(far_keep[1] + far_got[1] + far_first[1], 1)
    near_second = x_exchange(near_keep[1] + near_got[1] + near_first[1], 1)
    far_sum, far_early, far_late = group_sum(
        where, far_keep, far_got, far_first, far_second
    )
    near_sum, near_early, near_late = group_sum(
        where, near_keep, near_got, near_first, near_second
    )
    sums = (
        near_sum,
        edge_exchange(near_early, 0),
        edge_exchange(far_early, 0, 1),
        edge_exchange(near_late, 1),
        edge_exchange(far_late, 1, 1),
        shifted(far_sum, "y_hi", 1),
    )
    return proximal(where, block_slots, sums, omega)


def solution(mesh):
    devices = mesh.devices.reshape(4, 2, 2, 32)
    fine = Mesh(devices, ("x", "y_hi", "core", "col"))
    rows = ("x", "y_hi", "core")
    return jax.shard_map(
        on_device,
        mesh=fine,
        in_specs=(P(rows, "col"), P("col", None, None, None, None), P("col", None, None)),
        out_specs=P("col", None, rows, None, None),
        check_vma=False,
    )
```

```python
import jax
import jax.numpy as jnp
from jax import lax
from jax.experimental import pallas as pl
from jax.experimental.pallas import tpu as pltpu
from jax.sharding import Mesh, PartitionSpec as P

TILE = 1024
BLK = 128
NB = TILE // BLK
KMAX = 16
ROWS = 256
SAMPLES = 4096
step_size = 0.5
penalty = 0.1
f32 = jnp.float32
bf16 = jnp.bfloat16
VMEM_LIMIT = 16 * 1024 * 1024


def split(value):
    high = value.astype(bf16)
    low = (value - high.astype(f32)).astype(bf16)
    return high, low


def split_tile(x_ref, natural_ref, turned_ref, start=0):
    rows = x_ref.shape[0]
    for a in range(NB):
        block = x_ref[:, a * BLK : (a + 1) * BLK]
        high, low = split(block)
        natural_ref[a, :, :BLK] = high
        natural_ref[a, :, BLK:] = low
        high, low = split(block.T)
        turned_ref[a, :BLK, start : start + rows] = high
        turned_ref[a, BLK:, start : start + rows] = low


def add_products(slots_ref, omega_ref, natural_ref, residual_ref, offset, start=0):
    rows = natural_ref.shape[1]

    def body(j, carry):
        slot = slots_ref[0, offset, j]
        active = slot >= 0
        place = jnp.maximum(slot, 0)
        a = place // NB
        b = place % NB
        weight = jnp.where(active, omega_ref[0, 0, j], 0.0)
        high, low = split(weight)
        half = jnp.concatenate([high, low], axis=1)
        weights = jnp.concatenate([half, half], axis=0)
        out = jnp.dot(natural_ref[a], weights, preferred_element_type=f32)
        residual_ref[b, start : start + rows] += out[:, :BLK] + out[:, BLK:]
        return carry

    lax.fori_loop(0, KMAX, body, 0, unroll=4)


def partial_kernel(offset, first, *refs):
    if first:
        slots_ref, x_ref, omega_ref, residual_ref, turned_ref, natural_ref = refs
        residual_ref[...] = jnp.zeros_like(residual_ref)
    else:
        slots_ref, x_ref, omega_ref, before_ref, residual_ref, turned_ref, natural_ref = refs
        residual_ref[...] = before_ref[...]
    split_tile(x_ref, natural_ref, turned_ref)
    add_products(slots_ref, omega_ref, natural_ref, residual_ref, offset)


def quadrant_sum(out):
    out = out[:BLK] + out[BLK:]
    return out[:, :BLK] + out[:, BLK:]


def slot_block(slots_ref, e, j, turned, pieces_ref):
    place = jnp.maximum(slots_ref[0, e, j], 0)
    out = jnp.dot(
        turned[e][place // NB], pieces_ref[place % NB], preferred_element_type=f32
    )
    return quadrant_sum(out)


def group_products(slots_ref, where_ref, turned, pieces_ref, y_hi, keep_ref, pass_ref, send_ref):
    x, core = where_ref[0], where_ref[2]
    even_pair, odd_pair = x ^ 1, 3 - x
    first = jnp.where(core == 0, even_pair, odd_pair)
    second = jnp.where(core == 0, odd_pair, even_pair)
    for r, x_of in enumerate((x, second, first, x ^ 2)):
        i = 2 * x_of + y_hi
        for e in range(3):
            even = slot_block(slots_ref, e, 2 * i, turned, pieces_ref)
            odd = slot_block(slots_ref, e, 2 * i + 1, turned, pieces_ref)
            if e == 1:
                even_turned, odd_turned = even.T, odd.T
                diagonal = i < NB // 2
                even, odd = (
                    even + jnp.where(diagonal, even_turned, odd_turned),
                    odd + jnp.where(diagonal, odd_turned, even_turned),
                )
            own_ref = keep_ref if r < 2 else pass_ref
            own_ref[r % 2, e] = jnp.where(core == 0, even, odd)
            send_ref[(0, 2, 1, 3)[r], e] = jnp.where(core == 0, odd, even)


def far_kernel(
    slots_ref, where_ref, x_ref, omega_ref, before_ref, half_ref, below_ref, centre_ref,
    keep_ref, pass_ref, send_ref, above_ref, pieces_ref, residual_ref, natural_ref,
):
    residual_ref[...] = before_ref[...]
    done = half_ref.shape[2]
    above_ref[:, :, :done] = half_ref[...]
    split_tile(x_ref, natural_ref, above_ref, done)
    add_products(slots_ref, omega_ref, natural_ref, residual_ref, 2, done)
    for b in range(NB):
        high, low = split(residual_ref[b])
        pieces_ref[b, :, :BLK] = high
        pieces_ref[b, :, BLK:] = low
    group_products(
        slots_ref, where_ref, (below_ref, centre_ref, above_ref), pieces_ref,
        1 - where_ref[1], keep_ref, pass_ref, send_ref,
    )


def near_kernel(
    slots_ref, where_ref, below_ref, centre_ref, above_ref, pieces_ref,
    keep_ref, pass_ref, send_ref,
):
    group_products(
        slots_ref, where_ref, (below_ref, centre_ref, above_ref), pieces_ref,
        where_ref[1], keep_ref, pass_ref, send_ref,
    )


def proximal_kernel(
    where_ref, slots_ref, near_ref, other_ref, early_ref, late_ref, omega_ref, out_ref
):
    j = where_ref[3]
    odd_tile = where_ref[4] == 1
    rows = lax.broadcasted_iota(jnp.int32, (BLK, BLK), 0)
    columns = lax.broadcasted_iota(jnp.int32, (BLK, BLK), 1)
    for e in range(3):
        slot = slots_ref[0, e, j]
        total = near_ref[e] + other_ref[e]
        if e == 0:
            total = total + jnp.where(odd_tile, early_ref[...], late_ref[...]).T
        if e == 2:
            total = total + jnp.where(odd_tile, late_ref[...], early_ref[...]).T
        gradient = total * (0.5 / SAMPLES)
        omega = omega_ref[0, e, 0]
        if e == 1:
            diagonal = (slot >= 0) & (slot // NB == slot % NB)
            on_diagonal = (rows == columns) & diagonal
            inverse = 1.0 / jnp.where(on_diagonal, omega, 1.0)
            gradient = gradient - jnp.where(on_diagonal, inverse, 0.0)
        trial = omega - step_size * gradient
        shrunk = jnp.maximum(jnp.abs(trial) - step_size * penalty, 0.0)
        result = jnp.where(trial < 0.0, -shrunk, shrunk)
        if e == 1:
            result = jnp.where(on_diagonal, trial, result)
        out_ref[0, e, 0] = jnp.where(slot >= 0, result, 0.0)


def params():
    return pltpu.CompilerParams(vmem_limit_bytes=VMEM_LIMIT)


SMEM = pl.BlockSpec(memory_space=pltpu.SMEM)
WHOLE = pl.BlockSpec(memory_space=pltpu.VMEM)
TURNED = (NB, 2 * BLK, ROWS)
NATURAL = (NB, ROWS, 2 * BLK)


def omega_spec(offset):
    return pl.BlockSpec((1, 1, KMAX, BLK, BLK), lambda i: (0, offset, 0, 0, 0))


def full_spec(shape):
    return pl.BlockSpec(shape, lambda i: (0,) * len(shape))


def partial(offset, slots, tile, omega, before=None):
    first = before is None
    rows = tile.shape[0]
    turned = (NB, 2 * BLK, rows)
    in_specs = [SMEM, full_spec((rows, TILE)), omega_spec(offset)]
    inputs = [slots, tile, omega]
    if not first:
        in_specs.append(full_spec((NB, ROWS, BLK)))
        inputs.append(before)
    return pl.pallas_call(
        lambda *refs: partial_kernel(offset, first, *refs),
        name="partial_residual",
        grid=(1,),
        out_shape=(
            jax.ShapeDtypeStruct((NB, ROWS, BLK), f32),
            jax.ShapeDtypeStruct(turned, bf16),
        ),
        in_specs=in_specs,
        out_specs=(full_spec((NB, ROWS, BLK)), full_spec(turned)),
        scratch_shapes=[pltpu.VMEM((NB, rows, 2 * BLK), bf16)],
        compiler_params=params(),
        cost_estimate=pl.CostEstimate(
            flops=2 * KMAX * rows * 256 * 256, bytes_accessed=5 << 20, transcendentals=0
        ),
    )(*inputs)


HALF = (2, 3, BLK, BLK)
WAY = (4, 3, BLK, BLK)
GROUP_OUT = tuple(jax.ShapeDtypeStruct(shape, f32) for shape in (HALF, HALF, WAY))
GROUP_SPECS = tuple(full_spec(shape) for shape in (HALF, HALF, WAY))


def far_blocks(slots, where, tile, omega, before, half, below, centre):
    rows = tile.shape[0]
    return pl.pallas_call(
        far_kernel,
        name="far_blocks",
        grid=(1,),
        out_shape=GROUP_OUT
        + (jax.ShapeDtypeStruct(TURNED, bf16), jax.ShapeDtypeStruct(NATURAL, bf16)),
        in_specs=[
            SMEM,
            SMEM,
            full_spec((rows, TILE)),
            omega_spec(2),
            full_spec((NB, ROWS, BLK)),
            full_spec((NB, 2 * BLK, ROWS - rows)),
            full_spec(TURNED),
            full_spec(TURNED),
        ],
        out_specs=GROUP_SPECS + (full_spec(TURNED), full_spec(NATURAL)),
        scratch_shapes=[
            pltpu.VMEM((NB, ROWS, BLK), f32),
            pltpu.VMEM((NB, rows, 2 * BLK), bf16),
        ],
        compiler_params=params(),
        cost_estimate=pl.CostEstimate(
            flops=5 * KMAX * ROWS * 256 * 256, bytes_accessed=8 << 20, transcendentals=0
        ),
    )(slots, where, tile, omega, before, half, below, centre)


def near_blocks(slots, where, below, centre, above, pieces):
    return pl.pallas_call(
        near_kernel,
        name="near_blocks",
        grid=(1,),
        out_shape=GROUP_OUT,
        in_specs=[SMEM, SMEM]
        + [full_spec(TURNED)] * 3
        + [full_spec(NATURAL)],
        out_specs=GROUP_SPECS,
        compiler_params=params(),
        cost_estimate=pl.CostEstimate(
            flops=3 * KMAX * ROWS * 256 * 256, bytes_accessed=8 << 20, transcendentals=0
        ),
    )(slots, where, below, centre, above, pieces)


def edge_kernel(where_ref, near_ref, other_ref, late_ref, early_ref):
    odd_tile = where_ref[4] == 1
    downward = near_ref[0] + other_ref[0]
    upward = near_ref[2] + other_ref[2]
    late_ref[...] = jnp.where(odd_tile, upward, downward)
    early_ref[...] = jnp.where(odd_tile, downward, upward)


def edge_values(where, near, other):
    block = jax.ShapeDtypeStruct((BLK, BLK), f32)
    return pl.pallas_call(
        edge_kernel,
        name="edge_values",
        grid=(1,),
        out_shape=(block, block),
        in_specs=[SMEM] + [full_spec((3, BLK, BLK))] * 2,
        out_specs=(full_spec((BLK, BLK)),) * 2,
        compiler_params=params(),
        cost_estimate=pl.CostEstimate(
            flops=4 * BLK * BLK, bytes_accessed=6 * 4 * BLK * BLK, transcendentals=0
        ),
    )(where, near, other)


def proximal(where, slots, near, other, early, late, omega):
    block = pl.BlockSpec((BLK, BLK), lambda i, where, slots: (0, 0))
    triple = pl.BlockSpec((3, BLK, BLK), lambda i, where, slots: (0, 0, 0))
    own = pl.BlockSpec((1, 3, 1, BLK, BLK), lambda i, where, slots: (0, 0, where[3], 0, 0))
    return pl.pallas_call(
        proximal_kernel,
        name="proximal",
        grid_spec=pltpu.PrefetchScalarGridSpec(
            num_scalar_prefetch=2,
            grid=(1,),
            in_specs=[triple, triple, block, block, own],
            out_specs=pl.BlockSpec(
                (1, 3, 1, BLK, BLK), lambda i, where, slots: (0, 0, 0, 0, 0)
            ),
        ),
        out_shape=jax.ShapeDtypeStruct((1, 3, 1, BLK, BLK), f32),
        compiler_params=params(),
        cost_estimate=pl.CostEstimate(
            flops=20 * 3 * BLK * BLK, bytes_accessed=1 << 19, transcendentals=0
        ),
    )(where, slots, near, other, early, late, omega)


def shifted(value, axis, steps):
    count = lax.axis_size(axis)
    pairs = [(source, (source + steps) % count) for source in range(count)]
    return lax.ppermute(value, axis, pairs)


def x_exchange(value, step):
    pairs = []
    for x in range(4):
        for core in range(2):
            partner = x ^ 1 if core == step else 3 - x
            pairs.append((2 * x + core, 2 * partner + core))
    return lax.ppermute(value, ("x", "core"), pairs)


def edge_exchange(value, offset):
    count = lax.axis_size("col")
    pairs = []
    for t in range(offset, count + offset, 2):
        pairs += [(t % count, (t + 1) % count), ((t + 1) % count, t % count)]
    return lax.ppermute(value, "col", pairs)


def on_device(observations, omega, block_slots):
    x, y_hi, core = (lax.axis_index(n).astype(jnp.int32) for n in ("x", "y_hi", "core"))
    odd_tile = lax.axis_index("col").astype(jnp.int32) & 1
    where = jnp.stack([x, y_hi, core, 4 * x + 2 * y_hi + core, odd_tile])
    from_below = shifted(observations, "col", 1)
    cut = ROWS // 2
    above_early = shifted(observations[:cut], "col", -1)
    above_late = shifted(observations[cut:], "col", -1)
    residual, centre = partial(1, block_slots, observations, omega)
    residual, below = partial(0, block_slots, from_below, omega, residual)
    residual, half = partial(2, block_slots, above_early, omega, residual)
    far_keep, far_pass, far_send, above, pieces = far_blocks(
        block_slots, where, above_late, omega, residual, half, below, centre
    )
    far_got = shifted(far_send, "core", 1)
    near_keep, near_pass, near_send = near_blocks(
        block_slots, where, below, centre, above, pieces
    )
    near_got = shifted(near_send, "core", 1)
    far_first = x_exchange(far_pass + far_got[2:], 0)
    near_first = x_exchange(near_pass + near_got[2:], 0)
    far_second = x_exchange(far_keep[1] + far_got[1] + far_first[1], 1)
    far_sum = far_keep[0] + far_got[0] + far_first[0] + far_second
    other = shifted(far_sum, "y_hi", 1)
    near_second = x_exchange(near_keep[1] + near_got[1] + near_first[1], 1)
    near_sum = near_keep[0] + near_got[0] + near_first[0] + near_second
    late_out, early_out = edge_values(where, near_sum, other)
    late = edge_exchange(late_out, 1)
    early = edge_exchange(early_out, 0)
    return proximal(where, block_slots, near_sum, other, early, late, omega)


def solution(mesh):
    devices = mesh.devices.reshape(4, 2, 2, 32)
    fine = Mesh(devices, ("x", "y_hi", "core", "col"))
    rows = ("x", "y_hi", "core")
    return jax.shard_map(
        on_device,
        mesh=fine,
        in_specs=(P(rows, "col"), P("col", None, None, None, None), P("col", None, None)),
        out_specs=P("col", None, rows, None, None),
        check_vma=False,
    )
```

```python
import jax
import jax.numpy as jnp
from jax import lax
from jax.experimental import pallas as pl
from jax.experimental.pallas import tpu as pltpu
from jax.sharding import Mesh, PartitionSpec as P

TILE = 1024
BLK = 128
NB = TILE // BLK
KMAX = 16
ROWS = 256
SAMPLES = 4096
step_size = 0.5
penalty = 0.1
f32 = jnp.float32
bf16 = jnp.bfloat16
VMEM_LIMIT = 16 * 1024 * 1024


def split(value):
    high = value.astype(bf16)
    low = (value - high.astype(f32)).astype(bf16)
    return high, low


def split_tile(x_ref, natural_ref, turned_ref, start=0):
    rows = x_ref.shape[0]
    for a in range(NB):
        block = x_ref[:, a * BLK : (a + 1) * BLK]
        high, low = split(block)
        natural_ref[a, :, :BLK] = high
        natural_ref[a, :, BLK:] = low
        high, low = split(block.T)
        turned_ref[a, :BLK, start : start + rows] = high
        turned_ref[a, BLK:, start : start + rows] = low


def add_products(slots_ref, omega_ref, natural_ref, residual_ref, offset, start=0):
    rows = natural_ref.shape[1]

    def body(j, carry):
        slot = slots_ref[0, offset, j]
        active = slot >= 0
        place = jnp.maximum(slot, 0)
        a = place // NB
        b = place % NB
        weight = jnp.where(active, omega_ref[0, 0, j], 0.0)
        high, low = split(weight)
        half = jnp.concatenate([high, low], axis=1)
        weights = jnp.concatenate([half, half], axis=0)
        out = jnp.dot(natural_ref[a], weights, preferred_element_type=f32)
        residual_ref[b, start : start + rows] += out[:, :BLK] + out[:, BLK:]
        return carry

    lax.fori_loop(0, KMAX, body, 0, unroll=4)


def partial_kernel(offset, first, *refs):
    if first:
        slots_ref, x_ref, omega_ref, residual_ref, turned_ref, natural_ref = refs
        residual_ref[...] = jnp.zeros_like(residual_ref)
    else:
        slots_ref, x_ref, omega_ref, before_ref, residual_ref, turned_ref, natural_ref = refs
        residual_ref[...] = before_ref[...]
    split_tile(x_ref, natural_ref, turned_ref)
    add_products(slots_ref, omega_ref, natural_ref, residual_ref, offset)


def quadrant_sum(out):
    out = out[:BLK] + out[BLK:]
    return out[:, :BLK] + out[:, BLK:]


def slot_block(slots_ref, e, j, turned, pieces_ref):
    place = jnp.maximum(slots_ref[0, e, j], 0)
    out = jnp.dot(
        turned[e][place // NB], pieces_ref[place % NB], preferred_element_type=f32
    )
    return quadrant_sum(out)


def group_products(slots_ref, where_ref, turned, pieces_ref, y_hi, keep_ref, pass_ref, send_ref):
    x, core = where_ref[0], where_ref[2]
    even_pair, odd_pair = x ^ 1, 3 - x
    first = jnp.where(core == 0, even_pair, odd_pair)
    second = jnp.where(core == 0, odd_pair, even_pair)
    for r, x_of in enumerate((x, second, first, x ^ 2)):
        i = 2 * x_of + y_hi
        for e in range(3):
            even = slot_block(slots_ref, e, 2 * i, turned, pieces_ref)
            odd = slot_block(slots_ref, e, 2 * i + 1, turned, pieces_ref)
            if e == 1:
                even_turned, odd_turned = even.T, odd.T
                diagonal = i < NB // 2
                even, odd = (
                    even + jnp.where(diagonal, even_turned, odd_turned),
                    odd + jnp.where(diagonal, odd_turned, even_turned),
                )
            own_ref = keep_ref if r < 2 else pass_ref
            own_ref[r % 2, e] = jnp.where(core == 0, even, odd)
            send_ref[(0, 2, 1, 3)[r], e] = jnp.where(core == 0, odd, even)


def far_kernel(
    slots_ref, where_ref, x_ref, omega_ref, before_ref, half_ref, below_ref, centre_ref,
    keep_ref, pass_ref, send_ref, above_ref, pieces_ref, residual_ref, natural_ref,
):
    residual_ref[...] = before_ref[...]
    done = half_ref.shape[2]
    above_ref[:, :, :done] = half_ref[...]
    split_tile(x_ref, natural_ref, above_ref, done)
    add_products(slots_ref, omega_ref, natural_ref, residual_ref, 2, done)
    for b in range(NB):
        high, low = split(residual_ref[b])
        pieces_ref[b, :, :BLK] = high
        pieces_ref[b, :, BLK:] = low
    group_products(
        slots_ref, where_ref, (below_ref, centre_ref, above_ref), pieces_ref,
        1 - where_ref[1], keep_ref, pass_ref, send_ref,
    )


def near_kernel(
    slots_ref, where_ref, below_ref, centre_ref, above_ref, pieces_ref,
    keep_ref, pass_ref, send_ref,
):
    group_products(
        slots_ref, where_ref, (below_ref, centre_ref, above_ref), pieces_ref,
        where_ref[1], keep_ref, pass_ref, send_ref,
    )


def proximal_kernel(
    where_ref, slots_ref, near_ref, other_ref, early_ref, late_ref, last_ref, omega_ref, out_ref
):
    j = where_ref[3]
    odd_tile = where_ref[4] == 1
    rows = lax.broadcasted_iota(jnp.int32, (BLK, BLK), 0)
    columns = lax.broadcasted_iota(jnp.int32, (BLK, BLK), 1)
    early = early_ref[...] + last_ref[...]
    late = late_ref[...]
    for e in range(3):
        slot = slots_ref[0, e, j]
        total = near_ref[e] + other_ref[e]
        if e == 0:
            total = total + jnp.where(odd_tile, early, late).T
        if e == 2:
            total = total + jnp.where(odd_tile, late, early).T
        gradient = total * (0.5 / SAMPLES)
        omega = omega_ref[0, e, 0]
        if e == 1:
            diagonal = (slot >= 0) & (slot // NB == slot % NB)
            on_diagonal = (rows == columns) & diagonal
            inverse = 1.0 / jnp.where(on_diagonal, omega, 1.0)
            gradient = gradient - jnp.where(on_diagonal, inverse, 0.0)
        trial = omega - step_size * gradient
        shrunk = jnp.maximum(jnp.abs(trial) - step_size * penalty, 0.0)
        result = jnp.where(trial < 0.0, -shrunk, shrunk)
        if e == 1:
            result = jnp.where(on_diagonal, trial, result)
        out_ref[0, e, 0] = jnp.where(slot >= 0, result, 0.0)


def params():
    return pltpu.CompilerParams(vmem_limit_bytes=VMEM_LIMIT)


SMEM = pl.BlockSpec(memory_space=pltpu.SMEM)
WHOLE = pl.BlockSpec(memory_space=pltpu.VMEM)
TURNED = (NB, 2 * BLK, ROWS)
NATURAL = (NB, ROWS, 2 * BLK)


def omega_spec(offset):
    return pl.BlockSpec((1, 1, KMAX, BLK, BLK), lambda i: (0, offset, 0, 0, 0))


def full_spec(shape):
    return pl.BlockSpec(shape, lambda i: (0,) * len(shape))


def partial(offset, slots, tile, omega, before=None):
    first = before is None
    rows = tile.shape[0]
    turned = (NB, 2 * BLK, rows)
    in_specs = [SMEM, full_spec((rows, TILE)), omega_spec(offset)]
    inputs = [slots, tile, omega]
    if not first:
        in_specs.append(full_spec((NB, ROWS, BLK)))
        inputs.append(before)
    return pl.pallas_call(
        lambda *refs: partial_kernel(offset, first, *refs),
        name="partial_residual",
        grid=(1,),
        out_shape=(
            jax.ShapeDtypeStruct((NB, ROWS, BLK), f32),
            jax.ShapeDtypeStruct(turned, bf16),
        ),
        in_specs=in_specs,
        out_specs=(full_spec((NB, ROWS, BLK)), full_spec(turned)),
        scratch_shapes=[pltpu.VMEM((NB, rows, 2 * BLK), bf16)],
        compiler_params=params(),
        cost_estimate=pl.CostEstimate(
            flops=2 * KMAX * rows * 256 * 256, bytes_accessed=5 << 20, transcendentals=0
        ),
    )(*inputs)


HALF = (2, 3, BLK, BLK)
WAY = (4, 3, BLK, BLK)
GROUP_OUT = tuple(jax.ShapeDtypeStruct(shape, f32) for shape in (HALF, HALF, WAY))
GROUP_SPECS = tuple(full_spec(shape) for shape in (HALF, HALF, WAY))


def far_blocks(slots, where, tile, omega, before, half, below, centre):
    rows = tile.shape[0]
    return pl.pallas_call(
        far_kernel,
        name="far_blocks",
        grid=(1,),
        out_shape=GROUP_OUT
        + (jax.ShapeDtypeStruct(TURNED, bf16), jax.ShapeDtypeStruct(NATURAL, bf16)),
        in_specs=[
            SMEM,
            SMEM,
            full_spec((rows, TILE)),
            omega_spec(2),
            full_spec((NB, ROWS, BLK)),
            full_spec((NB, 2 * BLK, ROWS - rows)),
            full_spec(TURNED),
            full_spec(TURNED),
        ],
        out_specs=GROUP_SPECS + (full_spec(TURNED), full_spec(NATURAL)),
        scratch_shapes=[
            pltpu.VMEM((NB, ROWS, BLK), f32),
            pltpu.VMEM((NB, rows, 2 * BLK), bf16),
        ],
        compiler_params=params(),
        cost_estimate=pl.CostEstimate(
            flops=5 * KMAX * ROWS * 256 * 256, bytes_accessed=8 << 20, transcendentals=0
        ),
    )(slots, where, tile, omega, before, half, below, centre)


def near_blocks(slots, where, below, centre, above, pieces):
    return pl.pallas_call(
        near_kernel,
        name="near_blocks",
        grid=(1,),
        out_shape=GROUP_OUT,
        in_specs=[SMEM, SMEM]
        + [full_spec(TURNED)] * 3
        + [full_spec(NATURAL)],
        out_specs=GROUP_SPECS,
        compiler_params=params(),
        cost_estimate=pl.CostEstimate(
            flops=3 * KMAX * ROWS * 256 * 256, bytes_accessed=8 << 20, transcendentals=0
        ),
    )(slots, where, below, centre, above, pieces)


def edge_kernel(where_ref, near_ref, other_ref, early_ref, late_ref, last_ref):
    odd_tile = where_ref[4] == 1
    downward = near_ref[0] + other_ref[0]
    upward = near_ref[2] + other_ref[2]
    late_ref[...] = jnp.where(odd_tile, upward, downward)
    short = jnp.where(odd_tile, downward, upward)
    early_ref[...] = short
    last_ref[...] = short


def edge_values(where, near, other):
    block = jax.ShapeDtypeStruct((BLK, BLK), f32)
    return pl.pallas_call(
        edge_kernel,
        name="edge_values",
        grid=(1,),
        out_shape=(block,) * 3,
        in_specs=[SMEM] + [full_spec((3, BLK, BLK))] * 2,
        out_specs=(full_spec((BLK, BLK)),) * 3,
        compiler_params=params(),
        cost_estimate=pl.CostEstimate(
            flops=4 * BLK * BLK, bytes_accessed=6 * 4 * BLK * BLK, transcendentals=0
        ),
    )(where, near, other)


def proximal(where, slots, near, other, early, late, last, omega):
    block = pl.BlockSpec((BLK, BLK), lambda i, where, slots: (0, 0))
    triple = pl.BlockSpec((3, BLK, BLK), lambda i, where, slots: (0, 0, 0))
    own = pl.BlockSpec((1, 3, 1, BLK, BLK), lambda i, where, slots: (0, 0, where[3], 0, 0))
    return pl.pallas_call(
        proximal_kernel,
        name="proximal",
        grid_spec=pltpu.PrefetchScalarGridSpec(
            num_scalar_prefetch=2,
            grid=(1,),
            in_specs=[triple, triple, block, block, block, own],
            out_specs=pl.BlockSpec(
                (1, 3, 1, BLK, BLK), lambda i, where, slots: (0, 0, 0, 0, 0)
            ),
        ),
        out_shape=jax.ShapeDtypeStruct((1, 3, 1, BLK, BLK), f32),
        compiler_params=params(),
        cost_estimate=pl.CostEstimate(
            flops=20 * 3 * BLK * BLK, bytes_accessed=1 << 19, transcendentals=0
        ),
    )(where, slots, near, other, early, late, last, omega)


def shifted(value, axis, steps):
    count = lax.axis_size(axis)
    pairs = [(source, (source + steps) % count) for source in range(count)]
    return lax.ppermute(value, axis, pairs)


def x_exchange(value, step):
    pairs = []
    for x in range(4):
        for core in range(2):
            partner = x ^ 1 if core == step else 3 - x
            pairs.append((2 * x + core, 2 * partner + core))
    return lax.ppermute(value, ("x", "core"), pairs)


def edge_exchange(value, offset, step):
    count = lax.axis_size("col")
    pairs = []
    for t in range(offset, count, step):
        pairs += [(t, (t + 1) % count), ((t + 1) % count, t)]
    return lax.ppermute(value, "col", pairs)


def on_device(observations, omega, block_slots):
    x, y_hi, core = (lax.axis_index(n).astype(jnp.int32) for n in ("x", "y_hi", "core"))
    odd_tile = lax.axis_index("col").astype(jnp.int32) & 1
    where = jnp.stack([x, y_hi, core, 4 * x + 2 * y_hi + core, odd_tile])
    from_below = shifted(observations, "col", 1)
    cut = ROWS // 2
    above_early = shifted(observations[:cut], "col", -1)
    above_late = shifted(observations[cut:], "col", -1)
    residual, centre = partial(1, block_slots, observations, omega)
    residual, below = partial(0, block_slots, from_below, omega, residual)
    residual, half = partial(2, block_slots, above_early, omega, residual)
    far_keep, far_pass, far_send, above, pieces = far_blocks(
        block_slots, where, above_late, omega, residual, half, below, centre
    )
    far_got = shifted(far_send, "core", 1)
    near_keep, near_pass, near_send = near_blocks(
        block_slots, where, below, centre, above, pieces
    )
    near_got = shifted(near_send, "core", 1)
    far_first = x_exchange(far_pass + far_got[2:], 0)
    near_first = x_exchange(near_pass + near_got[2:], 0)
    far_second = x_exchange(far_keep[1] + far_got[1] + far_first[1], 1)
    far_sum = far_keep[0] + far_got[0] + far_first[0] + far_second
    other = shifted(far_sum, "y_hi", 1)
    near_second = x_exchange(near_keep[1] + near_got[1] + near_first[1], 1)
    near_sum = near_keep[0] + near_got[0] + near_first[0] + near_second
    early_out, late_out, last_out = edge_values(where, near_sum, other)
    early = edge_exchange(early_out, 0, 4)
    late = edge_exchange(late_out, 1, 2)
    last = edge_exchange(last_out, 2, 4)
    return proximal(where, block_slots, near_sum, other, early, late, last, omega)


def solution(mesh):
    devices = mesh.devices.reshape(4, 2, 2, 32)
    fine = Mesh(devices, ("x", "y_hi", "core", "col"))
    rows = ("x", "y_hi", "core")
    return jax.shard_map(
        on_device,
        mesh=fine,
        in_specs=(P(rows, "col"), P("col", None, None, None, None), P("col", None, None)),
        out_specs=P("col", None, rows, None, None),
        check_vma=False,
    )
```

```python
import jax
import jax.numpy as jnp
from jax import lax
from jax.experimental import pallas as pl
from jax.experimental.pallas import tpu as pltpu
from jax.sharding import Mesh, PartitionSpec as P

TILE = 1024
BLK = 128
NB = TILE // BLK
KMAX = 16
ROWS = 256
SAMPLES = 4096
step_size = 0.5
penalty = 0.1
f32 = jnp.float32
bf16 = jnp.bfloat16
PLACE = (0, 2, 1)
VMEM_LIMIT = 16 * 1024 * 1024


def split(value):
    high = value.astype(bf16)
    low = (value - high.astype(f32)).astype(bf16)
    return high, low


def split_tile(x_ref, natural_ref, turned_ref, start=0):
    rows = x_ref.shape[0]
    for a in range(NB):
        block = x_ref[:, a * BLK : (a + 1) * BLK]
        high, low = split(block)
        natural_ref[a, :, :BLK] = high
        natural_ref[a, :, BLK:] = low
        high, low = split(block.T)
        turned_ref[a, :BLK, start : start + rows] = high
        turned_ref[a, BLK:, start : start + rows] = low


def add_products(slots_ref, omega_ref, natural_ref, residual_ref, offset, start=0):
    rows = natural_ref.shape[1]

    def body(j, carry):
        slot = slots_ref[0, offset, j]
        active = slot >= 0
        place = jnp.maximum(slot, 0)
        a = place // NB
        b = place % NB
        weight = jnp.where(active, omega_ref[0, 0, j], 0.0)
        high, low = split(weight)
        half = jnp.concatenate([high, low], axis=1)
        weights = jnp.concatenate([half, half], axis=0)
        out = jnp.dot(natural_ref[a], weights, preferred_element_type=f32)
        residual_ref[b, start : start + rows] += out[:, :BLK] + out[:, BLK:]
        return carry

    lax.fori_loop(0, KMAX, body, 0, unroll=4)


def partial_kernel(offset, first, *refs):
    if first:
        slots_ref, x_ref, omega_ref, residual_ref, turned_ref, natural_ref = refs
        residual_ref[...] = jnp.zeros_like(residual_ref)
    else:
        slots_ref, x_ref, omega_ref, before_ref, residual_ref, turned_ref, natural_ref = refs
        residual_ref[...] = before_ref[...]
    split_tile(x_ref, natural_ref, turned_ref)
    add_products(slots_ref, omega_ref, natural_ref, residual_ref, offset)


def quadrant_sum(out):
    out = out[:BLK] + out[BLK:]
    return out[:, :BLK] + out[:, BLK:]


def slot_block(slots_ref, e, j, turned, pieces_ref):
    place = jnp.maximum(slots_ref[0, e, j], 0)
    out = jnp.dot(
        turned[e][place // NB], pieces_ref[place % NB], preferred_element_type=f32
    )
    return quadrant_sum(out)


def group_products(slots_ref, where_ref, turned, pieces_ref, y_hi, keep_ref, pass_ref, send_ref):
    x, core = where_ref[0], where_ref[2]
    even_pair, odd_pair = x ^ 1, 3 - x
    first = jnp.where(core == 0, even_pair, odd_pair)
    second = jnp.where(core == 0, odd_pair, even_pair)
    for r, x_of in enumerate((x, second, first, x ^ 2)):
        i = 2 * x_of + y_hi
        for e in range(3):
            even = slot_block(slots_ref, e, 2 * i, turned, pieces_ref)
            odd = slot_block(slots_ref, e, 2 * i + 1, turned, pieces_ref)
            if e == 1:
                even_turned, odd_turned = even.T, odd.T
                diagonal = i < NB // 2
                even, odd = (
                    even + jnp.where(diagonal, even_turned, odd_turned),
                    odd + jnp.where(diagonal, odd_turned, even_turned),
                )
            own_ref = keep_ref if r < 2 else pass_ref
            own_ref[r % 2, PLACE[e]] = jnp.where(core == 0, even, odd)
            send_ref[(0, 2, 1, 3)[r], PLACE[e]] = jnp.where(core == 0, odd, even)


def far_kernel(
    slots_ref, where_ref, x_ref, omega_ref, before_ref, half_ref, below_ref, centre_ref,
    keep_ref, pass_ref, send_ref, above_ref, pieces_ref, residual_ref, natural_ref,
):
    residual_ref[...] = before_ref[...]
    done = half_ref.shape[2]
    above_ref[:, :, :done] = half_ref[...]
    split_tile(x_ref, natural_ref, above_ref, done)
    add_products(slots_ref, omega_ref, natural_ref, residual_ref, 2, done)
    for b in range(NB):
        high, low = split(residual_ref[b])
        pieces_ref[b, :, :BLK] = high
        pieces_ref[b, :, BLK:] = low
    group_products(
        slots_ref, where_ref, (below_ref, centre_ref, above_ref), pieces_ref,
        1 - where_ref[1], keep_ref, pass_ref, send_ref,
    )


def near_kernel(
    slots_ref, where_ref, below_ref, centre_ref, above_ref, pieces_ref,
    keep_ref, pass_ref, send_ref,
):
    group_products(
        slots_ref, where_ref, (below_ref, centre_ref, above_ref), pieces_ref,
        where_ref[1], keep_ref, pass_ref, send_ref,
    )


def proximal_kernel(
    where_ref, slots_ref, near_ref, outer_ref, centre_ref, early_ref, late_ref, last_ref,
    omega_ref, out_ref,
):
    j = where_ref[3]
    odd_tile = where_ref[4] == 1
    rows = lax.broadcasted_iota(jnp.int32, (BLK, BLK), 0)
    columns = lax.broadcasted_iota(jnp.int32, (BLK, BLK), 1)
    early = early_ref[...] + last_ref[...]
    late = late_ref[...]
    for e in range(3):
        slot = slots_ref[0, e, j]
        total = near_ref[PLACE[e]] + (centre_ref[...] if e == 1 else outer_ref[PLACE[e]])
        if e == 0:
            total = total + jnp.where(odd_tile, early, late).T
        if e == 2:
            total = total + jnp.where(odd_tile, late, early).T
        gradient = total * (0.5 / SAMPLES)
        omega = omega_ref[0, e, 0]
        if e == 1:
            diagonal = (slot >= 0) & (slot // NB == slot % NB)
            on_diagonal = (rows == columns) & diagonal
            inverse = 1.0 / jnp.where(on_diagonal, omega, 1.0)
            gradient = gradient - jnp.where(on_diagonal, inverse, 0.0)
        trial = omega - step_size * gradient
        shrunk = jnp.maximum(jnp.abs(trial) - step_size * penalty, 0.0)
        result = jnp.where(trial < 0.0, -shrunk, shrunk)
        if e == 1:
            result = jnp.where(on_diagonal, trial, result)
        out_ref[0, e, 0] = jnp.where(slot >= 0, result, 0.0)


def params():
    return pltpu.CompilerParams(vmem_limit_bytes=VMEM_LIMIT)


SMEM = pl.BlockSpec(memory_space=pltpu.SMEM)
WHOLE = pl.BlockSpec(memory_space=pltpu.VMEM)
TURNED = (NB, 2 * BLK, ROWS)
NATURAL = (NB, ROWS, 2 * BLK)


def omega_spec(offset):
    return pl.BlockSpec((1, 1, KMAX, BLK, BLK), lambda i: (0, offset, 0, 0, 0))


def full_spec(shape):
    return pl.BlockSpec(shape, lambda i: (0,) * len(shape))


def partial(offset, slots, tile, omega, before=None):
    first = before is None
    rows = tile.shape[0]
    turned = (NB, 2 * BLK, rows)
    in_specs = [SMEM, full_spec((rows, TILE)), omega_spec(offset)]
    inputs = [slots, tile, omega]
    if not first:
        in_specs.append(full_spec((NB, ROWS, BLK)))
        inputs.append(before)
    return pl.pallas_call(
        lambda *refs: partial_kernel(offset, first, *refs),
        name="partial_residual",
        grid=(1,),
        out_shape=(
            jax.ShapeDtypeStruct((NB, ROWS, BLK), f32),
            jax.ShapeDtypeStruct(turned, bf16),
        ),
        in_specs=in_specs,
        out_specs=(full_spec((NB, ROWS, BLK)), full_spec(turned)),
        scratch_shapes=[pltpu.VMEM((NB, rows, 2 * BLK), bf16)],
        compiler_params=params(),
        cost_estimate=pl.CostEstimate(
            flops=2 * KMAX * rows * 256 * 256, bytes_accessed=5 << 20, transcendentals=0
        ),
    )(*inputs)


HALF = (2, 3, BLK, BLK)
WAY = (4, 3, BLK, BLK)
GROUP_OUT = tuple(jax.ShapeDtypeStruct(shape, f32) for shape in (HALF, HALF, WAY))
GROUP_SPECS = tuple(full_spec(shape) for shape in (HALF, HALF, WAY))


def far_blocks(slots, where, tile, omega, before, half, below, centre):
    rows = tile.shape[0]
    return pl.pallas_call(
        far_kernel,
        name="far_blocks",
        grid=(1,),
        out_shape=GROUP_OUT
        + (jax.ShapeDtypeStruct(TURNED, bf16), jax.ShapeDtypeStruct(NATURAL, bf16)),
        in_specs=[
            SMEM,
            SMEM,
            full_spec((rows, TILE)),
            omega_spec(2),
            full_spec((NB, ROWS, BLK)),
            full_spec((NB, 2 * BLK, ROWS - rows)),
            full_spec(TURNED),
            full_spec(TURNED),
        ],
        out_specs=GROUP_SPECS + (full_spec(TURNED), full_spec(NATURAL)),
        scratch_shapes=[
            pltpu.VMEM((NB, ROWS, BLK), f32),
            pltpu.VMEM((NB, rows, 2 * BLK), bf16),
        ],
        compiler_params=params(),
        cost_estimate=pl.CostEstimate(
            flops=5 * KMAX * ROWS * 256 * 256, bytes_accessed=8 << 20, transcendentals=0
        ),
    )(slots, where, tile, omega, before, half, below, centre)


def near_blocks(slots, where, below, centre, above, pieces):
    return pl.pallas_call(
        near_kernel,
        name="near_blocks",
        grid=(1,),
        out_shape=GROUP_OUT,
        in_specs=[SMEM, SMEM]
        + [full_spec(TURNED)] * 3
        + [full_spec(NATURAL)],
        out_specs=GROUP_SPECS,
        compiler_params=params(),
        cost_estimate=pl.CostEstimate(
            flops=3 * KMAX * ROWS * 256 * 256, bytes_accessed=8 << 20, transcendentals=0
        ),
    )(slots, where, below, centre, above, pieces)


def edge_kernel(where_ref, near_ref, outer_ref, early_ref, late_ref, last_ref):
    odd_tile = where_ref[4] == 1
    downward = near_ref[0] + outer_ref[0]
    upward = near_ref[1] + outer_ref[1]
    late_ref[...] = jnp.where(odd_tile, upward, downward)
    short = jnp.where(odd_tile, downward, upward)
    early_ref[...] = short
    last_ref[...] = short


def edge_values(where, near, outer):
    block = jax.ShapeDtypeStruct((BLK, BLK), f32)
    return pl.pallas_call(
        edge_kernel,
        name="edge_values",
        grid=(1,),
        out_shape=(block,) * 3,
        in_specs=[SMEM, full_spec((3, BLK, BLK)), full_spec((2, BLK, BLK))],
        out_specs=(full_spec((BLK, BLK)),) * 3,
        compiler_params=params(),
        cost_estimate=pl.CostEstimate(
            flops=4 * BLK * BLK, bytes_accessed=6 * 4 * BLK * BLK, transcendentals=0
        ),
    )(where, near, outer)


def proximal(where, slots, near, outer, centre, early, late, last, omega):
    block = pl.BlockSpec((BLK, BLK), lambda i, where, slots: (0, 0))
    triple = pl.BlockSpec((3, BLK, BLK), lambda i, where, slots: (0, 0, 0))
    pair = pl.BlockSpec((2, BLK, BLK), lambda i, where, slots: (0, 0, 0))
    own = pl.BlockSpec((1, 3, 1, BLK, BLK), lambda i, where, slots: (0, 0, where[3], 0, 0))
    return pl.pallas_call(
        proximal_kernel,
        name="proximal",
        grid_spec=pltpu.PrefetchScalarGridSpec(
            num_scalar_prefetch=2,
            grid=(1,),
            in_specs=[triple, pair] + [block] * 4 + [own],
            out_specs=pl.BlockSpec(
                (1, 3, 1, BLK, BLK), lambda i, where, slots: (0, 0, 0, 0, 0)
            ),
        ),
        out_shape=jax.ShapeDtypeStruct((1, 3, 1, BLK, BLK), f32),
        compiler_params=params(),
        cost_estimate=pl.CostEstimate(
            flops=20 * 3 * BLK * BLK, bytes_accessed=1 << 19, transcendentals=0
        ),
    )(where, slots, near, outer, centre, early, late, last, omega)


def shifted(value, axis, steps):
    count = lax.axis_size(axis)
    pairs = [(source, (source + steps) % count) for source in range(count)]
    return lax.ppermute(value, axis, pairs)


def x_exchange(value, step):
    pairs = []
    for x in range(4):
        for core in range(2):
            partner = x ^ 1 if core == step else 3 - x
            pairs.append((2 * x + core, 2 * partner + core))
    return lax.ppermute(value, ("x", "core"), pairs)


def after(value, earlier):
    return lax.optimization_barrier((value, earlier))[0]


def edge_exchange(value, offset, step):
    count = lax.axis_size("col")
    pairs = []
    for t in range(offset, count, step):
        pairs += [(t, (t + 1) % count), ((t + 1) % count, t)]
    return lax.ppermute(value, "col", pairs)


def on_device(observations, omega, block_slots):
    x, y_hi, core = (lax.axis_index(n).astype(jnp.int32) for n in ("x", "y_hi", "core"))
    odd_tile = lax.axis_index("col").astype(jnp.int32) & 1
    where = jnp.stack([x, y_hi, core, 4 * x + 2 * y_hi + core, odd_tile])
    from_below = shifted(observations, "col", 1)
    cut = ROWS // 2
    above_early = shifted(observations[:cut], "col", -1)
    above_late = shifted(observations[cut:], "col", -1)
    residual, centre = partial(1, block_slots, observations, omega)
    residual, below = partial(0, block_slots, from_below, omega, residual)
    residual, half = partial(2, block_slots, above_early, omega, residual)
    far_keep, far_pass, far_send, above, pieces = far_blocks(
        block_slots, where, above_late, omega, residual, half, below, centre
    )
    far_got = shifted(far_send, "core", 1)
    near_keep, near_pass, near_send = near_blocks(
        block_slots, where, below, centre, above, pieces
    )
    near_got = shifted(near_send, "core", 1)
    far_first = x_exchange(far_pass + far_got[2:], 0)
    near_first = x_exchange(near_pass + near_got[2:], 0)
    far_second = x_exchange(far_keep[1] + far_got[1] + far_first[1], 1)
    parts = (far_keep[0], far_got[0], far_first[0], far_second)
    outer_out = sum(x[:2] for x in parts)
    outer = shifted(outer_out, "y_hi", 1)
    centre_out = sum(after(x[2], outer_out) for x in parts)
    centre_sum = shifted(centre_out, "y_hi", 1)
    near_second = x_exchange(near_keep[1] + near_got[1] + near_first[1], 1)
    near_sum = near_keep[0] + near_got[0] + near_first[0] + near_second
    early_out, late_out, last_out = edge_values(where, near_sum, outer)
    early = edge_exchange(early_out, 0, 4)
    late = edge_exchange(late_out, 1, 2)
    last = edge_exchange(last_out, 2, 4)
    return proximal(where, block_slots, near_sum, outer, centre_sum, early, late, last, omega)


def solution(mesh):
    devices = mesh.devices.reshape(4, 2, 2, 32)
    fine = Mesh(devices, ("x", "y_hi", "core", "col"))
    rows = ("x", "y_hi", "core")
    return jax.shard_map(
        on_device,
        mesh=fine,
        in_specs=(P(rows, "col"), P("col", None, None, None, None), P("col", None, None)),
        out_specs=P("col", None, rows, None, None),
        check_vma=False,
    )
```

```python
import jax
import jax.numpy as jnp
from jax import lax
from jax.experimental import pallas as pl
from jax.experimental.pallas import tpu as pltpu
from jax.sharding import Mesh, PartitionSpec as P

TILE = 1024
BLK = 128
NB = TILE // BLK
KMAX = 16
ROWS = 256
SAMPLES = 4096
step_size = 0.5
penalty = 0.1
f32 = jnp.float32
bf16 = jnp.bfloat16
PLACE = (0, 2, 1)
VMEM_LIMIT = 16 * 1024 * 1024


def split(value):
    high = value.astype(bf16)
    low = (value - high.astype(f32)).astype(bf16)
    return high, low


def split_tile(x_ref, natural_ref, turned_ref, start=0):
    rows = x_ref.shape[0]
    for a in range(NB):
        block = x_ref[:, a * BLK : (a + 1) * BLK]
        high, low = split(block)
        natural_ref[a, :, :BLK] = high
        natural_ref[a, :, BLK:] = low
        high, low = split(block.T)
        turned_ref[a, :BLK, start : start + rows] = high
        turned_ref[a, BLK:, start : start + rows] = low


def add_products(slots_ref, omega_ref, natural_ref, residual_ref, offset, start=0):
    rows = natural_ref.shape[1]

    def body(j, carry):
        slot = slots_ref[0, offset, j]
        active = slot >= 0
        place = jnp.maximum(slot, 0)
        a = place // NB
        b = place % NB
        weight = jnp.where(active, omega_ref[0, 0, j], 0.0)
        high, low = split(weight)
        half = jnp.concatenate([high, low], axis=1)
        weights = jnp.concatenate([half, half], axis=0)
        out = jnp.dot(natural_ref[a], weights, preferred_element_type=f32)
        residual_ref[b, start : start + rows] += out[:, :BLK] + out[:, BLK:]
        return carry

    lax.fori_loop(0, KMAX, body, 0, unroll=4)


def partial_kernel(offset, first, *refs):
    if first:
        slots_ref, x_ref, omega_ref, residual_ref, turned_ref, natural_ref = refs
        residual_ref[...] = jnp.zeros_like(residual_ref)
    else:
        slots_ref, x_ref, omega_ref, before_ref, residual_ref, turned_ref, natural_ref = refs
        residual_ref[...] = before_ref[...]
    split_tile(x_ref, natural_ref, turned_ref)
    add_products(slots_ref, omega_ref, natural_ref, residual_ref, offset)


def quadrant_sum(out):
    out = out[:BLK] + out[BLK:]
    return out[:, :BLK] + out[:, BLK:]


def slot_block(slots_ref, e, j, turned, pieces_ref):
    place = jnp.maximum(slots_ref[0, e, j], 0)
    out = jnp.dot(
        turned[e][place // NB], pieces_ref[place % NB], preferred_element_type=f32
    )
    return quadrant_sum(out)


def group_products(slots_ref, where_ref, turned, pieces_ref, y_hi, keep_ref, pass_ref, send_ref):
    x, core = where_ref[0], where_ref[2]
    even_pair, odd_pair = x ^ 1, 3 - x
    first = jnp.where(core == 0, even_pair, odd_pair)
    second = jnp.where(core == 0, odd_pair, even_pair)
    for r, x_of in enumerate((x, second, first, x ^ 2)):
        i = 2 * x_of + y_hi
        for e in range(3):
            even = slot_block(slots_ref, e, 2 * i, turned, pieces_ref)
            odd = slot_block(slots_ref, e, 2 * i + 1, turned, pieces_ref)
            if e == 1:
                even_turned, odd_turned = even.T, odd.T
                diagonal = i < NB // 2
                even, odd = (
                    even + jnp.where(diagonal, even_turned, odd_turned),
                    odd + jnp.where(diagonal, odd_turned, even_turned),
                )
            own_ref = keep_ref if r < 2 else pass_ref
            own_ref[r % 2, PLACE[e]] = jnp.where(core == 0, even, odd)
            send_ref[(0, 2, 1, 3)[r], PLACE[e]] = jnp.where(core == 0, odd, even)


def far_kernel(
    slots_ref, where_ref, x_ref, omega_ref, before_ref, half_ref, below_ref, centre_ref,
    keep_ref, pass_ref, send_ref, above_ref, pieces_ref, residual_ref, natural_ref,
):
    residual_ref[...] = before_ref[...]
    done = half_ref.shape[2]
    above_ref[:, :, :done] = half_ref[...]
    split_tile(x_ref, natural_ref, above_ref, done)
    add_products(slots_ref, omega_ref, natural_ref, residual_ref, 2, done)
    for b in range(NB):
        high, low = split(residual_ref[b])
        pieces_ref[b, :, :BLK] = high
        pieces_ref[b, :, BLK:] = low
    group_products(
        slots_ref, where_ref, (below_ref, centre_ref, above_ref), pieces_ref,
        1 - where_ref[1], keep_ref, pass_ref, send_ref,
    )


def near_kernel(
    slots_ref, where_ref, below_ref, centre_ref, above_ref, pieces_ref,
    keep_ref, pass_ref, send_ref,
):
    group_products(
        slots_ref, where_ref, (below_ref, centre_ref, above_ref), pieces_ref,
        where_ref[1], keep_ref, pass_ref, send_ref,
    )


def proximal_kernel(
    where_ref, slots_ref, near_ref, outer_ref, centre_ref, early_ref, late_ref, last_ref,
    omega_ref, out_ref,
):
    j = where_ref[3]
    odd_tile = where_ref[4] == 1
    rows = lax.broadcasted_iota(jnp.int32, (BLK, BLK), 0)
    columns = lax.broadcasted_iota(jnp.int32, (BLK, BLK), 1)
    early = early_ref[...] + last_ref[...]
    late = late_ref[...]
    for e in range(3):
        slot = slots_ref[0, e, j]
        total = near_ref[PLACE[e]] + (centre_ref[...] if e == 1 else outer_ref[PLACE[e]])
        if e == 0:
            total = total + jnp.where(odd_tile, early, late).T
        if e == 2:
            total = total + jnp.where(odd_tile, late, early).T
        gradient = total * (0.5 / SAMPLES)
        omega = omega_ref[0, e, 0]
        if e == 1:
            diagonal = (slot >= 0) & (slot // NB == slot % NB)
            on_diagonal = (rows == columns) & diagonal
            inverse = 1.0 / jnp.where(on_diagonal, omega, 1.0)
            gradient = gradient - jnp.where(on_diagonal, inverse, 0.0)
        trial = omega - step_size * gradient
        shrunk = jnp.maximum(jnp.abs(trial) - step_size * penalty, 0.0)
        result = jnp.where(trial < 0.0, -shrunk, shrunk)
        if e == 1:
            result = jnp.where(on_diagonal, trial, result)
        out_ref[0, e, 0] = jnp.where(slot >= 0, result, 0.0)


def params():
    return pltpu.CompilerParams(vmem_limit_bytes=VMEM_LIMIT)


SMEM = pl.BlockSpec(memory_space=pltpu.SMEM)
WHOLE = pl.BlockSpec(memory_space=pltpu.VMEM)
TURNED = (NB, 2 * BLK, ROWS)
NATURAL = (NB, ROWS, 2 * BLK)


def omega_spec(offset):
    return pl.BlockSpec((1, 1, KMAX, BLK, BLK), lambda i: (0, offset, 0, 0, 0))


def full_spec(shape):
    return pl.BlockSpec(shape, lambda i: (0,) * len(shape))


def partial(offset, slots, tile, omega, before=None):
    first = before is None
    rows = tile.shape[0]
    turned = (NB, 2 * BLK, rows)
    in_specs = [SMEM, full_spec((rows, TILE)), omega_spec(offset)]
    inputs = [slots, tile, omega]
    if not first:
        in_specs.append(full_spec((NB, ROWS, BLK)))
        inputs.append(before)
    return pl.pallas_call(
        lambda *refs: partial_kernel(offset, first, *refs),
        name="partial_residual",
        grid=(1,),
        out_shape=(
            jax.ShapeDtypeStruct((NB, ROWS, BLK), f32),
            jax.ShapeDtypeStruct(turned, bf16),
        ),
        in_specs=in_specs,
        out_specs=(full_spec((NB, ROWS, BLK)), full_spec(turned)),
        scratch_shapes=[pltpu.VMEM((NB, rows, 2 * BLK), bf16)],
        compiler_params=params(),
        cost_estimate=pl.CostEstimate(
            flops=2 * KMAX * rows * 256 * 256, bytes_accessed=5 << 20, transcendentals=0
        ),
    )(*inputs)


HALF = (2, 3, BLK, BLK)
WAY = (4, 3, BLK, BLK)
GROUP_OUT = tuple(jax.ShapeDtypeStruct(shape, f32) for shape in (HALF, HALF, WAY))
GROUP_SPECS = tuple(full_spec(shape) for shape in (HALF, HALF, WAY))


def far_blocks(slots, where, tile, omega, before, half, below, centre):
    rows = tile.shape[0]
    return pl.pallas_call(
        far_kernel,
        name="far_blocks",
        grid=(1,),
        out_shape=GROUP_OUT
        + (jax.ShapeDtypeStruct(TURNED, bf16), jax.ShapeDtypeStruct(NATURAL, bf16)),
        in_specs=[
            SMEM,
            SMEM,
            full_spec((rows, TILE)),
            omega_spec(2),
            full_spec((NB, ROWS, BLK)),
            full_spec((NB, 2 * BLK, ROWS - rows)),
            full_spec(TURNED),
            full_spec(TURNED),
        ],
        out_specs=GROUP_SPECS + (full_spec(TURNED), full_spec(NATURAL)),
        scratch_shapes=[
            pltpu.VMEM((NB, ROWS, BLK), f32),
            pltpu.VMEM((NB, rows, 2 * BLK), bf16),
        ],
        compiler_params=params(),
        cost_estimate=pl.CostEstimate(
            flops=5 * KMAX * ROWS * 256 * 256, bytes_accessed=8 << 20, transcendentals=0
        ),
    )(slots, where, tile, omega, before, half, below, centre)


def near_blocks(slots, where, below, centre, above, pieces):
    return pl.pallas_call(
        near_kernel,
        name="near_blocks",
        grid=(1,),
        out_shape=GROUP_OUT,
        in_specs=[SMEM, SMEM]
        + [full_spec(TURNED)] * 3
        + [full_spec(NATURAL)],
        out_specs=GROUP_SPECS,
        compiler_params=params(),
        cost_estimate=pl.CostEstimate(
            flops=3 * KMAX * ROWS * 256 * 256, bytes_accessed=8 << 20, transcendentals=0
        ),
    )(slots, where, below, centre, above, pieces)


def edge_kernel(
    where_ref, outer_ref, keep_ref, got_ref, first_ref, second_ref,
    near_ref, early_ref, late_ref, last_ref,
):
    odd_tile = where_ref[4] == 1
    for e in range(3):
        near_ref[e] = keep_ref[0, e] + got_ref[0, e] + first_ref[0, e] + second_ref[e]
    downward = near_ref[0] + outer_ref[0]
    upward = near_ref[1] + outer_ref[1]
    late_ref[...] = jnp.where(odd_tile, upward, downward)
    short = jnp.where(odd_tile, downward, upward)
    early_ref[...] = short
    last_ref[...] = short


def edge_values(where, *parts):
    shapes = ((3, BLK, BLK),) + ((BLK, BLK),) * 3
    return pl.pallas_call(
        edge_kernel,
        name="edge_values",
        grid=(1,),
        out_shape=tuple(jax.ShapeDtypeStruct(shape, f32) for shape in shapes),
        in_specs=[SMEM] + [full_spec(part.shape) for part in parts],
        out_specs=tuple(full_spec(shape) for shape in shapes),
        compiler_params=params(),
        cost_estimate=pl.CostEstimate(
            flops=16 * BLK * BLK, bytes_accessed=20 * 4 * BLK * BLK, transcendentals=0
        ),
    )(where, *parts)


def proximal(where, slots, near, outer, centre, early, late, last, omega):
    block = pl.BlockSpec((BLK, BLK), lambda i, where, slots: (0, 0))
    triple = pl.BlockSpec((3, BLK, BLK), lambda i, where, slots: (0, 0, 0))
    pair = pl.BlockSpec((2, BLK, BLK), lambda i, where, slots: (0, 0, 0))
    own = pl.BlockSpec((1, 3, 1, BLK, BLK), lambda i, where, slots: (0, 0, where[3], 0, 0))
    return pl.pallas_call(
        proximal_kernel,
        name="proximal",
        grid_spec=pltpu.PrefetchScalarGridSpec(
            num_scalar_prefetch=2,
            grid=(1,),
            in_specs=[triple, pair] + [block] * 4 + [own],
            out_specs=pl.BlockSpec(
                (1, 3, 1, BLK, BLK), lambda i, where, slots: (0, 0, 0, 0, 0)
            ),
        ),
        out_shape=jax.ShapeDtypeStruct((1, 3, 1, BLK, BLK), f32),
        compiler_params=params(),
        cost_estimate=pl.CostEstimate(
            flops=20 * 3 * BLK * BLK, bytes_accessed=1 << 19, transcendentals=0
        ),
    )(where, slots, near, outer, centre, early, late, last, omega)


def shifted(value, axis, steps):
    count = lax.axis_size(axis)
    pairs = [(source, (source + steps) % count) for source in range(count)]
    return lax.ppermute(value, axis, pairs)


def x_exchange(value, step):
    pairs = []
    for x in range(4):
        for core in range(2):
            partner = x ^ 1 if core == step else 3 - x
            pairs.append((2 * x + core, 2 * partner + core))
    return lax.ppermute(value, ("x", "core"), pairs)


def after(value, earlier):
    return lax.optimization_barrier((value, earlier))[0]


def edge_exchange(value, offset, step):
    count = lax.axis_size("col")
    pairs = []
    for t in range(offset, count, step):
        pairs += [(t, (t + 1) % count), ((t + 1) % count, t)]
    return lax.ppermute(value, "col", pairs)


def on_device(observations, omega, block_slots):
    x, y_hi, core = (lax.axis_index(n).astype(jnp.int32) for n in ("x", "y_hi", "core"))
    odd_tile = lax.axis_index("col").astype(jnp.int32) & 1
    where = jnp.stack([x, y_hi, core, 4 * x + 2 * y_hi + core, odd_tile])
    from_below = shifted(observations, "col", 1)
    cut = ROWS // 2
    above_early = shifted(observations[:cut], "col", -1)
    above_late = shifted(observations[cut:], "col", -1)
    residual, centre = partial(1, block_slots, observations, omega)
    residual, below = partial(0, block_slots, from_below, omega, residual)
    residual, half = partial(2, block_slots, above_early, omega, residual)
    far_keep, far_pass, far_send, above, pieces = far_blocks(
        block_slots, where, above_late, omega, residual, half, below, centre
    )
    far_got = shifted(far_send, "core", 1)
    near_keep, near_pass, near_send = near_blocks(
        block_slots, where, below, centre, above, pieces
    )
    near_got = shifted(near_send, "core", 1)
    far_first = x_exchange(far_pass + far_got[2:], 0)
    near_first = x_exchange(near_pass + near_got[2:], 0)
    far_second = x_exchange(far_keep[1] + far_got[1] + far_first[1], 1)
    parts = (far_keep[0], far_got[0], far_first[0], far_second)
    outer_out = sum(x[:2] for x in parts)
    outer = shifted(outer_out, "y_hi", 1)
    centre_out = sum(x[2] for x in parts[:3]) + after(far_second, outer_out)[2]
    centre_sum = shifted(centre_out, "y_hi", 1)
    near_second = x_exchange(near_keep[1] + near_got[1] + near_first[1], 1)
    near_sum, early_out, late_out, last_out = edge_values(
        where, outer, near_keep, near_got, near_first, near_second
    )
    early = edge_exchange(early_out, 0, 4)
    late = edge_exchange(late_out, 1, 2)
    last = edge_exchange(last_out, 2, 4)
    return proximal(where, block_slots, near_sum, outer, centre_sum, early, late, last, omega)


def solution(mesh):
    devices = mesh.devices.reshape(4, 2, 2, 32)
    fine = Mesh(devices, ("x", "y_hi", "core", "col"))
    rows = ("x", "y_hi", "core")
    return jax.shard_map(
        on_device,
        mesh=fine,
        in_specs=(P(rows, "col"), P("col", None, None, None, None), P("col", None, None)),
        out_specs=P("col", None, rows, None, None),
        check_vma=False,
    )
```

```python
import jax
import jax.numpy as jnp
from jax import lax
from jax.experimental import pallas as pl
from jax.experimental.pallas import tpu as pltpu
from jax.sharding import Mesh, PartitionSpec as P

TILE = 1024
BLK = 128
NB = TILE // BLK
KMAX = 16
ROWS = 256
SAMPLES = 4096
step_size = 0.5
penalty = 0.1
f32 = jnp.float32
bf16 = jnp.bfloat16
PLACE = (0, 2, 1)
VMEM_LIMIT = 16 * 1024 * 1024


def split(value):
    high = value.astype(bf16)
    low = (value - high.astype(f32)).astype(bf16)
    return high, low


def split_tile(x_ref, natural_ref, turned_ref, start=0):
    rows = x_ref.shape[0]
    for a in range(NB):
        block = x_ref[:, a * BLK : (a + 1) * BLK]
        high, low = split(block)
        natural_ref[a, :, :BLK] = high
        natural_ref[a, :, BLK:] = low
        high, low = split(block.T)
        turned_ref[a, :BLK, start : start + rows] = high
        turned_ref[a, BLK:, start : start + rows] = low


def add_products(slots_ref, omega_ref, natural_ref, residual_ref, offset, start=0):
    rows = natural_ref.shape[1]

    def body(j, carry):
        slot = slots_ref[0, offset, j]
        active = slot >= 0
        place = jnp.maximum(slot, 0)
        a = place // NB
        b = place % NB
        weight = jnp.where(active, omega_ref[0, 0, j], 0.0)
        high, low = split(weight)
        half = jnp.concatenate([high, low], axis=1)
        weights = jnp.concatenate([half, half], axis=0)
        out = jnp.dot(natural_ref[a], weights, preferred_element_type=f32)
        residual_ref[b, start : start + rows] += out[:, :BLK] + out[:, BLK:]
        return carry

    lax.fori_loop(0, KMAX, body, 0, unroll=4)


def partial_kernel(offset, first, *refs):
    if first:
        slots_ref, x_ref, omega_ref, residual_ref, turned_ref, natural_ref = refs
        residual_ref[...] = jnp.zeros_like(residual_ref)
    else:
        slots_ref, x_ref, omega_ref, before_ref, residual_ref, turned_ref, natural_ref = refs
        residual_ref[...] = before_ref[...]
    split_tile(x_ref, natural_ref, turned_ref)
    add_products(slots_ref, omega_ref, natural_ref, residual_ref, offset)


def quadrant_sum(out):
    out = out[:BLK] + out[BLK:]
    return out[:, :BLK] + out[:, BLK:]


def slot_block(slots_ref, e, j, turned, pieces_ref):
    place = jnp.maximum(slots_ref[0, e, j], 0)
    out = jnp.dot(
        turned[e][place // NB], pieces_ref[place % NB], preferred_element_type=f32
    )
    return quadrant_sum(out)


def group_products(slots_ref, where_ref, turned, pieces_ref, y_hi, keep_ref, pass_ref, send_ref):
    x, core = where_ref[0], where_ref[2]
    even_pair, odd_pair = x ^ 1, 3 - x
    first = jnp.where(core == 0, even_pair, odd_pair)
    second = jnp.where(core == 0, odd_pair, even_pair)
    for r, x_of in enumerate((x, second, first, x ^ 2)):
        i = 2 * x_of + y_hi
        for e in range(3):
            even = slot_block(slots_ref, e, 2 * i, turned, pieces_ref)
            odd = slot_block(slots_ref, e, 2 * i + 1, turned, pieces_ref)
            if e == 1:
                even_turned, odd_turned = even.T, odd.T
                diagonal = i < NB // 2
                even, odd = (
                    even + jnp.where(diagonal, even_turned, odd_turned),
                    odd + jnp.where(diagonal, odd_turned, even_turned),
                )
            own_ref = keep_ref if r < 2 else pass_ref
            own_ref[r % 2, PLACE[e]] = jnp.where(core == 0, even, odd)
            send_ref[(0, 2, 1, 3)[r], PLACE[e]] = jnp.where(core == 0, odd, even)


def far_kernel(
    slots_ref, where_ref, x_ref, omega_ref, before_ref, half_ref, below_ref, centre_ref,
    keep_ref, pass_ref, send_ref, above_ref, pieces_ref, residual_ref, natural_ref,
):
    residual_ref[...] = before_ref[...]
    done = half_ref.shape[2]
    above_ref[:, :, :done] = half_ref[...]
    split_tile(x_ref, natural_ref, above_ref, done)
    add_products(slots_ref, omega_ref, natural_ref, residual_ref, 2, done)
    for b in range(NB):
        high, low = split(residual_ref[b])
        pieces_ref[b, :, :BLK] = high
        pieces_ref[b, :, BLK:] = low
    group_products(
        slots_ref, where_ref, (below_ref, centre_ref, above_ref), pieces_ref,
        1 - where_ref[1], keep_ref, pass_ref, send_ref,
    )


def near_kernel(
    slots_ref, where_ref, below_ref, centre_ref, above_ref, pieces_ref,
    keep_ref, pass_ref, send_ref,
):
    group_products(
        slots_ref, where_ref, (below_ref, centre_ref, above_ref), pieces_ref,
        where_ref[1], keep_ref, pass_ref, send_ref,
    )


def proximal_kernel(
    where_ref, slots_ref, near_ref, outer_ref, centre_ref, early_ref, late_ref, last_ref,
    omega_ref, out_ref,
):
    j = where_ref[3]
    odd_tile = where_ref[4] == 1
    rows = lax.broadcasted_iota(jnp.int32, (BLK, BLK), 0)
    columns = lax.broadcasted_iota(jnp.int32, (BLK, BLK), 1)
    early = early_ref[...] + last_ref[...]
    late = late_ref[...]
    for e in range(3):
        slot = slots_ref[0, e, j]
        total = near_ref[PLACE[e]] + (centre_ref[...] if e == 1 else outer_ref[PLACE[e]])
        if e == 0:
            total = total + jnp.where(odd_tile, early, late).T
        if e == 2:
            total = total + jnp.where(odd_tile, late, early).T
        gradient = total * (0.5 / SAMPLES)
        omega = omega_ref[0, e, 0]
        if e == 1:
            diagonal = (slot >= 0) & (slot // NB == slot % NB)
            on_diagonal = (rows == columns) & diagonal
            inverse = 1.0 / jnp.where(on_diagonal, omega, 1.0)
            gradient = gradient - jnp.where(on_diagonal, inverse, 0.0)
        trial = omega - step_size * gradient
        shrunk = jnp.maximum(jnp.abs(trial) - step_size * penalty, 0.0)
        result = jnp.where(trial < 0.0, -shrunk, shrunk)
        if e == 1:
            result = jnp.where(on_diagonal, trial, result)
        out_ref[0, e, 0] = jnp.where(slot >= 0, result, 0.0)


def params():
    return pltpu.CompilerParams(vmem_limit_bytes=VMEM_LIMIT)


SMEM = pl.BlockSpec(memory_space=pltpu.SMEM)
WHOLE = pl.BlockSpec(memory_space=pltpu.VMEM)
TURNED = (NB, 2 * BLK, ROWS)
NATURAL = (NB, ROWS, 2 * BLK)


def omega_spec(offset):
    return pl.BlockSpec((1, 1, KMAX, BLK, BLK), lambda i: (0, offset, 0, 0, 0))


def full_spec(shape):
    return pl.BlockSpec(shape, lambda i: (0,) * len(shape))


def partial(offset, slots, tile, omega, before=None):
    first = before is None
    rows = tile.shape[0]
    turned = (NB, 2 * BLK, rows)
    in_specs = [SMEM, full_spec((rows, TILE)), omega_spec(offset)]
    inputs = [slots, tile, omega]
    if not first:
        in_specs.append(full_spec((NB, ROWS, BLK)))
        inputs.append(before)
    return pl.pallas_call(
        lambda *refs: partial_kernel(offset, first, *refs),
        name="partial_residual",
        grid=(1,),
        out_shape=(
            jax.ShapeDtypeStruct((NB, ROWS, BLK), f32),
            jax.ShapeDtypeStruct(turned, bf16),
        ),
        in_specs=in_specs,
        out_specs=(full_spec((NB, ROWS, BLK)), full_spec(turned)),
        scratch_shapes=[pltpu.VMEM((NB, rows, 2 * BLK), bf16)],
        compiler_params=params(),
        cost_estimate=pl.CostEstimate(
            flops=2 * KMAX * rows * 256 * 256, bytes_accessed=5 << 20, transcendentals=0
        ),
    )(*inputs)


HALF = (2, 3, BLK, BLK)
WAY = (4, 3, BLK, BLK)
GROUP_OUT = tuple(jax.ShapeDtypeStruct(shape, f32) for shape in (HALF, HALF, WAY))
GROUP_SPECS = tuple(full_spec(shape) for shape in (HALF, HALF, WAY))


def far_blocks(slots, where, tile, omega, before, half, below, centre):
    rows = tile.shape[0]
    return pl.pallas_call(
        far_kernel,
        name="far_blocks",
        grid=(1,),
        out_shape=GROUP_OUT
        + (jax.ShapeDtypeStruct(TURNED, bf16), jax.ShapeDtypeStruct(NATURAL, bf16)),
        in_specs=[
            SMEM,
            SMEM,
            full_spec((rows, TILE)),
            omega_spec(2),
            full_spec((NB, ROWS, BLK)),
            full_spec((NB, 2 * BLK, ROWS - rows)),
            full_spec(TURNED),
            full_spec(TURNED),
        ],
        out_specs=GROUP_SPECS + (full_spec(TURNED), full_spec(NATURAL)),
        scratch_shapes=[
            pltpu.VMEM((NB, ROWS, BLK), f32),
            pltpu.VMEM((NB, rows, 2 * BLK), bf16),
        ],
        compiler_params=params(),
        cost_estimate=pl.CostEstimate(
            flops=5 * KMAX * ROWS * 256 * 256, bytes_accessed=8 << 20, transcendentals=0
        ),
    )(slots, where, tile, omega, before, half, below, centre)


def near_blocks(slots, where, below, centre, above, pieces):
    return pl.pallas_call(
        near_kernel,
        name="near_blocks",
        grid=(1,),
        out_shape=GROUP_OUT,
        in_specs=[SMEM, SMEM]
        + [full_spec(TURNED)] * 3
        + [full_spec(NATURAL)],
        out_specs=GROUP_SPECS,
        compiler_params=params(),
        cost_estimate=pl.CostEstimate(
            flops=3 * KMAX * ROWS * 256 * 256, bytes_accessed=8 << 20, transcendentals=0
        ),
    )(slots, where, below, centre, above, pieces)


def edge_kernel(
    where_ref, outer_ref, keep_ref, got_ref, first_ref, second_ref,
    near_ref, early_ref, late_ref, last_ref,
):
    odd_tile = where_ref[4] == 1
    for e in range(3):
        near_ref[e] = keep_ref[0, e] + got_ref[0, e] + first_ref[0, e] + second_ref[e]
    downward = near_ref[0] + outer_ref[0]
    upward = near_ref[1] + outer_ref[1]
    late_ref[...] = jnp.where(odd_tile, upward, downward)
    short = jnp.where(odd_tile, downward, upward)
    early_ref[...] = short
    last_ref[...] = short


def edge_values(where, *parts):
    shapes = ((3, BLK, BLK),) + ((BLK, BLK),) * 3
    return pl.pallas_call(
        edge_kernel,
        name="edge_values",
        grid=(1,),
        out_shape=tuple(jax.ShapeDtypeStruct(shape, f32) for shape in shapes),
        in_specs=[SMEM] + [full_spec(part.shape) for part in parts],
        out_specs=tuple(full_spec(shape) for shape in shapes),
        compiler_params=params(),
        cost_estimate=pl.CostEstimate(
            flops=16 * BLK * BLK, bytes_accessed=20 * 4 * BLK * BLK, transcendentals=0
        ),
    )(where, *parts)


def proximal(where, slots, near, outer, centre, early, late, last, omega):
    block = pl.BlockSpec((BLK, BLK), lambda i, where, slots: (0, 0))
    triple = pl.BlockSpec((3, BLK, BLK), lambda i, where, slots: (0, 0, 0))
    pair = pl.BlockSpec((2, BLK, BLK), lambda i, where, slots: (0, 0, 0))
    own = pl.BlockSpec((1, 3, 1, BLK, BLK), lambda i, where, slots: (0, 0, where[3], 0, 0))
    return pl.pallas_call(
        proximal_kernel,
        name="proximal",
        grid_spec=pltpu.PrefetchScalarGridSpec(
            num_scalar_prefetch=2,
            grid=(1,),
            in_specs=[triple, pair] + [block] * 4 + [own],
            out_specs=pl.BlockSpec(
                (1, 3, 1, BLK, BLK), lambda i, where, slots: (0, 0, 0, 0, 0)
            ),
        ),
        out_shape=jax.ShapeDtypeStruct((1, 3, 1, BLK, BLK), f32),
        compiler_params=params(),
        cost_estimate=pl.CostEstimate(
            flops=20 * 3 * BLK * BLK, bytes_accessed=1 << 19, transcendentals=0
        ),
    )(where, slots, near, outer, centre, early, late, last, omega)


def shifted(value, axis, steps):
    count = lax.axis_size(axis)
    pairs = [(source, (source + steps) % count) for source in range(count)]
    return lax.ppermute(value, axis, pairs)


def x_exchange(value, step):
    pairs = []
    for x in range(4):
        for core in range(2):
            partner = x ^ 1 if core == step else 3 - x
            pairs.append((2 * x + core, 2 * partner + core))
    return lax.ppermute(value, ("x", "core"), pairs)


def after(value, earlier):
    return lax.optimization_barrier((value, earlier))[0]


def edge_exchange(value, offset, step):
    count = lax.axis_size("col")
    pairs = []
    for t in range(offset, count, step):
        pairs += [(t, (t + 1) % count), ((t + 1) % count, t)]
    return lax.ppermute(value, "col", pairs)


def on_device(observations, omega, block_slots):
    x, y_hi, core = (lax.axis_index(n).astype(jnp.int32) for n in ("x", "y_hi", "core"))
    odd_tile = lax.axis_index("col").astype(jnp.int32) & 1
    where = jnp.stack([x, y_hi, core, 4 * x + 2 * y_hi + core, odd_tile])
    from_below = shifted(observations, "col", 1)
    cut = ROWS // 2
    above_early = shifted(observations[:cut], "col", -1)
    above_late = shifted(observations[cut:], "col", -1)
    residual, centre = partial(1, block_slots, observations, omega)
    residual, below = partial(0, block_slots, from_below, omega, residual)
    residual, half = partial(2, block_slots, above_early, omega, residual)
    far_keep, far_pass, far_send, above, pieces = far_blocks(
        block_slots, where, above_late, omega, residual, half, below, centre
    )
    far_got = shifted(far_send, "core", 1)
    near_keep, near_pass, near_send = near_blocks(
        block_slots, where, below, centre, above, pieces
    )
    near_got = shifted(near_send, "core", 1)
    far_first = x_exchange(far_pass + far_got[2:], 0)
    near_first = x_exchange(near_pass + near_got[2:], 0)
    far_second = x_exchange(far_keep[1] + far_got[1] + far_first[1], 1)
    parts = (far_keep[0], far_got[0], far_first[0], far_second)
    outer_out = sum(x[:2] for x in parts)
    outer = shifted(outer_out, "y_hi", 1)
    centre_out = sum(x[2] for x in parts[:3]) + after(far_second, outer_out)[2]
    centre_sum = shifted(centre_out, "y_hi", 1)
    near_out = after(near_keep[1] + near_got[1] + near_first[1], outer_out)
    near_second = x_exchange(near_out, 1)
    near_sum, early_out, late_out, last_out = edge_values(
        where, outer, near_keep, near_got, near_first, near_second
    )
    early = edge_exchange(early_out, 0, 4)
    late = edge_exchange(late_out, 1, 2)
    last = edge_exchange(last_out, 2, 4)
    return proximal(where, block_slots, near_sum, outer, centre_sum, early, late, last, omega)


def solution(mesh):
    devices = mesh.devices.reshape(4, 2, 2, 32)
    fine = Mesh(devices, ("x", "y_hi", "core", "col"))
    rows = ("x", "y_hi", "core")
    return jax.shard_map(
        on_device,
        mesh=fine,
        in_specs=(P(rows, "col"), P("col", None, None, None, None), P("col", None, None)),
        out_specs=P("col", None, rows, None, None),
        check_vma=False,
    )
```

```python
import jax
import jax.numpy as jnp
from jax import lax
from jax.experimental import pallas as pl
from jax.experimental.pallas import tpu as pltpu
from jax.sharding import Mesh, PartitionSpec as P

TILE = 1024
BLK = 128
NB = TILE // BLK
KMAX = 16
ROWS = 256
SAMPLES = 4096
step_size = 0.5
penalty = 0.1
f32 = jnp.float32
bf16 = jnp.bfloat16
PLACE = (0, 2, 1)
VMEM_LIMIT = 16 * 1024 * 1024


def split(value):
    high = value.astype(bf16)
    low = (value - high.astype(f32)).astype(bf16)
    return high, low


def split_tile(x_ref, natural_ref, turned_ref, start=0):
    rows = x_ref.shape[0]
    for a in range(NB):
        block = x_ref[:, a * BLK : (a + 1) * BLK]
        high, low = split(block)
        natural_ref[a, :, :BLK] = high
        natural_ref[a, :, BLK:] = low
        high, low = split(block.T)
        turned_ref[a, :BLK, start : start + rows] = high
        turned_ref[a, BLK:, start : start + rows] = low


def add_products(slots_ref, omega_ref, natural_ref, residual_ref, offset, start=0):
    rows = natural_ref.shape[1]

    def body(j, carry):
        slot = slots_ref[0, offset, j]
        active = slot >= 0
        place = jnp.maximum(slot, 0)
        a = place // NB
        b = place % NB
        weight = jnp.where(active, omega_ref[0, 0, j], 0.0)
        high, low = split(weight)
        half = jnp.concatenate([high, low], axis=1)
        weights = jnp.concatenate([half, half], axis=0)
        out = jnp.dot(natural_ref[a], weights, preferred_element_type=f32)
        residual_ref[b, start : start + rows] += out[:, :BLK] + out[:, BLK:]
        return carry

    lax.fori_loop(0, KMAX, body, 0, unroll=8)


def partial_kernel(offset, first, *refs):
    if first:
        slots_ref, x_ref, omega_ref, residual_ref, turned_ref, natural_ref = refs
        residual_ref[...] = jnp.zeros_like(residual_ref)
    else:
        slots_ref, x_ref, omega_ref, before_ref, residual_ref, turned_ref, natural_ref = refs
        residual_ref[...] = before_ref[...]
    split_tile(x_ref, natural_ref, turned_ref)
    add_products(slots_ref, omega_ref, natural_ref, residual_ref, offset)


def quadrant_sum(out):
    out = out[:BLK] + out[BLK:]
    return out[:, :BLK] + out[:, BLK:]


def slot_block(slots_ref, e, j, turned, pieces_ref):
    place = jnp.maximum(slots_ref[0, e, j], 0)
    out = jnp.dot(
        turned[e][place // NB], pieces_ref[place % NB], preferred_element_type=f32
    )
    return quadrant_sum(out)


def group_products(slots_ref, where_ref, turned, pieces_ref, y_hi, keep_ref, pass_ref, send_ref):
    x, core = where_ref[0], where_ref[2]
    even_pair, odd_pair = x ^ 1, 3 - x
    first = jnp.where(core == 0, even_pair, odd_pair)
    second = jnp.where(core == 0, odd_pair, even_pair)
    for r, x_of in enumerate((x, second, first, x ^ 2)):
        i = 2 * x_of + y_hi
        for e in range(3):
            even = slot_block(slots_ref, e, 2 * i, turned, pieces_ref)
            odd = slot_block(slots_ref, e, 2 * i + 1, turned, pieces_ref)
            if e == 1:
                even_turned, odd_turned = even.T, odd.T
                diagonal = i < NB // 2
                even, odd = (
                    even + jnp.where(diagonal, even_turned, odd_turned),
                    odd + jnp.where(diagonal, odd_turned, even_turned),
                )
            own_ref = keep_ref if r < 2 else pass_ref
            own_ref[r % 2, PLACE[e]] = jnp.where(core == 0, even, odd)
            send_ref[(0, 2, 1, 3)[r], PLACE[e]] = jnp.where(core == 0, odd, even)


def far_kernel(
    slots_ref, where_ref, x_ref, omega_ref, before_ref, half_ref, below_ref, centre_ref,
    keep_ref, pass_ref, send_ref, above_ref, pieces_ref, residual_ref, natural_ref,
):
    residual_ref[...] = before_ref[...]
    done = half_ref.shape[2]
    above_ref[:, :, :done] = half_ref[...]
    split_tile(x_ref, natural_ref, above_ref, done)
    add_products(slots_ref, omega_ref, natural_ref, residual_ref, 2, done)
    for b in range(NB):
        high, low = split(residual_ref[b])
        pieces_ref[b, :, :BLK] = high
        pieces_ref[b, :, BLK:] = low
    group_products(
        slots_ref, where_ref, (below_ref, centre_ref, above_ref), pieces_ref,
        1 - where_ref[1], keep_ref, pass_ref, send_ref,
    )


def near_kernel(
    slots_ref, where_ref, below_ref, centre_ref, above_ref, pieces_ref,
    keep_ref, pass_ref, send_ref,
):
    group_products(
        slots_ref, where_ref, (below_ref, centre_ref, above_ref), pieces_ref,
        where_ref[1], keep_ref, pass_ref, send_ref,
    )


def proximal_kernel(
    where_ref, slots_ref, near_ref, outer_ref, centre_ref, early_ref, late_ref, last_ref,
    omega_ref, out_ref,
):
    j = where_ref[3]
    odd_tile = where_ref[4] == 1
    rows = lax.broadcasted_iota(jnp.int32, (BLK, BLK), 0)
    columns = lax.broadcasted_iota(jnp.int32, (BLK, BLK), 1)
    early = early_ref[...] + last_ref[...]
    late = late_ref[...]
    for e in range(3):
        slot = slots_ref[0, e, j]
        total = near_ref[PLACE[e]] + (centre_ref[...] if e == 1 else outer_ref[PLACE[e]])
        if e == 0:
            total = total + jnp.where(odd_tile, early, late).T
        if e == 2:
            total = total + jnp.where(odd_tile, late, early).T
        gradient = total * (0.5 / SAMPLES)
        omega = omega_ref[0, e, 0]
        if e == 1:
            diagonal = (slot >= 0) & (slot // NB == slot % NB)
            on_diagonal = (rows == columns) & diagonal
            inverse = 1.0 / jnp.where(on_diagonal, omega, 1.0)
            gradient = gradient - jnp.where(on_diagonal, inverse, 0.0)
        trial = omega - step_size * gradient
        shrunk = jnp.maximum(jnp.abs(trial) - step_size * penalty, 0.0)
        result = jnp.where(trial < 0.0, -shrunk, shrunk)
        if e == 1:
            result = jnp.where(on_diagonal, trial, result)
        out_ref[0, e, 0] = jnp.where(slot >= 0, result, 0.0)


def params():
    return pltpu.CompilerParams(vmem_limit_bytes=VMEM_LIMIT)


SMEM = pl.BlockSpec(memory_space=pltpu.SMEM)
WHOLE = pl.BlockSpec(memory_space=pltpu.VMEM)
TURNED = (NB, 2 * BLK, ROWS)
NATURAL = (NB, ROWS, 2 * BLK)


def omega_spec(offset):
    return pl.BlockSpec((1, 1, KMAX, BLK, BLK), lambda i: (0, offset, 0, 0, 0))


def full_spec(shape):
    return pl.BlockSpec(shape, lambda i: (0,) * len(shape))


def partial(offset, slots, tile, omega, before=None):
    first = before is None
    rows = tile.shape[0]
    turned = (NB, 2 * BLK, rows)
    in_specs = [SMEM, full_spec((rows, TILE)), omega_spec(offset)]
    inputs = [slots, tile, omega]
    if not first:
        in_specs.append(full_spec((NB, ROWS, BLK)))
        inputs.append(before)
    return pl.pallas_call(
        lambda *refs: partial_kernel(offset, first, *refs),
        name="partial_residual",
        grid=(1,),
        out_shape=(
            jax.ShapeDtypeStruct((NB, ROWS, BLK), f32),
            jax.ShapeDtypeStruct(turned, bf16),
        ),
        in_specs=in_specs,
        out_specs=(full_spec((NB, ROWS, BLK)), full_spec(turned)),
        scratch_shapes=[pltpu.VMEM((NB, rows, 2 * BLK), bf16)],
        compiler_params=params(),
        cost_estimate=pl.CostEstimate(
            flops=2 * KMAX * rows * 256 * 256, bytes_accessed=5 << 20, transcendentals=0
        ),
    )(*inputs)


HALF = (2, 3, BLK, BLK)
WAY = (4, 3, BLK, BLK)
GROUP_OUT = tuple(jax.ShapeDtypeStruct(shape, f32) for shape in (HALF, HALF, WAY))
GROUP_SPECS = tuple(full_spec(shape) for shape in (HALF, HALF, WAY))


def far_blocks(slots, where, tile, omega, before, half, below, centre):
    rows = tile.shape[0]
    return pl.pallas_call(
        far_kernel,
        name="far_blocks",
        grid=(1,),
        out_shape=GROUP_OUT
        + (jax.ShapeDtypeStruct(TURNED, bf16), jax.ShapeDtypeStruct(NATURAL, bf16)),
        in_specs=[
            SMEM,
            SMEM,
            full_spec((rows, TILE)),
            omega_spec(2),
            full_spec((NB, ROWS, BLK)),
            full_spec((NB, 2 * BLK, ROWS - rows)),
            full_spec(TURNED),
            full_spec(TURNED),
        ],
        out_specs=GROUP_SPECS + (full_spec(TURNED), full_spec(NATURAL)),
        scratch_shapes=[
            pltpu.VMEM((NB, ROWS, BLK), f32),
            pltpu.VMEM((NB, rows, 2 * BLK), bf16),
        ],
        compiler_params=params(),
        cost_estimate=pl.CostEstimate(
            flops=5 * KMAX * ROWS * 256 * 256, bytes_accessed=8 << 20, transcendentals=0
        ),
    )(slots, where, tile, omega, before, half, below, centre)


def near_blocks(slots, where, below, centre, above, pieces):
    return pl.pallas_call(
        near_kernel,
        name="near_blocks",
        grid=(1,),
        out_shape=GROUP_OUT,
        in_specs=[SMEM, SMEM]
        + [full_spec(TURNED)] * 3
        + [full_spec(NATURAL)],
        out_specs=GROUP_SPECS,
        compiler_params=params(),
        cost_estimate=pl.CostEstimate(
            flops=3 * KMAX * ROWS * 256 * 256, bytes_accessed=8 << 20, transcendentals=0
        ),
    )(slots, where, below, centre, above, pieces)


def edge_kernel(
    where_ref, outer_ref, keep_ref, got_ref, first_ref, second_ref,
    near_ref, early_ref, late_ref, last_ref,
):
    odd_tile = where_ref[4] == 1
    for e in range(3):
        near_ref[e] = keep_ref[0, e] + got_ref[0, e] + first_ref[0, e] + second_ref[e]
    downward = near_ref[0] + outer_ref[0]
    upward = near_ref[1] + outer_ref[1]
    late_ref[...] = jnp.where(odd_tile, upward, downward)
    short = jnp.where(odd_tile, downward, upward)
    early_ref[...] = short
    last_ref[...] = short


def edge_values(where, *parts):
    shapes = ((3, BLK, BLK),) + ((BLK, BLK),) * 3
    return pl.pallas_call(
        edge_kernel,
        name="edge_values",
        grid=(1,),
        out_shape=tuple(jax.ShapeDtypeStruct(shape, f32) for shape in shapes),
        in_specs=[SMEM] + [full_spec(part.shape) for part in parts],
        out_specs=tuple(full_spec(shape) for shape in shapes),
        compiler_params=params(),
        cost_estimate=pl.CostEstimate(
            flops=16 * BLK * BLK, bytes_accessed=20 * 4 * BLK * BLK, transcendentals=0
        ),
    )(where, *parts)


def proximal(where, slots, near, outer, centre, early, late, last, omega):
    block = pl.BlockSpec((BLK, BLK), lambda i, where, slots: (0, 0))
    triple = pl.BlockSpec((3, BLK, BLK), lambda i, where, slots: (0, 0, 0))
    pair = pl.BlockSpec((2, BLK, BLK), lambda i, where, slots: (0, 0, 0))
    own = pl.BlockSpec((1, 3, 1, BLK, BLK), lambda i, where, slots: (0, 0, where[3], 0, 0))
    return pl.pallas_call(
        proximal_kernel,
        name="proximal",
        grid_spec=pltpu.PrefetchScalarGridSpec(
            num_scalar_prefetch=2,
            grid=(1,),
            in_specs=[triple, pair] + [block] * 4 + [own],
            out_specs=pl.BlockSpec(
                (1, 3, 1, BLK, BLK), lambda i, where, slots: (0, 0, 0, 0, 0)
            ),
        ),
        out_shape=jax.ShapeDtypeStruct((1, 3, 1, BLK, BLK), f32),
        compiler_params=params(),
        cost_estimate=pl.CostEstimate(
            flops=20 * 3 * BLK * BLK, bytes_accessed=1 << 19, transcendentals=0
        ),
    )(where, slots, near, outer, centre, early, late, last, omega)


def shifted(value, axis, steps):
    count = lax.axis_size(axis)
    pairs = [(source, (source + steps) % count) for source in range(count)]
    return lax.ppermute(value, axis, pairs)


def x_exchange(value, step):
    pairs = []
    for x in range(4):
        for core in range(2):
            partner = x ^ 1 if core == step else 3 - x
            pairs.append((2 * x + core, 2 * partner + core))
    return lax.ppermute(value, ("x", "core"), pairs)


def after(value, earlier):
    return lax.optimization_barrier((value, earlier))[0]


def edge_exchange(value, offset, step):
    count = lax.axis_size("col")
    pairs = []
    for t in range(offset, count, step):
        pairs += [(t, (t + 1) % count), ((t + 1) % count, t)]
    return lax.ppermute(value, "col", pairs)


def on_device(observations, omega, block_slots):
    x, y_hi, core = (lax.axis_index(n).astype(jnp.int32) for n in ("x", "y_hi", "core"))
    odd_tile = lax.axis_index("col").astype(jnp.int32) & 1
    where = jnp.stack([x, y_hi, core, 4 * x + 2 * y_hi + core, odd_tile])
    from_below = shifted(observations, "col", 1)
    cut = ROWS // 2
    above_early = shifted(observations[:cut], "col", -1)
    above_late = shifted(observations[cut:], "col", -1)
    residual, centre = partial(1, block_slots, observations, omega)
    residual, below = partial(0, block_slots, from_below, omega, residual)
    residual, half = partial(2, block_slots, above_early, omega, residual)
    far_keep, far_pass, far_send, above, pieces = far_blocks(
        block_slots, where, above_late, omega, residual, half, below, centre
    )
    far_got = shifted(far_send, "core", 1)
    near_keep, near_pass, near_send = near_blocks(
        block_slots, where, below, centre, above, pieces
    )
    near_got = shifted(near_send, "core", 1)
    far_first = x_exchange(far_pass + far_got[2:], 0)
    near_first = x_exchange(near_pass + near_got[2:], 0)
    far_second = x_exchange(far_keep[1] + far_got[1] + far_first[1], 1)
    parts = (far_keep[0], far_got[0], far_first[0], far_second)
    outer_out = sum(x[:2] for x in parts)
    outer = shifted(outer_out, "y_hi", 1)
    centre_out = sum(x[2] for x in parts[:3]) + after(far_second, outer_out)[2]
    centre_sum = shifted(centre_out, "y_hi", 1)
    near_second = x_exchange(near_keep[1] + near_got[1] + near_first[1], 1)
    near_sum, early_out, late_out, last_out = edge_values(
        where, outer, near_keep, near_got, near_first, near_second
    )
    early = edge_exchange(early_out, 0, 4)
    late = edge_exchange(late_out, 1, 2)
    last = edge_exchange(last_out, 2, 4)
    return proximal(where, block_slots, near_sum, outer, centre_sum, early, late, last, omega)


def solution(mesh):
    devices = mesh.devices.reshape(4, 2, 2, 32)
    fine = Mesh(devices, ("x", "y_hi", "core", "col"))
    rows = ("x", "y_hi", "core")
    return jax.shard_map(
        on_device,
        mesh=fine,
        in_specs=(P(rows, "col"), P("col", None, None, None, None), P("col", None, None)),
        out_specs=P("col", None, rows, None, None),
        check_vma=False,
    )
```
